32 devices in a mesh: cfg: 2 (over core), seq: 8 (over z, x), wt: 2 (over y).
Axes of the slice: x: 2, y: 2, z: 4, core: 2. Of those that a mesh axis runs over, the one named last changes fastest.
Arguments:
- hidden: bfloat16 [2, 1280, 5120], P('cfg', 'seq'), may hold values from -1.5 to 1.5
- latent: float32 [1280, 64], P('seq', 'cfg'), may hold values from -6 to 6
- tenant_lengths: int32 [4], replicated, may hold values from 1 to 960, 1280 in all
- grid_positions: int32 [1280, 3], P('seq'), may hold values from 0 to 47
- text_kv: bfloat16 [2, 2, 2048, 3072], P(None, 'cfg', None, 'wt'), may hold values from -6 to 6
- text_lengths: int32 [2, 4], P('cfg'), may hold values from 1 to 512
- w_query: bfloat16 [5120, 3072], P(('cfg', 'seq'), 'wt'), may hold values from -0.078125 to 0.078125
- w_key: bfloat16 [5120, 3072], P(('cfg', 'seq'), 'wt'), may hold values from -0.078125 to 0.078125
- w_value: bfloat16 [5120, 3072], P(('cfg', 'seq'), 'wt'), may hold values from -0.078125 to 0.078125
- w_out: bfloat16 [5120, 3072], P(('cfg', 'seq'), 'wt'), may hold values from -0.109375 to 0.109375
- w_cross_query: bfloat16 [5120, 3072], P(('cfg', 'seq'), 'wt'), may hold values from -0.078125 to 0.078125
- w_cross_out: bfloat16 [5120, 3072], P(('cfg', 'seq'), 'wt'), may hold values from -0.109375 to 0.109375
- w_head: bfloat16 [5120, 64], replicated, may hold values from -0.078125 to 0.078125
- guidance: float32 [1], replicated, may hold values from 3 to 7
- step_size: float32 [1], replicated, may hold values from -0.3 to -0.05
Outputs:
- hidden_out: bfloat16 [2, 1280, 5120], P('cfg', 'seq', 'wt')
- latent_next: float32 [1280, 64], P('seq', 'cfg')
The draws below stay inside these ranges and needn't reach their ends.
Inputs may be any that keep to these rules, and one draw needn't show every extreme that they name: `tenant_lengths`: the lengths sum to 1280; the largest is exactly 960.
All inputs are finite; a program needn't handle non-finite values.
Results may differ from the reference program's by a relative error of at most 0.013.
Values may be sent and summed in bfloat16 or wider, within the bound.
A program may use at most 192 MiB of HBM per device.

```python
import math
import jax
import jax.numpy as jnp
import numpy as np
from jax import lax

D = 5120
HEADS = 24
HD = 128
TEXT = 512
TENANTS = 4
OUTC = 64
C = 3072
TOKENS = 1280
N_WT = 2


def set_ends(result, own_key, least, high):
    longest = result.shape.index(max(result.shape))
    spots = []
    for shift in (0, 1):
        where = [jax.random.randint(jax.random.fold_in(own_key, axis), (), 0, length) for axis, length in enumerate(result.shape)]
        where[longest] = (where[longest] + shift) % result.shape[longest]
        spots.append(tuple(where))
    return result.at[spots[0]].set(least).at[spots[1]].set(high)


def block_levels(key, extent, split, smallest, top_value):
    loudness, own = 1.0, jax.random.fold_in(key, 6)
    for dim, blocks in split:
        heights = jnp.exp(jax.random.uniform(jax.random.fold_in(own, dim), (blocks,), jnp.float32, smallest / len(split), top_value / len(split)))
        loudness = loudness * jnp.repeat(heights, extent[dim] // blocks).reshape([-1 if axis == dim else 1 for axis in range(len(extent))])
    return loudness


def length_profile(amount, total, limit, slope):
    weights = [(1 << 20) // math.isqrt(grade ** slope) + 1 for grade in range(2, amount + 1)]
    rest, given = total - limit - (amount - 1), [1] * (amount - 1)
    while rest > 0:
        free = [i for i in range(amount - 1) if given[i] < limit]
        whole, remaining = sum([weights[i] for i in free]), rest
        for i in free:
            addition = min(limit - given[i], max(1, remaining * weights[i] // whole), rest)
            given[i] = given[i] + addition
            rest = rest - addition
    return np.array([limit] + given)


def uneven(rng, count, total, bound, lean):
    if count == 2:
        one = jax.random.randint(rng, (), max(1, total - bound), min(bound, total - 1) + 1)
        return jnp.stack([one, total - one])
    lengths = jnp.asarray(length_profile(count, total, bound, lean), jnp.int32)
    twos = (count - 1) // 2
    giver, receiver = lengths[1:1 + 2 * twos:2], lengths[2:2 + 2 * twos:2]
    margin = jnp.minimum(giver - 1, bound - receiver)
    moved = jax.random.randint(jax.random.fold_in(rng, 1), (twos,), 0, 1 << 20) % (margin + 1)
    lengths = lengths.at[1:1 + 2 * twos:2].set(giver - moved).at[2:2 + 2 * twos:2].set(receiver + moved)
    return lengths[jax.random.permutation(jax.random.fold_in(rng, 2), count)]


def normal_values(stream_key, shape, deviation, bound, shards=(), kind=jnp.bfloat16):
    level = block_levels(stream_key, shape, shards, -0.22, 0.18) if shards else 1.0
    values = jax.random.normal(stream_key, shape, jnp.float32) * deviation * level
    return jnp.minimum(jnp.maximum(values, -bound), bound).astype(kind)


def setup_inputs(seed: int = 0) -> dict:
    splits = jax.random.split(jax.random.key(seed), 16)
    return {
        "hidden": normal_values(splits[0], (2, TOKENS, D), 0.25, 1.5, ((0, 2), (1, 8))),
        "latent": normal_values(splits[1], (TOKENS, OUTC), 1.0, 6.0, ((0, 8), (1, 2)), jnp.float32),
        "tenant_lengths": uneven(splits[2], TENANTS, TOKENS, 3 * TOKENS // 4, 2).astype(jnp.int32),
        "grid_positions": set_ends(jax.random.randint(splits[3], (TOKENS, 3), 0, 48), jax.random.fold_in(splits[3], 1), 0, 47).astype(jnp.int32),
        "text_kv": normal_values(splits[4], (2, 2, TENANTS * TEXT, C), 1.0, 6.0, ((1, 2), (3, 2))),
        "text_lengths": set_ends(jax.random.randint(splits[5], (2, TENANTS), 1, TEXT + 1), jax.random.fold_in(splits[5], 1), 1, TEXT).astype(jnp.int32),
        "w_query": normal_values(splits[6], (D, C), D ** -0.5, 0.078125, ((0, 16), (1, 2))),
        "w_key": normal_values(splits[7], (D, C), D ** -0.5, 0.078125, ((0, 16), (1, 2))),
        "w_value": normal_values(splits[8], (D, C), D ** -0.5, 0.078125, ((0, 16), (1, 2))),
        "w_out": normal_values(splits[9], (D, C), C ** -0.5, 0.109375, ((0, 16), (1, 2))),
        "w_cross_query": normal_values(splits[10], (D, C), D ** -0.5, 0.078125, ((0, 16), (1, 2))),
        "w_cross_out": normal_values(splits[11], (D, C), C ** -0.5, 0.109375, ((0, 16), (1, 2))),
        "w_head": normal_values(splits[12], (D, OUTC), D ** -0.5, 0.078125),
        "guidance": jnp.clip(jax.random.uniform(splits[13], (1,), jnp.float32, 3.0, 7.0), 3.0, 7.0),
        "step_size": jnp.clip(jax.random.uniform(splits[14], (1,), jnp.float32, -0.3, -0.05), -0.3, -0.05),
    }


epsilon = 1e-06

def layer_norm(inputs):
    average = lax.optimization_barrier(jnp.mean(inputs, axis=-1, keepdims=True))
    centred = inputs - average
    variance = lax.optimization_barrier(jnp.mean(centred * centred, axis=-1, keepdims=True))
    return centred * lax.rsqrt(variance + epsilon)

def head_norm(inputs, head_dim):
    shaped = inputs.reshape(inputs.shape[:-1] + (inputs.shape[-1] // head_dim, head_dim))
    return shaped * lax.rsqrt(lax.optimization_barrier(jnp.mean(shaped * shaped, axis=-1, keepdims=True)) + epsilon)

def rotary(inputs, grid):
    head_dim = inputs.shape[-1]
    sixth_part = head_dim // 6
    angle_parts = []
    for dim_index, span_width in enumerate((head_dim - 4 * sixth_part, 2 * sixth_part, 2 * sixth_part)):
        exponent = jnp.arange(0, span_width, 2).astype(jnp.float32) / span_width
        frequency = 1.0 / 10000.0 ** exponent
        angle_parts.append(grid[:, dim_index:dim_index + 1].astype(jnp.float32) * frequency[None, :])
    angles = jnp.concatenate(angle_parts, axis=1)[:, None, :]
    paired = inputs.reshape(inputs.shape[:-1] + (head_dim // 2, 2))
    even_part = paired[..., 0]
    odd_part = paired[..., 1]
    cosine = jnp.cos(angles)
    sinus = jnp.sin(angles)
    rotated = jnp.stack([even_part * cosine - odd_part * sinus, even_part * sinus + odd_part * cosine], axis=-1)
    return rotated.reshape(inputs.shape)

def attention(queries, keys, values, allowed):
    score_scale = 1.0 / math.sqrt(queries.shape[-1])

    def one_head(operands):
        query_head, key_head, value_head = operands
        scores = jnp.dot(query_head, key_head.T, preferred_element_type=jnp.float32) * score_scale
        weights = jnp.where(allowed, jnp.exp(scores), 0.0).astype(jnp.bfloat16)
        running_sum = lax.optimization_barrier(jnp.sum(weights.astype(jnp.float32), axis=1))
        summed = jnp.dot(weights, value_head, preferred_element_type=jnp.float32)
        return (summed / running_sum[:, None]).astype(jnp.bfloat16)
    outputs = lax.map(one_head, (jnp.swapaxes(queries, 0, 1), jnp.swapaxes(keys, 0, 1), jnp.swapaxes(values, 0, 1)))
    return jnp.swapaxes(outputs, 0, 1).reshape(queries.shape[0], -1)

def grouped_project(mixed, weight):
    group_cols = weight.shape[1] // N_WT
    running_sum = jnp.zeros((mixed.shape[0], weight.shape[0]), jnp.float32)
    for number in range(N_WT):
        lower = number * group_cols
        partial_value = jnp.dot(mixed[:, lower:lower + group_cols], weight[:, lower:lower + group_cols].T, preferred_element_type=jnp.float32)
        rounded = lax.optimization_barrier(partial_value.astype(jnp.bfloat16))
        running_sum = running_sum + rounded.astype(jnp.float32)
    return running_sum

def reference(hidden, latent, tenant_lengths, grid_positions, text_kv, text_lengths, w_query, w_key, w_value, w_out, w_cross_query, w_cross_out, w_head, guidance, step_size):
    ends = jnp.cumsum(tenant_lengths)
    positions = jnp.arange(TOKENS, dtype=jnp.int32)
    tenant = lax.optimization_barrier(jnp.sum((positions[:, None] >= ends[None, :]).astype(jnp.int32), axis=1))
    same_tenant = tenant[:, None] == tenant[None, :]
    text_index = jnp.arange(TENANTS * TEXT, dtype=jnp.int32)
    text_tenant = text_index // TEXT
    text_slot = text_index % TEXT
    tenant_table = text_tenant[:, None] == jnp.arange(TENANTS, dtype=jnp.int32)[None, :]
    outputs = []
    velocities = []
    for half in range(2):
        state = hidden[half].astype(jnp.float32)
        normed = layer_norm(state).astype(jnp.bfloat16)
        queries = rotary(head_norm(jnp.dot(normed, w_query, preferred_element_type=jnp.float32), HD), grid_positions).astype(jnp.bfloat16)
        keys = rotary(head_norm(jnp.dot(normed, w_key, preferred_element_type=jnp.float32), HD), grid_positions).astype(jnp.bfloat16)
        values = jnp.dot(normed, w_value, preferred_element_type=jnp.float32).astype(jnp.bfloat16)
        values = values.reshape(TOKENS, HEADS, HD)
        mixed = attention(queries, keys, values, same_tenant)
        state = state + grouped_project(mixed, w_out)
        normed = layer_norm(state).astype(jnp.bfloat16)
        cross_queries = head_norm(jnp.dot(normed, w_cross_query, preferred_element_type=jnp.float32), HD).astype(jnp.bfloat16)
        text_keys = head_norm(text_kv[0, half].astype(jnp.float32), HD).astype(jnp.bfloat16)
        text_values = text_kv[1, half].reshape(TENANTS * TEXT, HEADS, HD)
        live_length = lax.optimization_barrier(jnp.sum(jnp.where(tenant_table, text_lengths[half][None, :], 0), axis=1))
        live = text_slot < live_length
        allowed = (tenant[:, None] == text_tenant[None, :]) & live[None, :]
        mixed = attention(cross_queries, text_keys, text_values, allowed)
        state = state + grouped_project(mixed, w_cross_out)
        outputs.append(state.astype(jnp.bfloat16))
        velocities.append(jnp.dot(layer_norm(state).astype(jnp.bfloat16), w_head, preferred_element_type=jnp.float32))
    guided = velocities[1] + guidance[0] * (velocities[0] - velocities[1])
    return (jnp.stack(outputs), latent + step_size[0] * guided)
```

```python
import math

import jax
import jax.numpy as jnp
import numpy as np
from jax import lax
from jax.experimental import pallas as pl
from jax.experimental.pallas import tpu as pltpu
from jax.sharding import Mesh
from jax.sharding import PartitionSpec as P

HD = 128
TEXT = 512
TENANTS = 4
EPS = 1e-06
CHUNKS = 2
BF = jnp.bfloat16
F32 = jnp.float32


def flip(block, axis):
    return lax.ppermute(block, axis, [(0, 1), (1, 0)])


def rotary_tables():
    sixth = HD // 6
    table = np.zeros((3, HD), np.float32)
    lane = 0
    for column, span in enumerate((HD - 4 * sixth, 2 * sixth, 2 * sixth)):
        exponent = np.arange(0, span, 2).astype(np.float32) / np.float32(span)
        frequency = (1.0 / 10000.0**exponent).astype(np.float32)
        table[column, lane : lane + span] = np.repeat(frequency, 2)
        lane += span
    swap = np.zeros((HD, HD), np.float32)
    for pair in range(0, HD, 2):
        swap[pair + 1, pair] = -1.0
        swap[pair, pair + 1] = 1.0
    return table, swap


def running_ends(lengths):
    upto = np.tril(np.ones((TENANTS, TENANTS), np.int32))
    return jnp.sum(jnp.asarray(upto) * lengths[None, :], axis=1)


def head_scale(shaped):
    return lax.rsqrt(jnp.mean(shaped * shaped, axis=-1, keepdims=True) + EPS)


def attend(queries, keys, values, allowed):
    scores = jnp.einsum("qhd,khd->hqk", queries, keys, preferred_element_type=F32)
    scores = scores * (1.0 / math.sqrt(queries.shape[-1]))
    weights = jnp.where(allowed[None], jnp.exp(scores), 0.0).astype(BF)
    summed = jnp.einsum("hqk,khd->qhd", weights, values, preferred_element_type=F32)
    totals = jnp.sum(weights.astype(F32), axis=2).T
    return (summed / totals[..., None]).astype(BF).reshape(queries.shape[0], -1)


MESH = pl.DeviceIdType.MESH
NEAR = (1, 3, 2)


def remote(src, dst, sent, got, device):
    return pltpu.make_async_remote_copy(
        src_ref=src, dst_ref=dst, send_sem=sent, recv_sem=got, device_id=device, device_id_type=MESH
    )


def meet(devices):
    barrier = pltpu.get_barrier_semaphore()
    for device in devices:
        pl.semaphore_signal(barrier, inc=1, device_id=device, device_id_type=MESH)
    pl.semaphore_wait(barrier, len(devices))


def gather_project(
    hid, pos, wk, wv, wq, k_out, v_out, q_out, raw_out, mean_out, pos_out,
    wide, rows, loc_w, loc_h, zs, zr, hs, hr, ps, pr, xs, xr, cs, cr, ys, yr,
):
    c, z, x, y = (lax.axis_index(a) for a in ("cfg", "z", "t", "wt"))
    groups = 4
    tok = hid.shape[0]
    depth = wk.shape[0]
    wid = rows.shape[2]
    cols = wide.shape[3]
    at_z = [{"z": lax.rem(z + d, groups)} for d in range(groups)]
    from_z = [lax.rem(z + groups - d, groups) for d in range(groups)]
    at_x, at_c, at_y = {"t": 1 - x}, {"cfg": 1 - c}, {"wt": 1 - y}
    weights = (wk, wv, wq)
    mine = c * groups + z

    def span(index, size):
        return pl.ds(pl.multiple_of(index * size, size), size)

    own_rows = [
        pltpu.make_async_copy(hid.at[:, kb * wid : (kb + 1) * wid], rows.at[kb, span(z, tok)], loc_h.at[kb])
        for kb in range(2 * groups)
    ]
    own_weights = [
        pltpu.make_async_copy(w.at[:, span(z, cols)], wide.at[j, mine, span(x, depth)], loc_w.at[j])
        for j, w in enumerate(weights)
    ]
    own_pos = pltpu.make_async_copy(pos, pos_out.at[z], loc_w.at[3])
    for copy in own_rows + own_weights + [own_pos]:
        copy.start()
    meet([at_z[1], at_z[2], at_z[3], at_x, at_c, at_y])

    def block(j, d, column):
        return wide.at[j, c * groups + from_z[d], span(column, depth)]

    def x_copy(j, d):
        return remote(block(j, d, x), block(j, d, x), xs.at[d, j], xr.at[d, j], at_x)

    def x_arrival(j, d):
        return remote(block(j, d, 1 - x), block(j, d, 1 - x), xs.at[d, j], xr.at[d, j], at_x)

    def c_copy(j, d, second):
        part = block(j, d, 1 - x if second else x)
        return remote(part, part, cs.at[second, d, j], cr.at[second, d, j], at_c)

    def c_arrival(j, d, second):
        part = wide.at[j, (1 - c) * groups + from_z[d], span(1 - x if second else x, depth)]
        return remote(part, part, cs.at[second, d, j], cr.at[second, d, j], at_c)

    def z_copy(j, d):
        target = lax.rem(z + d, groups)
        return remote(
            weights[j].at[:, span(target, cols)], wide.at[j, mine, span(x, depth)], zs.at[d - 1, j], zr.at[d - 1, j], at_z[d]
        )

    def z_arrival(j, d):
        return remote(block(j, d, x), block(j, d, x), zs.at[d - 1, j], zr.at[d - 1, j], at_z[d])

    def rows_of(d, column):
        return rows.at[pl.ds(pl.multiple_of(column * groups, groups), groups), span(from_z[d], tok)]

    def h_copy(d):
        return remote(rows_of(0, y), rows_of(0, y), hs.at[d - 1], hr.at[d - 1], at_z[d])

    def h_arrival(d):
        return remote(rows_of(d, y), rows_of(d, y), hs.at[d - 1], hr.at[d - 1], at_z[d])

    def y_copy(d):
        return remote(rows_of(d, y), rows_of(d, y), ys.at[d - 1], yr.at[d - 1], at_y)

    def y_arrival(d):
        return remote(rows_of(d, 1 - y), rows_of(d, 1 - y), ys.at[d - 1], yr.at[d - 1], at_y)

    def p_copy(d):
        return remote(pos_out.at[z], pos_out.at[z], ps.at[d - 1], pr.at[d - 1], at_z[d])

    def p_arrival(d):
        part = pos_out.at[from_z[d]]
        return remote(part, part, ps.at[d - 1], pr.at[d - 1], at_z[d])

    for copy in own_rows + [own_pos]:
        copy.wait()
    for d in NEAR:
        p_copy(d).start()
        h_copy(d).start()
    for j in range(3):
        for d in NEAR:
            z_copy(j, d).start()
    for j in range(3):
        own_weights[j].wait()
        x_copy(j, 0).start()
        c_copy(j, 0, 0).start()
    for j, d in enumerate(NEAR):
        x_arrival(j, 0).wait_recv()
        c_copy(j, 0, 1).start()
        h_arrival(d).wait_recv()
        y_copy(d).start()

    def relay(j):
        for d in NEAR:
            z_arrival(j, d).wait_recv()
            x_copy(j, d).start()
            c_copy(j, d, 0).start()
        for d in NEAR:
            x_arrival(j, d).wait_recv()
            c_copy(j, d, 1).start()

    def project(j, out):
        for d in range(groups):
            c_arrival(j, d, 0).wait_recv()
            c_arrival(j, d, 1).wait_recv()

        def step(m, carry):
            total = jnp.dot(rows[0, span(m, tok)], wide[j, 0], preferred_element_type=F32)
            for kb in range(1, 2 * groups):
                total += jnp.dot(rows[kb, span(m, tok)], wide[j, kb], preferred_element_type=F32)
            out[span(m, tok)] = total
            return carry

        lax.fori_loop(0, groups, step, 0)

    relay(0)
    for d in NEAR:
        y_arrival(d).wait_recv()
        y_copy(d).wait_send()
        h_copy(d).wait_send()
    raw_out[0] = rows[z]
    raw_out[1] = rows[groups + z]
    some = 16
    width = 2 * groups * wid

    def norm(i, carry):
        these = span(i, some)
        total = jnp.zeros((some, wid), F32)
        for kb in range(2 * groups):
            total += rows[kb, these].astype(F32)
        mean = jnp.sum(total, axis=1, keepdims=True) / width
        total = jnp.zeros((some, wid), F32)
        for kb in range(2 * groups):
            centred = rows[kb, these].astype(F32) - mean
            total += centred * centred
        scale = lax.rsqrt(jnp.sum(total, axis=1, keepdims=True) / width + EPS)
        for kb in range(2 * groups):
            rows[kb, these] = ((rows[kb, these].astype(F32) - mean) * scale).astype(BF)
        mean_out[these] = mean
        return carry

    lax.fori_loop(0, groups * tok // some, norm, 0)
    project(0, k_out)
    relay(1)
    project(1, v_out)
    relay(2)
    project(2, q_out)
    for d in NEAR:
        p_arrival(d).wait_recv()
        p_copy(d).wait_send()
        for j in range(3):
            z_copy(j, d).wait_send()
    for d in range(groups):
        for j in range(3):
            x_copy(j, d).wait_send()
            c_copy(j, d, 0).wait_send()
            c_copy(j, d, 1).wait_send()


def first_kernel(hidden, positions, wk, wv, wq):
    tok, width = hidden.shape
    groups = 4
    depth, local_cols = wk.shape
    cols = local_cols // groups
    rows = groups * tok
    wid = width // (2 * groups)
    anywhere = pl.BlockSpec(memory_space=pl.ANY)
    vmem = pl.BlockSpec(memory_space=pltpu.VMEM)
    dma = pltpu.SemaphoreType.DMA
    made = [jax.ShapeDtypeStruct((rows, cols), F32)] * 3
    made += [
        jax.ShapeDtypeStruct((2, rows, wid), BF),
        jax.ShapeDtypeStruct((rows, 1), F32),
        jax.ShapeDtypeStruct((groups,) + positions.shape, F32),
    ]
    return pl.pallas_call(
        gather_project,
        out_shape=made,
        in_specs=[anywhere, vmem, anywhere, anywhere, anywhere],
        out_specs=[vmem] * 6,
        scratch_shapes=[
            pltpu.VMEM((3, 2 * groups, 2 * depth, cols), BF),
            pltpu.VMEM((2 * groups, rows, wid), BF),
            dma((4,)), dma((2 * groups,)),
            dma((3, 3)), dma((3, 3)),
            dma((3,)), dma((3,)),
            dma((3,)), dma((3,)),
            dma((4, 3)), dma((4, 3)),
            dma((2, 4, 3)), dma((2, 4, 3)),
            dma((3,)), dma((3,)),
        ],
        compiler_params=pltpu.CompilerParams(
            collective_id=0, has_side_effects=True, vmem_limit_bytes=56 * 2**20
        ),
        cost_estimate=pl.CostEstimate(
            flops=6 * rows * width * cols, bytes_accessed=20 * 2**20, transcendentals=0
        ),
    )(hidden, positions, wk, wv, wq)


def on_device(
    hidden,
    latent,
    tenant_lengths,
    grid_positions,
    text_kv,
    text_lengths,
    w_query,
    w_key,
    w_value,
    w_out,
    w_cross_query,
    w_cross_out,
    w_head,
    guidance,
    step_size,
):
    halves, groups, parts, columns = (lax.axis_size(a) for a in ("cfg", "z", "t", "wt"))
    half_index, z_index, t_index, wt_index = (
        lax.axis_index(a) for a in ("cfg", "z", "t", "wt")
    )
    tok, width = hidden.shape[1:]
    rows = groups * tok
    local_cols = w_query.shape[1]
    my_cols = local_cols // groups
    heads = my_cols // HD
    paired = halves == 2 and parts == 2
    block = w_query.shape[0]
    ends = running_ends(tenant_lengths)

    def tenant_of(indices):
        return jnp.sum((indices[:, None] >= ends[None, :]).astype(jnp.int32), axis=1)

    def ordered(mine, other, index):
        return jnp.where(
            index == 0, jnp.concatenate([mine, other]), jnp.concatenate([other, mine])
        )

    def wide(w):
        if not paired:
            return lax.all_gather(w, ("cfg", "t"), axis=0, tiled=True)
        two = ordered(w, flip(w, "t"), t_index)
        return ordered(two, flip(two, "cfg"), half_index)

    def over_groups(x):
        return x if groups == 1 else lax.all_to_all(x, "z", 0, 0, tiled=True)

    def join_groups(x):
        if groups == 1:
            return x
        x = lax.all_gather(x, "z", axis=0)
        return jnp.swapaxes(x, 0, 1).reshape(x.shape[1], local_cols)

    def sum_at_owner(x):
        if groups == 1:
            return x[0].astype(F32)
        return jnp.sum(lax.all_to_all(x, "z", 0, 0).astype(F32), axis=0)

    def sum_groups(x):
        if groups == 1:
            return x
        return lax.psum_scatter(x, "z", scatter_dimension=0, tiled=True)

    def to_groups(x, n):
        return jnp.swapaxes(x.reshape(x.shape[0], groups, n), 0, 1)

    def both_columns(terms):
        terms = terms.astype(BF)
        if columns == 1:
            return terms.astype(F32)
        if columns == 2:
            return terms.astype(F32) + flip(terms, "wt").astype(F32)
        return lax.psum(terms, "wt").astype(F32)

    fast = paired and groups == 4 and columns == 2 and tok % 16 == 0 and block % 16 == 0
    fast = fast and my_cols % 128 == 0 and width == 16 * block
    if fast:
        wide_key = wide_query = wide_value = None
    elif paired:
        key_pair = ordered(w_key, flip(w_key, "t"), t_index)
        key_pair, w_query, w_value = lax.optimization_barrier((key_pair, w_query, w_value))
        wide_key = ordered(key_pair, flip(key_pair, "cfg"), half_index)
    else:
        wide_key = wide(w_key)
    if not fast:
        wide_query, wide_value = wide(w_query), wide(w_value)
    wide_out, wide_cross, wide_cross_out = wide(w_out), wide(w_cross_query), wide(w_cross_out)

    chunks = CHUNKS if groups > 1 and tok % (CHUNKS * 16) == 0 else 1
    part = tok // chunks
    chunk_rows = rows // chunks

    def by_chunk(x):
        shape = (groups, chunks, part) + x.shape[2:]
        return jnp.swapaxes(x.reshape(shape), 0, 1).reshape((rows,) + x.shape[2:])

    def chunked(x):
        return by_chunk(x.reshape((groups, tok) + x.shape[1:]))

    def three_terms(x):
        high = lax.reduce_precision(x, 8, 7)
        middle = lax.reduce_precision(x - high, 8, 7)
        return [term.astype(BF) for term in (high, middle, x - high - middle)]

    slice_width = width // groups
    if fast:
        positions = jnp.pad(grid_positions.T.astype(F32), ((0, 5), (0, -tok % 128)))
        raw_keys, raw_values, raw_queries, raw, mean, positions = first_kernel(
            hidden[0], positions, w_key, w_value, w_query
        )
        positions = jnp.swapaxes(positions[:, :3, :tok], 1, 2).reshape(rows, 3)
        facts = chunked(jnp.concatenate([mean, mean, positions], axis=1))
        projected_keys = chunked(raw_keys).astype(BF)
        projected = chunked(jnp.concatenate([raw_queries, raw_values], axis=1)).astype(BF)
        sliced = chunked(jnp.concatenate([raw[0], raw[1]], axis=1)).astype(F32)
    else:
        own = hidden[0].astype(F32)
        mean = jnp.mean(own, axis=-1, keepdims=True)
        centred = own - mean
        scale = lax.rsqrt(jnp.mean(centred * centred, axis=-1, keepdims=True) + EPS)
        facts = jnp.concatenate([mean, scale, grid_positions.astype(F32)], axis=1)
        if groups == 1:
            sliced = own
        else:
            extra = jnp.concatenate(three_terms(facts), axis=1)
            extra = jnp.pad(extra, ((0, 0), (0, 128 - extra.shape[1])))
            features = hidden[0].reshape(tok, halves, groups, slice_width // halves)
            features = jnp.concatenate(
                [features[:, half] for half in range(halves)]
                + [jnp.broadcast_to(extra[:, None], (tok, groups, 128))],
                axis=2,
            )
            arrived = lax.all_to_all(jnp.swapaxes(features, 0, 1), "z", 0, 0)
            arrived = by_chunk(arrived).astype(F32)
            sliced = arrived[:, :slice_width]
            extra = arrived[:, slice_width : slice_width + 15]
            facts = extra[:, 0:5] + extra[:, 5:10] + extra[:, 10:15]
        normed = ((sliced - facts[:, 0:1]) * facts[:, 1:2]).astype(BF)

        def project(w):
            return to_groups(jnp.dot(normed, w, preferred_element_type=F32).astype(BF), my_cols)

        projected_keys = sum_at_owner(project(wide_key)).astype(BF)
        projected = jnp.concatenate([project(wide_query), project(wide_value)], axis=2)
        projected = sum_groups(projected.reshape(groups * rows, 2 * my_cols))

    table, swap = rotary_tables()
    angles = (
        facts[:, 2:3] * table[0][None] + facts[:, 3:4] * table[1][None] + facts[:, 4:5] * table[2][None]
    )
    cosine, sinus = jnp.cos(angles)[:, None, :], jnp.sin(angles)[:, None, :]

    def rotated(x):
        shaped = x.reshape(rows, heads, HD)
        swapped = jnp.einsum("thd,de->the", shaped, jnp.asarray(swap, BF), preferred_element_type=F32)
        shaped = shaped.astype(F32)
        return ((shaped * cosine + swapped * sinus) * head_scale(shaped)).astype(BF)

    keys = rotated(projected_keys).reshape(rows, my_cols)
    queries = rotated(projected[:, :my_cols])
    values = projected[:, my_cols:]

    base = jnp.arange(groups, dtype=jnp.int32)[:, None] * (parts * tok)
    base = by_chunk(base + jnp.arange(tok, dtype=jnp.int32)[None])
    my_tenant = tenant_of(base + t_index * tok)
    if parts == 2:
        keys = jnp.concatenate([keys, flip(keys, "t")], axis=0)
        values = jnp.concatenate([values, flip(values, "t")], axis=0)
        key_tenant = jnp.concatenate([my_tenant, tenant_of(base + (1 - t_index) * tok)])
    else:
        keys = lax.all_gather(keys, "t", axis=0, tiled=True)
        values = lax.all_gather(values, "t", axis=0, tiled=True)
        key_tenant = tenant_of(
            (jnp.arange(parts, dtype=jnp.int32)[:, None] * tok + base[None]).reshape(-1)
        )
    keys = keys.reshape(-1, heads, HD)
    values = values.reshape(-1, heads, HD)

    spans = [slice(i * chunk_rows, (i + 1) * chunk_rows) for i in range(chunks)]
    mixed = [
        attend(queries[i], keys, values, my_tenant[i][:, None] == key_tenant[None, :])
        for i in spans
    ]

    def project_out(mixed, weight):
        return lax.dot_general(
            join_groups(mixed), weight, (((1,), (1,)), ((), ())), preferred_element_type=F32
        )

    column_sums = jnp.dot(jnp.ones((8, slice_width), BF), wide_cross, preferred_element_type=F32)
    column_sums = column_sums[0].reshape(groups, 1, my_cols)
    riding = groups > 1 and chunk_rows <= my_cols

    text = lax.dynamic_slice_in_dim(text_kv[:, 0], z_index * my_cols, my_cols, 2)
    text_keys = text[0].reshape(-1, heads, HD).astype(F32)
    text_keys = (text_keys * head_scale(text_keys)).astype(BF)
    text_values = text[1].reshape(-1, heads, HD)
    text_index = jnp.arange(text_kv.shape[2], dtype=jnp.int32)
    text_tenant = text_index // TEXT
    slots = text_tenant[:, None] == jnp.arange(TENANTS, dtype=jnp.int32)[None, :]
    live_length = jnp.sum(jnp.where(slots, text_lengths[0][None, :], 0), axis=1)
    live = text_index % TEXT < live_length

    states, cross_mixed = [], []
    for i, block_mixed in zip(spans, mixed):
        shifted = (sliced[i] - facts[i, 0:1]) + both_columns(project_out(block_mixed, wide_out))
        states.append(shifted)
        sums = jnp.stack([jnp.sum(shifted, axis=1), jnp.sum(shifted * shifted, axis=1)])
        crossed = jnp.dot(shifted.astype(BF), wide_cross, preferred_element_type=F32).astype(BF)
        crossed = to_groups(crossed, my_cols)
        if riding:
            sums = jnp.concatenate(three_terms(sums))
            sums = jnp.pad(sums, ((0, 0), (0, my_cols - chunk_rows)))
            sums = jnp.broadcast_to(sums[None], (groups,) + sums.shape)
            below = jnp.concatenate([sums] + three_terms(column_sums), axis=1)
            below = jnp.pad(below, ((0, 0), (0, 16 - below.shape[1]), (0, 0)))
            arrived = sum_at_owner(jnp.concatenate([crossed, below], axis=1))
            crossed, below = arrived[:chunk_rows], arrived[chunk_rows:]
            sums = (below[0:2] + below[2:4] + below[4:6])[:, :chunk_rows]
            all_columns = below[6:7] + below[7:8] + below[8:9]
        else:
            sums = sum_at_owner(jnp.broadcast_to(sums[None], (groups,) + sums.shape))
            all_columns = sum_at_owner(column_sums)
            crossed = sum_at_owner(crossed)
        sums = sums / width
        variance = jnp.maximum(sums[1] - sums[0] * sums[0], 0.0)[:, None, None]
        shaped = (crossed - sums[0][:, None] * all_columns).reshape(chunk_rows, heads, HD)
        square = jnp.mean(shaped * shaped, axis=-1, keepdims=True)
        cross_queries = (shaped * lax.rsqrt(square + EPS * (variance + EPS))).astype(BF)
        allowed = (my_tenant[i][:, None] == text_tenant[None, :]) & live[None]
        cross_mixed.append(attend(cross_queries, text_keys, text_values, allowed))

    channels = w_head.shape[1]
    head_rows = lax.dynamic_index_in_dim(
        w_head.reshape(halves, groups, parts * block, channels), z_index, 1, keepdims=False
    ).reshape(-1, channels)
    totals = jnp.sum(w_head.astype(F32), axis=0)[None]
    out_width = width // columns

    leaving, sums = [], []
    for i, shifted, block_mixed in zip(spans, states, cross_mixed):
        shifted = shifted + both_columns(project_out(block_mixed, wide_cross_out))
        final = (shifted + facts[i, 0:1]).astype(BF)
        if groups > 1 and columns == halves:
            span = slice_width // halves
            final = lax.dynamic_slice_in_dim(final, wt_index * span, span, 1)
        leaving.append(final.reshape(groups, part, -1))
        some = jnp.concatenate(
            [
                jnp.dot(shifted.astype(BF), head_rows, preferred_element_type=F32),
                jnp.sum(shifted, axis=1, keepdims=True),
                jnp.sum(shifted * shifted, axis=1, keepdims=True),
            ],
            axis=1,
        )
        sums.append(some.reshape(groups, part, channels + 2))
    sums = sum_at_owner(jnp.concatenate(sums, axis=1))
    mean = sums[:, channels : channels + 1] / width
    variance = jnp.maximum(sums[:, channels + 1 :] / width - mean * mean, 0.0)
    velocity = (sums[:, :channels] - mean * totals) * lax.rsqrt(variance + EPS)

    leaving = jnp.concatenate(leaving, axis=1)
    if groups == 1:
        hidden_out = lax.dynamic_slice_in_dim(leaving[0], wt_index * out_width, out_width, 1)
    else:
        leaving = jnp.swapaxes(lax.all_to_all(leaving, "z", 0, 0), 0, 1)
        if columns == halves:
            hidden_out = leaving.reshape(tok, out_width)
        else:
            leaving = jnp.swapaxes(leaving.reshape(tok, groups, halves, -1), 1, 2)
            hidden_out = lax.dynamic_slice_in_dim(
                leaving.reshape(tok, width), wt_index * out_width, out_width, 1
            )

    channel_half = latent.shape[1]
    outgoing = lax.dynamic_slice_in_dim(velocity, (1 - half_index) * channel_half, channel_half, 1)
    partner = flip(outgoing, "cfg")
    own_part = lax.dynamic_slice_in_dim(velocity, half_index * channel_half, channel_half, 1)
    conditional = jnp.where(half_index == 0, own_part, partner)
    null_text = jnp.where(half_index == 0, partner, own_part)
    latent_next = latent + step_size[0] * (null_text + guidance[0] * (conditional - null_text))
    return (hidden_out[None], latent_next)


def solution(mesh):
    halves, seq, columns = (mesh.shape[a] for a in ("cfg", "seq", "wt"))

    def run(*args):
        heads_here = args[6].shape[1] // columns // HD
        groups = math.gcd(heads_here, seq)
        fine = Mesh(
            mesh.devices.reshape(halves, groups, seq // groups, columns), ("cfg", "z", "t", "wt")
        )
        seq_axes = ("z", "t")
        weight = P(("cfg", "z", "t"), "wt")
        return jax.shard_map(
            on_device,
            mesh=fine,
            in_specs=(
                P("cfg", seq_axes, None),
                P(seq_axes, "cfg"),
                P(),
                P(seq_axes, None),
                P(None, "cfg", None, "wt"),
                P("cfg", None),
                weight,
                weight,
                weight,
                weight,
                weight,
                weight,
                P(),
                P(),
                P(),
            ),
            out_specs=(P("cfg", seq_axes, "wt"), P(seq_axes, "cfg")),
            check_vma=False,
        )(*args)

    return run
```

```python
import math

import jax
import jax.numpy as jnp
import numpy as np
from jax import lax
from jax.experimental import pallas as pl
from jax.experimental.pallas import tpu as pltpu
from jax.sharding import Mesh
from jax.sharding import PartitionSpec as P

HD = 128
TEXT = 512
TENANTS = 4
EPS = 1e-06
CHUNKS = 2
BF = jnp.bfloat16
F32 = jnp.float32


def flip(block, axis):
    return lax.ppermute(block, axis, [(0, 1), (1, 0)])


def rotary_tables():
    sixth = HD // 6
    table = np.zeros((3, HD), np.float32)
    lane = 0
    for column, span in enumerate((HD - 4 * sixth, 2 * sixth, 2 * sixth)):
        exponent = np.arange(0, span, 2).astype(np.float32) / np.float32(span)
        frequency = (1.0 / 10000.0**exponent).astype(np.float32)
        table[column, lane : lane + span] = np.repeat(frequency, 2)
        lane += span
    swap = np.zeros((HD, HD), np.float32)
    for pair in range(0, HD, 2):
        swap[pair + 1, pair] = -1.0
        swap[pair, pair + 1] = 1.0
    return table, swap


def running_ends(lengths):
    upto = np.tril(np.ones((TENANTS, TENANTS), np.int32))
    return jnp.sum(jnp.asarray(upto) * lengths[None, :], axis=1)


def head_scale(shaped):
    return lax.rsqrt(jnp.mean(shaped * shaped, axis=-1, keepdims=True) + EPS)


def attend(queries, keys, values, allowed):
    scores = jnp.einsum("qhd,khd->hqk", queries, keys, preferred_element_type=F32)
    scores = scores * (1.0 / math.sqrt(queries.shape[-1]))
    weights = jnp.where(allowed[None], jnp.exp(scores), 0.0).astype(BF)
    summed = jnp.einsum("hqk,khd->qhd", weights, values, preferred_element_type=F32)
    totals = jnp.sum(weights.astype(F32), axis=2).T
    return (summed / totals[..., None]).astype(BF).reshape(queries.shape[0], -1)


MESH = pl.DeviceIdType.MESH
NEAR = (1, 3, 2)
LINE = 4


def remote(src, dst, sent, got, device):
    return pltpu.make_async_remote_copy(
        src_ref=src, dst_ref=dst, send_sem=sent, recv_sem=got, device_id=device, device_id_type=MESH
    )


def meet(devices):
    barrier = pltpu.get_barrier_semaphore()
    for device in devices:
        pl.semaphore_signal(barrier, inc=1, device_id=device, device_id_type=MESH)
    pl.semaphore_wait(barrier, len(devices))


def span(index, size):
    return pl.ds(pl.multiple_of(index * size, size), size)


def nt_dot(a, b):
    return lax.dot_general(a, b, (((1,), (1,)), ((), ())), preferred_element_type=F32)


def tenants_at(index, lengths):
    found, end = jnp.zeros(index.shape, jnp.int32), 0
    for tenant in range(TENANTS):
        end = end + lengths[tenant]
        found = found + (index >= end).astype(jnp.int32)
    return found


def self_attention_kernel(
    lengths, pos, table, key_index, hid, wk, wv, wq, mixed_out, raw_out, mean_out,
    wide, rows, keys, vals, queries, pos_all, rot,
    loc_w, loc_h, zs, zr, hs, hr, ps, pr, xs, xr, cs, cr, ys, yr, ks, kr,
):
    c, z, x, y = (lax.axis_index(a) for a in ("cfg", "z", "t", "wt"))
    groups = LINE
    tok = hid.shape[0]
    depth = wk.shape[0]
    wid = rows.shape[2]
    cols = wide.shape[3]
    heads = cols // HD
    at_z = [{"z": lax.rem(z + d, groups)} for d in range(groups)]
    from_z = [lax.rem(z + groups - d, groups) for d in range(groups)]
    at_x, at_c, at_y = {"t": 1 - x}, {"cfg": 1 - c}, {"wt": 1 - y}
    at_line = ({"z": jnp.minimum(z + 1, groups - 1)}, {"z": jnp.maximum(z - 1, 0)})
    weights = (wk, wv, wq)
    mine = c * groups + z

    own_rows = [
        pltpu.make_async_copy(hid.at[:, kb * wid : (kb + 1) * wid], rows.at[kb, span(z, tok)], loc_h.at[kb])
        for kb in range(2 * groups)
    ]
    own_weights = [
        pltpu.make_async_copy(w.at[:, span(z, cols)], wide.at[j, mine, span(x, depth)], loc_w.at[j])
        for j, w in enumerate(weights)
    ]
    own_pos = pltpu.make_async_copy(pos, pos_all.at[z], loc_w.at[3])
    for copy in own_rows + [own_pos] + own_weights:
        copy.start()
    meet([at_z[1], at_z[2], at_z[3], at_x, at_c, at_y])

    def block(j, d, column):
        return wide.at[j, c * groups + from_z[d], span(column, depth)]

    def x_copy(j, d):
        return remote(block(j, d, x), block(j, d, x), xs.at[d, j], xr.at[d, j], at_x)

    def x_arrival(j, d):
        return remote(block(j, d, 1 - x), block(j, d, 1 - x), xs.at[d, j], xr.at[d, j], at_x)

    def c_copy(j, d, second):
        part = block(j, d, 1 - x if second else x)
        return remote(part, part, cs.at[second, d, j], cr.at[second, d, j], at_c)

    def c_arrival(j, d, second):
        part = wide.at[j, (1 - c) * groups + from_z[d], span(1 - x if second else x, depth)]
        return remote(part, part, cs.at[second, d, j], cr.at[second, d, j], at_c)

    def z_copy(j, d):
        target = lax.rem(z + d, groups)
        return remote(
            weights[j].at[:, span(target, cols)], wide.at[j, mine, span(x, depth)], zs.at[d - 1, j], zr.at[d - 1, j], at_z[d]
        )

    def z_arrival(j, d):
        return remote(block(j, d, x), block(j, d, x), zs.at[d - 1, j], zr.at[d - 1, j], at_z[d])

    def rows_of(b, column):
        return rows.at[pl.ds(pl.multiple_of(column * groups, groups), groups), span(b, tok)]

    def line_block(way, s):
        return z - s if way == 0 else z + s

    def line_sends(way, s):
        if way == 0:
            return jnp.logical_and(z - s >= 0, z + 1 < groups)
        return jnp.logical_and(z + s < groups, z >= 1)

    def line_gets(way, s):
        return z - 1 - s >= 0 if way == 0 else z + 1 + s < groups

    def h_copy(way, s):
        part = rows_of(line_block(way, s), y)
        return remote(part, part, hs.at[way, s], hr.at[way, s], at_line[way])

    def h_arrival(way, s):
        part = rows_of(line_block(way, s + 1), y)
        return remote(part, part, hs.at[way, s], hr.at[way, s], at_line[way])

    def y_copy(way, s):
        part = rows_of(line_block(way, s + 1), y)
        return remote(part, part, ys.at[way, s], yr.at[way, s], at_y)

    def y_arrival(way, s):
        part = rows_of(line_block(way, s + 1), 1 - y)
        return remote(part, part, ys.at[way, s], yr.at[way, s], at_y)

    def p_copy(d):
        return remote(pos_all.at[z], pos_all.at[z], ps.at[d - 1], pr.at[d - 1], at_z[d])

    def p_arrival(d):
        part = pos_all.at[from_z[d]]
        return remote(part, part, ps.at[d - 1], pr.at[d - 1], at_z[d])

    def hidden_step(s):
        for way in (0, 1):
            @pl.when(line_gets(way, s))
            def _():
                h_arrival(way, s).wait_recv()
                if s + 1 < groups - 1:
                    @pl.when(line_sends(way, s + 1))
                    def _():
                        h_copy(way, s + 1).start()
                y_copy(way, s).start()

    for copy in own_rows + [own_pos]:
        copy.wait()
    for way in (0, 1):
        @pl.when(line_sends(way, 0))
        def _():
            h_copy(way, 0).start()
    for d in NEAR:
        p_copy(d).start()
    for j in range(3):
        own_weights[j].wait()
        x_copy(j, 0).start()
        c_copy(j, 0, 0).start()
    for d in NEAR:
        z_copy(0, d).start()
    hidden_step(0)
    for d in NEAR:
        z_copy(1, d).start()
    for j in range(3):
        x_arrival(j, 0).wait_recv()
        c_copy(j, 0, 1).start()
    hidden_step(1)
    for d in NEAR:
        z_copy(2, d).start()

    def relay(j, d):
        z_arrival(j, d).wait_recv()
        x_copy(j, d).start()
        c_copy(j, d, 0).start()

    def second_relay(j, d):
        x_arrival(j, d).wait_recv()
        c_copy(j, d, 1).start()

    relay(0, NEAR[0])
    relay(0, NEAR[1])
    hidden_step(2)
    relay(0, NEAR[2])
    for d in NEAR:
        second_relay(0, d)

    for d in NEAR:
        p_arrival(d).wait_recv()
    lane = lax.broadcasted_iota(jnp.int32, (tok, HD), 1)
    even = lax.rem(lane, 2) == 0
    for m in range(groups):
        held = pos_all[m]
        full = jnp.concatenate([held, jnp.zeros((HD - held.shape[0], held.shape[1]), F32)], axis=0)
        column = jnp.transpose(full)[:tok]
        angles = sum(column[:, a : a + 1] * table[a : a + 1, :] for a in range(3))
        rot[0, m * tok : (m + 1) * tok] = jnp.cos(angles)
        sinus = jnp.sin(angles)
        rot[1, m * tok : (m + 1) * tok] = jnp.where(even, -sinus, sinus)

    for s in range(groups - 1):
        for way in (0, 1):
            @pl.when(line_gets(way, s))
            def _():
                y_arrival(way, s).wait_recv()
                y_copy(way, s).wait_send()

            @pl.when(line_sends(way, s))
            def _():
                h_copy(way, s).wait_send()
    raw_out[0] = rows[z]
    raw_out[1] = rows[groups + z]
    some = 16
    width = 2 * groups * wid

    def norm(i, carry):
        these = span(i, some)
        total = jnp.zeros((some, wid), F32)
        for kb in range(2 * groups):
            total += rows[kb, these].astype(F32)
        mean = jnp.sum(total, axis=1, keepdims=True) / width
        total = jnp.zeros((some, wid), F32)
        for kb in range(2 * groups):
            centred = rows[kb, these].astype(F32) - mean
            total += centred * centred
        scale = lax.rsqrt(jnp.sum(total, axis=1, keepdims=True) / width + EPS)
        for kb in range(2 * groups):
            rows[kb, these] = ((rows[kb, these].astype(F32) - mean) * scale).astype(BF)
        mean_out[these] = mean
        return carry

    lax.fori_loop(0, groups * tok // some, norm, 0)

    def project(j, store):
        for d in range(groups):
            c_arrival(j, d, 0).wait_recv()
            c_arrival(j, d, 1).wait_recv()

        def step(m, carry):
            total = jnp.dot(rows[0, span(m, tok)], wide[j, 0], preferred_element_type=F32)
            for kb in range(1, 2 * groups):
                total += jnp.dot(rows[kb, span(m, tok)], wide[j, kb], preferred_element_type=F32)
            store(span(m, tok), total)
            return carry

        lax.fori_loop(0, groups, step, 0)

    def rotated(these, total):
        turned = []
        for h in range(heads):
            part = total[:, h * HD : (h + 1) * HD]
            scale = lax.rsqrt(jnp.mean(part * part, axis=1, keepdims=True) + EPS)
            swapped = jnp.where(even, pltpu.roll(part, HD - 1, 1), pltpu.roll(part, 1, 1))
            turned.append((part * rot[0, these] + swapped * rot[1, these]) * scale)
        return jnp.concatenate(turned, axis=1).astype(BF)

    def store_keys(these, total):
        keys[x, these] = rotated(these, total)

    def store_values(these, total):
        vals[x, these] = total.astype(BF)

    def store_queries(these, total):
        queries[these] = rotated(these, total)

    def kv_copy(i):
        held = (keys, vals)[i].at[x]
        return remote(held, held, ks.at[i], kr.at[i], at_x)

    def kv_arrival(i):
        held = (keys, vals)[i].at[1 - x]
        return remote(held, held, ks.at[i], kr.at[i], at_x)

    project(0, store_keys)
    kv_copy(0).start()
    for d in NEAR:
        relay(1, d)
    for d in NEAR:
        second_relay(1, d)
    project(1, store_values)
    kv_copy(1).start()
    for d in NEAR:
        relay(2, d)
    for d in NEAR:
        second_relay(2, d)
    project(2, store_queries)
    kv_arrival(0).wait_recv()
    kv_arrival(1).wait_recv()

    key_tenant = tenants_at(key_index[0:1], lengths)
    ones = jnp.ones((groups * tok, HD), BF)

    def attend_block(m, carry):
        these = span(m, tok)
        index = lax.broadcasted_iota(jnp.int32, (tok, 1), 0) + (m * 2 + x) * tok
        allowed = tenants_at(index, lengths) == key_tenant
        for h in range(heads):
            lanes = slice(h * HD, (h + 1) * HD)
            summed = jnp.zeros((tok, 2 * HD), F32)
            for part in (0, 1):
                scores = nt_dot(queries[these, lanes], keys[part, :, lanes]) * (1.0 / math.sqrt(HD))
                here = allowed[:, part * groups * tok : (part + 1) * groups * tok]
                chances = jnp.where(here, jnp.exp(scores), 0.0).astype(BF)
                both = jnp.concatenate([vals[part, :, lanes], ones], axis=1)
                summed += jnp.dot(chances, both, preferred_element_type=F32)
            mixed_out[these, lanes] = (summed[:, :HD] / summed[:, HD:]).astype(BF)
        return carry

    lax.fori_loop(0, groups, attend_block, 0)

    for d in NEAR:
        p_copy(d).wait_send()
        for j in range(3):
            z_copy(j, d).wait_send()
    for d in range(groups):
        for j in range(3):
            x_copy(j, d).wait_send()
            c_copy(j, d, 0).wait_send()
            c_copy(j, d, 1).wait_send()
    kv_copy(0).wait_send()
    kv_copy(1).wait_send()


def self_attention_call(lengths, hidden, positions, wk, wv, wq):
    tok, width = hidden.shape
    groups = LINE
    depth, local_cols = wk.shape
    cols = local_cols // groups
    rows = groups * tok
    wid = width // (2 * groups)
    anywhere = pl.BlockSpec(memory_space=pl.ANY)
    vmem = pl.BlockSpec(memory_space=pltpu.VMEM)
    smem = pl.BlockSpec(memory_space=pltpu.SMEM)
    dma = pltpu.SemaphoreType.DMA
    made = [
        jax.ShapeDtypeStruct((rows, cols), BF),
        jax.ShapeDtypeStruct((2, rows, wid), BF),
        jax.ShapeDtypeStruct((rows, 1), F32),
    ]
    table = np.zeros((8, HD), np.float32)
    table[:3] = rotary_tables()[0]
    place = np.arange(2 * rows)
    place = (place % rows // tok * 2 + place // rows) * tok + place % tok
    place = np.broadcast_to(place.astype(np.int32), (8, 2 * rows))
    pos = jnp.pad(positions.T.astype(F32), ((0, 5), (0, -tok % 128)))
    return pl.pallas_call(
        self_attention_kernel,
        out_shape=made,
        in_specs=[smem, vmem, vmem, vmem] + [anywhere] * 4,
        out_specs=[vmem] * 3,
        scratch_shapes=[
            pltpu.VMEM((3, 2 * groups, 2 * depth, cols), BF),
            pltpu.VMEM((2 * groups, rows, wid), BF),
            pltpu.VMEM((2, rows, cols), BF),
            pltpu.VMEM((2, rows, cols), BF),
            pltpu.VMEM((rows, cols), BF),
            pltpu.VMEM((groups,) + pos.shape, F32),
            pltpu.VMEM((2, rows, HD), F32),
            dma((4,)), dma((2 * groups,)),
            dma((3, 3)), dma((3, 3)),
            dma((2, 3)), dma((2, 3)),
            dma((3,)), dma((3,)),
            dma((4, 3)), dma((4, 3)),
            dma((2, 4, 3)), dma((2, 4, 3)),
            dma((2, 3)), dma((2, 3)),
            dma((2,)), dma((2,)),
        ],
        compiler_params=pltpu.CompilerParams(
            collective_id=0, has_side_effects=True, vmem_limit_bytes=56 * 2**20
        ),
        cost_estimate=pl.CostEstimate(
            flops=6 * rows * width * cols, bytes_accessed=20 * 2**20, transcendentals=0
        ),
    )(lengths, pos, jnp.asarray(table), jnp.asarray(place), hidden, wk, wv, wq)


def on_device(
    hidden,
    latent,
    tenant_lengths,
    grid_positions,
    text_kv,
    text_lengths,
    w_query,
    w_key,
    w_value,
    w_out,
    w_cross_query,
    w_cross_out,
    w_head,
    guidance,
    step_size,
):
    halves, groups, parts, columns = (lax.axis_size(a) for a in ("cfg", "z", "t", "wt"))
    half_index, z_index, t_index, wt_index = (
        lax.axis_index(a) for a in ("cfg", "z", "t", "wt")
    )
    tok, width = hidden.shape[1:]
    rows = groups * tok
    local_cols = w_query.shape[1]
    my_cols = local_cols // groups
    heads = my_cols // HD
    paired = halves == 2 and parts == 2
    block = w_query.shape[0]
    ends = running_ends(tenant_lengths)

    def tenant_of(indices):
        return jnp.sum((indices[:, None] >= ends[None, :]).astype(jnp.int32), axis=1)

    def ordered(mine, other, index):
        return jnp.where(
            index == 0, jnp.concatenate([mine, other]), jnp.concatenate([other, mine])
        )

    def wide(w):
        if not paired:
            return lax.all_gather(w, ("cfg", "t"), axis=0, tiled=True)
        two = ordered(w, flip(w, "t"), t_index)
        return ordered(two, flip(two, "cfg"), half_index)

    def over_groups(x):
        return x if groups == 1 else lax.all_to_all(x, "z", 0, 0, tiled=True)

    def join_groups(x):
        if groups == 1:
            return x
        x = lax.all_gather(x, "z", axis=0)
        return jnp.swapaxes(x, 0, 1).reshape(x.shape[1], local_cols)

    def sum_at_owner(x):
        if groups == 1:
            return x[0].astype(F32)
        return jnp.sum(lax.all_to_all(x, "z", 0, 0).astype(F32), axis=0)

    def sum_groups(x):
        if groups == 1:
            return x
        return lax.psum_scatter(x, "z", scatter_dimension=0, tiled=True)

    def to_groups(x, n):
        return jnp.swapaxes(x.reshape(x.shape[0], groups, n), 0, 1)

    def both_columns(terms):
        terms = terms.astype(BF)
        if columns == 1:
            return terms.astype(F32)
        if columns == 2:
            return terms.astype(F32) + flip(terms, "wt").astype(F32)
        return lax.psum(terms, "wt").astype(F32)

    fast = paired and groups == 4 and columns == 2 and tok % 16 == 0 and block % 16 == 0
    fast = fast and my_cols % 128 == 0 and width == 16 * block
    if fast:
        wide_key = wide_query = wide_value = None
    elif paired:
        key_pair = ordered(w_key, flip(w_key, "t"), t_index)
        key_pair, w_query, w_value = lax.optimization_barrier((key_pair, w_query, w_value))
        wide_key = ordered(key_pair, flip(key_pair, "cfg"), half_index)
    else:
        wide_key = wide(w_key)
    if not fast:
        wide_query, wide_value = wide(w_query), wide(w_value)
    wide_out, wide_cross, wide_cross_out = wide(w_out), wide(w_cross_query), wide(w_cross_out)

    chunks = CHUNKS if groups > 1 and tok % (CHUNKS * 16) == 0 else 1
    part = tok // chunks
    chunk_rows = rows // chunks

    def by_chunk(x):
        shape = (groups, chunks, part) + x.shape[2:]
        return jnp.swapaxes(x.reshape(shape), 0, 1).reshape((rows,) + x.shape[2:])

    def chunked(x):
        return by_chunk(x.reshape((groups, tok) + x.shape[1:]))

    def three_terms(x):
        high = lax.reduce_precision(x, 8, 7)
        middle = lax.reduce_precision(x - high, 8, 7)
        return [term.astype(BF) for term in (high, middle, x - high - middle)]

    slice_width = width // groups
    if fast:
        all_mixed, raw, mean = self_attention_call(
            tenant_lengths, hidden[0], grid_positions, w_key, w_value, w_query
        )
        facts = chunked(mean)
        sliced = chunked(jnp.concatenate([raw[0], raw[1]], axis=1)).astype(F32)
        all_mixed = chunked(all_mixed)
    else:
        own = hidden[0].astype(F32)
        mean = jnp.mean(own, axis=-1, keepdims=True)
        centred = own - mean
        scale = lax.rsqrt(jnp.mean(centred * centred, axis=-1, keepdims=True) + EPS)
        facts = jnp.concatenate([mean, scale, grid_positions.astype(F32)], axis=1)
        if groups == 1:
            sliced = own
        else:
            extra = jnp.concatenate(three_terms(facts), axis=1)
            extra = jnp.pad(extra, ((0, 0), (0, 128 - extra.shape[1])))
            features = hidden[0].reshape(tok, halves, groups, slice_width // halves)
            features = jnp.concatenate(
                [features[:, half] for half in range(halves)]
                + [jnp.broadcast_to(extra[:, None], (tok, groups, 128))],
                axis=2,
            )
            arrived = lax.all_to_all(jnp.swapaxes(features, 0, 1), "z", 0, 0)
            arrived = by_chunk(arrived).astype(F32)
            sliced = arrived[:, :slice_width]
            extra = arrived[:, slice_width : slice_width + 15]
            facts = extra[:, 0:5] + extra[:, 5:10] + extra[:, 10:15]
        normed = ((sliced - facts[:, 0:1]) * facts[:, 1:2]).astype(BF)

        def project(w):
            return to_groups(jnp.dot(normed, w, preferred_element_type=F32).astype(BF), my_cols)

        projected_keys = sum_at_owner(project(wide_key)).astype(BF)
        projected = jnp.concatenate([project(wide_query), project(wide_value)], axis=2)
        projected = sum_groups(projected.reshape(groups * rows, 2 * my_cols))

        table, swap = rotary_tables()
        angles = (
            facts[:, 2:3] * table[0][None] + facts[:, 3:4] * table[1][None] + facts[:, 4:5] * table[2][None]
        )
        cosine, sinus = jnp.cos(angles)[:, None, :], jnp.sin(angles)[:, None, :]

        def rotated(x):
            shaped = x.reshape(rows, heads, HD)
            swapped = jnp.einsum("thd,de->the", shaped, jnp.asarray(swap, BF), preferred_element_type=F32)
            shaped = shaped.astype(F32)
            return ((shaped * cosine + swapped * sinus) * head_scale(shaped)).astype(BF)

        keys = rotated(projected_keys).reshape(rows, my_cols)
        queries = rotated(projected[:, :my_cols])
        values = projected[:, my_cols:]

    base = jnp.arange(groups, dtype=jnp.int32)[:, None] * (parts * tok)
    base = by_chunk(base + jnp.arange(tok, dtype=jnp.int32)[None])
    my_tenant = tenant_of(base + t_index * tok)
    if fast:
        pass
    elif parts == 2:
        keys = jnp.concatenate([keys, flip(keys, "t")], axis=0)
        values = jnp.concatenate([values, flip(values, "t")], axis=0)
        key_tenant = jnp.concatenate([my_tenant, tenant_of(base + (1 - t_index) * tok)])
    else:
        keys = lax.all_gather(keys, "t", axis=0, tiled=True)
        values = lax.all_gather(values, "t", axis=0, tiled=True)
        key_tenant = tenant_of(
            (jnp.arange(parts, dtype=jnp.int32)[:, None] * tok + base[None]).reshape(-1)
        )
    if not fast:
        keys = keys.reshape(-1, heads, HD)
        values = values.reshape(-1, heads, HD)

    spans = [slice(i * chunk_rows, (i + 1) * chunk_rows) for i in range(chunks)]
    mixed = [all_mixed[i] for i in spans] if fast else [
        attend(queries[i], keys, values, my_tenant[i][:, None] == key_tenant[None, :])
        for i in spans
    ]

    def project_out(mixed, weight):
        return lax.dot_general(
            join_groups(mixed), weight, (((1,), (1,)), ((), ())), preferred_element_type=F32
        )

    column_sums = jnp.dot(jnp.ones((8, slice_width), BF), wide_cross, preferred_element_type=F32)
    column_sums = column_sums[0].reshape(groups, 1, my_cols)
    riding = groups > 1 and chunk_rows <= my_cols

    text = lax.dynamic_slice_in_dim(text_kv[:, 0], z_index * my_cols, my_cols, 2)
    text_keys = text[0].reshape(-1, heads, HD).astype(F32)
    text_keys = (text_keys * head_scale(text_keys)).astype(BF)
    text_values = text[1].reshape(-1, heads, HD)
    text_index = jnp.arange(text_kv.shape[2], dtype=jnp.int32)
    text_tenant = text_index // TEXT
    slots = text_tenant[:, None] == jnp.arange(TENANTS, dtype=jnp.int32)[None, :]
    live_length = jnp.sum(jnp.where(slots, text_lengths[0][None, :], 0), axis=1)
    live = text_index % TEXT < live_length

    states, cross_mixed = [], []
    for i, block_mixed in zip(spans, mixed):
        shifted = (sliced[i] - facts[i, 0:1]) + both_columns(project_out(block_mixed, wide_out))
        states.append(shifted)
        sums = jnp.stack([jnp.sum(shifted, axis=1), jnp.sum(shifted * shifted, axis=1)])
        crossed = jnp.dot(shifted.astype(BF), wide_cross, preferred_element_type=F32).astype(BF)
        crossed = to_groups(crossed, my_cols)
        if riding:
            sums = jnp.concatenate(three_terms(sums))
            sums = jnp.pad(sums, ((0, 0), (0, my_cols - chunk_rows)))
            sums = jnp.broadcast_to(sums[None], (groups,) + sums.shape)
            below = jnp.concatenate([sums] + three_terms(column_sums), axis=1)
            below = jnp.pad(below, ((0, 0), (0, 16 - below.shape[1]), (0, 0)))
            arrived = sum_at_owner(jnp.concatenate([crossed, below], axis=1))
            crossed, below = arrived[:chunk_rows], arrived[chunk_rows:]
            sums = (below[0:2] + below[2:4] + below[4:6])[:, :chunk_rows]
            all_columns = below[6:7] + below[7:8] + below[8:9]
        else:
            sums = sum_at_owner(jnp.broadcast_to(sums[None], (groups,) + sums.shape))
            all_columns = sum_at_owner(column_sums)
            crossed = sum_at_owner(crossed)
        sums = sums / width
        variance = jnp.maximum(sums[1] - sums[0] * sums[0], 0.0)[:, None, None]
        shaped = (crossed - sums[0][:, None] * all_columns).reshape(chunk_rows, heads, HD)
        square = jnp.mean(shaped * shaped, axis=-1, keepdims=True)
        cross_queries = (shaped * lax.rsqrt(square + EPS * (variance + EPS))).astype(BF)
        allowed = (my_tenant[i][:, None] == text_tenant[None, :]) & live[None]
        cross_mixed.append(attend(cross_queries, text_keys, text_values, allowed))

    channels = w_head.shape[1]
    head_rows = lax.dynamic_index_in_dim(
        w_head.reshape(halves, groups, parts * block, channels), z_index, 1, keepdims=False
    ).reshape(-1, channels)
    totals = jnp.sum(w_head.astype(F32), axis=0)[None]
    out_width = width // columns

    leaving, sums = [], []
    for i, shifted, block_mixed in zip(spans, states, cross_mixed):
        shifted = shifted + both_columns(project_out(block_mixed, wide_cross_out))
        final = (shifted + facts[i, 0:1]).astype(BF)
        if groups > 1 and columns == halves:
            span = slice_width // halves
            final = lax.dynamic_slice_in_dim(final, wt_index * span, span, 1)
        leaving.append(final.reshape(groups, part, -1))
        some = jnp.concatenate(
            [
                jnp.dot(shifted.astype(BF), head_rows, preferred_element_type=F32),
                jnp.sum(shifted, axis=1, keepdims=True),
                jnp.sum(shifted * shifted, axis=1, keepdims=True),
            ],
            axis=1,
        )
        sums.append(some.reshape(groups, part, channels + 2))
    sums = sum_at_owner(jnp.concatenate(sums, axis=1))
    mean = sums[:, channels : channels + 1] / width
    variance = jnp.maximum(sums[:, channels + 1 :] / width - mean * mean, 0.0)
    velocity = (sums[:, :channels] - mean * totals) * lax.rsqrt(variance + EPS)

    leaving = jnp.concatenate(leaving, axis=1)
    if groups == 1:
        hidden_out = lax.dynamic_slice_in_dim(leaving[0], wt_index * out_width, out_width, 1)
    else:
        leaving = jnp.swapaxes(lax.all_to_all(leaving, "z", 0, 0), 0, 1)
        if columns == halves:
            hidden_out = leaving.reshape(tok, out_width)
        else:
            leaving = jnp.swapaxes(leaving.reshape(tok, groups, halves, -1), 1, 2)
            hidden_out = lax.dynamic_slice_in_dim(
                leaving.reshape(tok, width), wt_index * out_width, out_width, 1
            )

    channel_half = latent.shape[1]
    outgoing = lax.dynamic_slice_in_dim(velocity, (1 - half_index) * channel_half, channel_half, 1)
    partner = flip(outgoing, "cfg")
    own_part = lax.dynamic_slice_in_dim(velocity, half_index * channel_half, channel_half, 1)
    conditional = jnp.where(half_index == 0, own_part, partner)
    null_text = jnp.where(half_index == 0, partner, own_part)
    latent_next = latent + step_size[0] * (null_text + guidance[0] * (conditional - null_text))
    return (hidden_out[None], latent_next)


def solution(mesh):
    halves, seq, columns = (mesh.shape[a] for a in ("cfg", "seq", "wt"))

    def run(*args):
        heads_here = args[6].shape[1] // columns // HD
        groups = math.gcd(heads_here, seq)
        fine = Mesh(
            mesh.devices.reshape(halves, groups, seq // groups, columns), ("cfg", "z", "t", "wt")
        )
        seq_axes = ("z", "t")
        weight = P(("cfg", "z", "t"), "wt")
        return jax.shard_map(
            on_device,
            mesh=fine,
            in_specs=(
                P("cfg", seq_axes, None),
                P(seq_axes, "cfg"),
                P(),
                P(seq_axes, None),
                P(None, "cfg", None, "wt"),
                P("cfg", None),
                weight,
                weight,
                weight,
                weight,
                weight,
                weight,
                P(),
                P(),
                P(),
            ),
            out_specs=(P("cfg", seq_axes, "wt"), P(seq_axes, "cfg")),
            check_vma=False,
        )(*args)

    return run
```

```python
import math

import jax
import jax.numpy as jnp
import numpy as np
from jax import lax
from jax.experimental import pallas as pl
from jax.experimental.pallas import tpu as pltpu
from jax.sharding import Mesh
from jax.sharding import PartitionSpec as P

HD = 128
TEXT = 512
TENANTS = 4
EPS = 1e-06
CHUNKS = 2
BF = jnp.bfloat16
F32 = jnp.float32


def flip(block, axis):
    return lax.ppermute(block, axis, [(0, 1), (1, 0)])


def rotary_tables():
    sixth = HD // 6
    table = np.zeros((3, HD), np.float32)
    lane = 0
    for column, span in enumerate((HD - 4 * sixth, 2 * sixth, 2 * sixth)):
        exponent = np.arange(0, span, 2).astype(np.float32) / np.float32(span)
        frequency = (1.0 / 10000.0**exponent).astype(np.float32)
        table[column, lane : lane + span] = np.repeat(frequency, 2)
        lane += span
    swap = np.zeros((HD, HD), np.float32)
    for pair in range(0, HD, 2):
        swap[pair + 1, pair] = -1.0
        swap[pair, pair + 1] = 1.0
    return table, swap


def running_ends(lengths):
    upto = np.tril(np.ones((TENANTS, TENANTS), np.int32))
    return jnp.sum(jnp.asarray(upto) * lengths[None, :], axis=1)


def head_scale(shaped):
    return lax.rsqrt(jnp.mean(shaped * shaped, axis=-1, keepdims=True) + EPS)


def attend(queries, keys, values, allowed):
    scores = jnp.einsum("qhd,khd->hqk", queries, keys, preferred_element_type=F32)
    scores = scores * (1.0 / math.sqrt(queries.shape[-1]))
    weights = jnp.where(allowed[None], jnp.exp(scores), 0.0).astype(BF)
    summed = jnp.einsum("hqk,khd->qhd", weights, values, preferred_element_type=F32)
    totals = jnp.sum(weights.astype(F32), axis=2).T
    return (summed / totals[..., None]).astype(BF).reshape(queries.shape[0], -1)


MESH = pl.DeviceIdType.MESH
NEAR = (1, 3, 2)
LINE = 4


def remote(src, dst, sent, got, device):
    return pltpu.make_async_remote_copy(
        src_ref=src, dst_ref=dst, send_sem=sent, recv_sem=got, device_id=device, device_id_type=MESH
    )


def meet(devices):
    barrier = pltpu.get_barrier_semaphore()
    for device in devices:
        pl.semaphore_signal(barrier, inc=1, device_id=device, device_id_type=MESH)
    pl.semaphore_wait(barrier, len(devices))


def span(index, size):
    return pl.ds(pl.multiple_of(index * size, size), size)


def nt_dot(a, b):
    return lax.dot_general(a, b, (((1,), (1,)), ((), ())), preferred_element_type=F32)


def tenants_at(index, lengths):
    found, end = jnp.zeros(index.shape, jnp.int32), 0
    for tenant in range(TENANTS):
        end = end + lengths[tenant]
        found = found + (index >= end).astype(jnp.int32)
    return found


def self_attention_kernel(
    lengths, pos, table, key_index, hid, wk, wv, wq, mixed_out, raw_out, mean_out,
    wide, rows, normed, keys, vals, queries, pos_all, rot,
    loc_w, loc_h, raw_sem, zs, zr, hs, hr, ps, pr, xs, xr, cs, cr, ys, yr, ks, kr,
):
    c, z, x, y = (lax.axis_index(a) for a in ("cfg", "z", "t", "wt"))
    groups = LINE
    tok = hid.shape[0]
    depth = wk.shape[0]
    wid = rows.shape[2]
    cols = wide.shape[3]
    heads = cols // HD
    at_z = [{"z": lax.rem(z + d, groups)} for d in range(groups)]
    from_z = [lax.rem(z + groups - d, groups) for d in range(groups)]
    at_x, at_c, at_y = {"t": 1 - x}, {"cfg": 1 - c}, {"wt": 1 - y}
    at_line = ({"z": jnp.minimum(z + 1, groups - 1)}, {"z": jnp.maximum(z - 1, 0)})
    weights = (wk, wv, wq)
    mine = c * groups + z

    own_rows = [
        pltpu.make_async_copy(hid.at[:, kb * wid : (kb + 1) * wid], rows.at[kb, span(z, tok)], loc_h.at[kb])
        for kb in range(2 * groups)
    ]
    own_weights = [
        pltpu.make_async_copy(w.at[:, span(z, cols)], wide.at[j, mine, span(x, depth)], loc_w.at[j])
        for j, w in enumerate(weights)
    ]
    own_pos = pltpu.make_async_copy(pos, pos_all.at[z], loc_w.at[3])
    for copy in own_rows + [own_pos] + own_weights:
        copy.start()
    meet([at_z[1], at_z[2], at_z[3], at_x, at_c, at_y])

    def block(j, d, column):
        return wide.at[j, c * groups + from_z[d], span(column, depth)]

    def x_copy(j, d):
        return remote(block(j, d, x), block(j, d, x), xs.at[d, j], xr.at[d, j], at_x)

    def x_arrival(j, d):
        return remote(block(j, d, 1 - x), block(j, d, 1 - x), xs.at[d, j], xr.at[d, j], at_x)

    def c_copy(j, d, second):
        part = block(j, d, 1 - x if second else x)
        return remote(part, part, cs.at[second, d, j], cr.at[second, d, j], at_c)

    def c_arrival(j, d, second):
        part = wide.at[j, (1 - c) * groups + from_z[d], span(1 - x if second else x, depth)]
        return remote(part, part, cs.at[second, d, j], cr.at[second, d, j], at_c)

    def z_copy(j, d):
        target = lax.rem(z + d, groups)
        return remote(
            weights[j].at[:, span(target, cols)], wide.at[j, mine, span(x, depth)], zs.at[d - 1, j], zr.at[d - 1, j], at_z[d]
        )

    def z_arrival(j, d):
        return remote(block(j, d, x), block(j, d, x), zs.at[d - 1, j], zr.at[d - 1, j], at_z[d])

    def rows_of(b, column, piece):
        return rows.at[column * groups + piece, span(b, tok)]

    def line_block(way, s):
        return z - s if way == 0 else z + s

    def line_sends(way, s):
        if way == 0:
            return jnp.logical_and(z - s >= 0, z + 1 < groups)
        return jnp.logical_and(z + s < groups, z >= 1)

    def line_gets(way, s):
        return z - 1 - s >= 0 if way == 0 else z + 1 + s < groups

    def h_copy(way, s, p):
        part = rows_of(line_block(way, s), y, p)
        return remote(part, part, hs.at[way, s, p], hr.at[way, s, p], at_line[way])

    def h_arrival(way, s, p):
        part = rows_of(line_block(way, s + 1), y, p)
        return remote(part, part, hs.at[way, s, p], hr.at[way, s, p], at_line[way])

    def y_copy(way, s, p):
        part = rows_of(line_block(way, s + 1), y, p)
        return remote(part, part, ys.at[way, s, p], yr.at[way, s, p], at_y)

    def y_arrival(way, s, p):
        part = rows_of(line_block(way, s + 1), 1 - y, p)
        return remote(part, part, ys.at[way, s, p], yr.at[way, s, p], at_y)

    def p_copy(d):
        return remote(pos_all.at[z], pos_all.at[z], ps.at[d - 1], pr.at[d - 1], at_z[d])

    def p_arrival(d):
        part = pos_all.at[from_z[d]]
        return remote(part, part, ps.at[d - 1], pr.at[d - 1], at_z[d])

    def hidden_step(s):
        for p in range(groups):
            for way in (0, 1):
                @pl.when(line_gets(way, s))
                def _():
                    h_arrival(way, s, p).wait_recv()
                    if s + 1 < groups - 1:
                        @pl.when(line_sends(way, s + 1))
                        def _():
                            h_copy(way, s + 1, p).start()
                    y_copy(way, s, p).start()

    some = 16
    width = 2 * groups * wid

    def norm_block(b):
        def norm(i, carry):
            these = pl.ds(pl.multiple_of(b * tok + i * some, some), some)
            total = jnp.zeros((some, wid), F32)
            for kb in range(2 * groups):
                total += rows[kb, these].astype(F32)
            mean = jnp.sum(total, axis=1, keepdims=True) / width
            total = jnp.zeros((some, wid), F32)
            for kb in range(2 * groups):
                centred = rows[kb, these].astype(F32) - mean
                total += centred * centred
            scale = lax.rsqrt(jnp.sum(total, axis=1, keepdims=True) / width + EPS)
            for kb in range(2 * groups):
                normed[kb, these] = ((rows[kb, these].astype(F32) - mean) * scale).astype(BF)
            mean_out[these] = mean
            return carry

        lax.fori_loop(0, tok // some, norm, 0)

    def hidden_finish(s):
        for way in (0, 1):
            @pl.when(line_gets(way, s))
            def _():
                for p in range(groups):
                    y_arrival(way, s, p).wait_recv()
                norm_block(line_block(way, s + 1))

    for copy in own_rows + [own_pos]:
        copy.wait()
    for p in range(groups):
        for way in (0, 1):
            @pl.when(line_sends(way, 0))
            def _():
                h_copy(way, 0, p).start()
    for d in NEAR:
        p_copy(d).start()
    for j in range(3):
        for d in NEAR:
            z_copy(j, d).start()
    for j in range(3):
        own_weights[j].wait()
        x_copy(j, 0).start()
        c_copy(j, 0, 0).start()
    norm_block(z)

    def relay(j, d):
        z_arrival(j, d).wait_recv()
        x_copy(j, d).start()
        c_copy(j, d, 0).start()

    def second_relay(j, d):
        x_arrival(j, d).wait_recv()
        c_copy(j, d, 1).start()

    second_relay(0, 0)
    hidden_step(0)
    second_relay(1, 0)
    second_relay(2, 0)
    relay(0, NEAR[0])
    relay(0, NEAR[1])
    hidden_step(1)
    second_relay(0, NEAR[0])
    second_relay(0, NEAR[1])
    hidden_finish(0)
    relay(0, NEAR[2])
    relay(1, NEAR[0])
    relay(1, NEAR[1])
    hidden_step(2)
    second_relay(0, NEAR[2])
    second_relay(1, NEAR[0])
    second_relay(1, NEAR[1])
    hidden_finish(1)
    relay(1, NEAR[2])
    for d in NEAR:
        p_arrival(d).wait_recv()
    lane = lax.broadcasted_iota(jnp.int32, (tok, HD), 1)
    even = lax.rem(lane, 2) == 0
    for m in range(groups):
        held = pos_all[m]
        full = jnp.concatenate([held, jnp.zeros((HD - held.shape[0], held.shape[1]), F32)], axis=0)
        column = jnp.transpose(full)[:tok]
        angles = sum(column[:, a : a + 1] * table[a : a + 1, :] for a in range(3))
        rot[0, m * tok : (m + 1) * tok] = jnp.cos(angles)
        sinus = jnp.sin(angles)
        rot[1, m * tok : (m + 1) * tok] = jnp.where(even, -sinus, sinus)

    hidden_finish(2)

    def project(j, store):
        for d in range(groups):
            c_arrival(j, d, 0).wait_recv()
            c_arrival(j, d, 1).wait_recv()

        def step(m, carry):
            total = jnp.dot(normed[0, span(m, tok)], wide[j, 0], preferred_element_type=F32)
            for kb in range(1, 2 * groups):
                total += jnp.dot(normed[kb, span(m, tok)], wide[j, kb], preferred_element_type=F32)
            store(span(m, tok), total)
            return carry

        lax.fori_loop(0, groups, step, 0)

    def rotated(these, total):
        turned = []
        for h in range(heads):
            part = total[:, h * HD : (h + 1) * HD]
            scale = lax.rsqrt(jnp.mean(part * part, axis=1, keepdims=True) + EPS)
            swapped = jnp.where(even, pltpu.roll(part, HD - 1, 1), pltpu.roll(part, 1, 1))
            turned.append((part * rot[0, these] + swapped * rot[1, these]) * scale)
        return jnp.concatenate(turned, axis=1).astype(BF)

    def store_keys(these, total):
        keys[x, these] = rotated(these, total)

    def store_values(these, total):
        vals[x, these] = total.astype(BF)

    def store_queries(these, total):
        queries[these] = rotated(these, total)

    def kv_copy(i):
        held = (keys, vals)[i].at[x]
        return remote(held, held, ks.at[i], kr.at[i], at_x)

    def kv_arrival(i):
        held = (keys, vals)[i].at[1 - x]
        return remote(held, held, ks.at[i], kr.at[i], at_x)

    raws = [
        pltpu.make_async_copy(rows.at[half * groups + z], raw_out.at[half], raw_sem.at[half]) for half in (0, 1)
    ]
    for copy in raws:
        copy.start()
    project(0, store_keys)
    kv_copy(0).start()
    relay(2, NEAR[0])
    relay(2, NEAR[1])
    second_relay(1, NEAR[2])
    project(1, store_values)
    kv_copy(1).start()
    relay(2, NEAR[2])
    for d in NEAR:
        second_relay(2, d)
    project(2, store_queries)
    kv_arrival(0).wait_recv()
    kv_arrival(1).wait_recv()

    key_tenant = tenants_at(key_index[0:1], lengths)
    ones = jnp.ones((groups * tok, HD), BF)

    def attend_block(m, carry):
        these = span(m, tok)
        index = lax.broadcasted_iota(jnp.int32, (tok, 1), 0) + (m * 2 + x) * tok
        allowed = tenants_at(index, lengths) == key_tenant
        for h in range(heads):
            lanes = slice(h * HD, (h + 1) * HD)
            summed = jnp.zeros((tok, 2 * HD), F32)
            for part in (0, 1):
                scores = nt_dot(queries[these, lanes], keys[part, :, lanes]) * (1.0 / math.sqrt(HD))
                here = allowed[:, part * groups * tok : (part + 1) * groups * tok]
                chances = jnp.where(here, jnp.exp(scores), 0.0).astype(BF)
                both = jnp.concatenate([vals[part, :, lanes], ones], axis=1)
                summed += jnp.dot(chances, both, preferred_element_type=F32)
            mixed_out[these, lanes] = (summed[:, :HD] / summed[:, HD:]).astype(BF)
        return carry

    lax.fori_loop(0, groups, attend_block, 0)

    for copy in raws:
        copy.wait()
    for s in range(groups - 1):
        for way in (0, 1):
            for p in range(groups):
                @pl.when(line_gets(way, s))
                def _():
                    y_copy(way, s, p).wait_send()

                @pl.when(line_sends(way, s))
                def _():
                    h_copy(way, s, p).wait_send()
    for d in NEAR:
        p_copy(d).wait_send()
        for j in range(3):
            z_copy(j, d).wait_send()
    for d in range(groups):
        for j in range(3):
            x_copy(j, d).wait_send()
            c_copy(j, d, 0).wait_send()
            c_copy(j, d, 1).wait_send()
    kv_copy(0).wait_send()
    kv_copy(1).wait_send()


def self_attention_call(lengths, hidden, positions, wk, wv, wq):
    tok, width = hidden.shape
    groups = LINE
    depth, local_cols = wk.shape
    cols = local_cols // groups
    rows = groups * tok
    wid = width // (2 * groups)
    anywhere = pl.BlockSpec(memory_space=pl.ANY)
    vmem = pl.BlockSpec(memory_space=pltpu.VMEM)
    smem = pl.BlockSpec(memory_space=pltpu.SMEM)
    dma = pltpu.SemaphoreType.DMA
    made = [
        jax.ShapeDtypeStruct((rows, cols), BF),
        jax.ShapeDtypeStruct((2, rows, wid), BF),
        jax.ShapeDtypeStruct((rows, 1), F32),
    ]
    table = np.zeros((8, HD), np.float32)
    table[:3] = rotary_tables()[0]
    place = np.arange(2 * rows)
    place = (place % rows // tok * 2 + place // rows) * tok + place % tok
    place = np.broadcast_to(place.astype(np.int32), (8, 2 * rows))
    pos = jnp.pad(positions.T.astype(F32), ((0, 5), (0, -tok % 128)))
    return pl.pallas_call(
        self_attention_kernel,
        out_shape=made,
        in_specs=[smem, vmem, vmem, vmem] + [anywhere] * 4,
        out_specs=[vmem] * 3,
        scratch_shapes=[
            pltpu.VMEM((3, 2 * groups, 2 * depth, cols), BF),
            pltpu.VMEM((2 * groups, rows, wid), BF),
            pltpu.VMEM((2 * groups, rows, wid), BF),
            pltpu.VMEM((2, rows, cols), BF),
            pltpu.VMEM((2, rows, cols), BF),
            pltpu.VMEM((rows, cols), BF),
            pltpu.VMEM((groups,) + pos.shape, F32),
            pltpu.VMEM((2, rows, HD), F32),
            dma((4,)), dma((2 * groups,)), dma((2,)),
            dma((3, 3)), dma((3, 3)),
            dma((2, 3, 4)), dma((2, 3, 4)),
            dma((3,)), dma((3,)),
            dma((4, 3)), dma((4, 3)),
            dma((2, 4, 3)), dma((2, 4, 3)),
            dma((2, 3, 4)), dma((2, 3, 4)),
            dma((2,)), dma((2,)),
        ],
        compiler_params=pltpu.CompilerParams(
            collective_id=0, has_side_effects=True, vmem_limit_bytes=56 * 2**20
        ),
        cost_estimate=pl.CostEstimate(
            flops=6 * rows * width * cols, bytes_accessed=20 * 2**20, transcendentals=0
        ),
    )(lengths, pos, jnp.asarray(table), jnp.asarray(place), hidden, wk, wv, wq)


def line_places(z):
    def block(way, s):
        return z - s if way == 0 else z + s

    def sends(way, s):
        if way == 0:
            return jnp.logical_and(z - s >= 0, z + 1 < LINE)
        return jnp.logical_and(z + s < LINE, z >= 1)

    def gets(way, s):
        return z - 1 - s >= 0 if way == 0 else z + 1 + s < LINE

    return block, sends, gets


def pack_columns(first, second):
    tok = first.shape[0]
    lane = lax.broadcasted_iota(jnp.int32, (tok, HD), 1)
    both = jnp.where(lane == 0, first, jnp.where(lane == 1, second, 0.0))
    both = jnp.concatenate([both, jnp.zeros((-tok % HD, HD), F32)], axis=0)
    return jnp.transpose(both)[:8]


def unpack_columns(packed, tok):
    full = jnp.concatenate([packed, jnp.zeros((HD - packed.shape[0], packed.shape[1]), F32)], axis=0)
    column = jnp.transpose(full)[:tok]
    return column[:, 0:1], column[:, 1:2]


def cross_attention_kernel(
    lengths, text_lengths, guidance, step_size, mixed, raw, mean, head, latent, text_kv, w_out, w_cross, w_last,
    hidden_out, latent_out,
    wide, text, gath, own, left, right, left2, right2, kept, state, asked, answers, facts, facts_in, cols_out, cols_in,
    leaving, vel, vel_in, half_out, half_in, core_out, core_in,
    loc_w, loc_t, loc_g, loc_f, ws, wr, wcs, wcr, gs, gr, ys, yr, y2s, y2r, qs, qr, fs, fr, ss, sr, os_, or_, vs, vr, es, er,
):
    c, z, x, y = (lax.axis_index(a) for a in ("cfg", "z", "t", "wt"))
    groups = LINE
    rows, cols = mixed.shape
    tok = rows // groups
    depth = w_out.shape[0]
    wid = raw.shape[2]
    width = 2 * groups * wid
    heads = cols // HD
    channels = head.shape[1]
    slots = text.shape[1] // TENANTS
    at_z = [{"z": lax.rem(z + d, groups)} for d in range(groups)]
    from_z = [lax.rem(z + groups - d, groups) for d in range(groups)]
    at_x, at_c, at_y = {"t": 1 - x}, {"cfg": 1 - c}, {"wt": 1 - y}
    at_line = ({"z": jnp.minimum(z + 1, groups - 1)}, {"z": jnp.maximum(z - 1, 0)})
    line_block, line_sends, line_gets = line_places(z)
    weights = (w_out, w_cross, w_last)

    own_weights = [
        pltpu.make_async_copy(w, wide.at[j, c, span(x, depth)], loc_w.at[j]) for j, w in enumerate(weights)
    ]
    own_text = [pltpu.make_async_copy(text_kv.at[k, 0, :, span(z, cols)], text.at[k], loc_t.at[k]) for k in (0, 1)]
    for copy in own_weights + own_text:
        copy.start()
    own[0] = mixed[...].reshape(groups, tok, cols)
    meet([at_z[1], at_z[2], at_z[3], at_x, at_c, at_y])

    def g_local(f, i):
        return pltpu.make_async_copy(own.at[f, i], gath.at[f, i, :, span(z, cols)], loc_g.at[f, i])

    def g_copy(f, i, way, s):
        part = gath.at[f, i, :, span(line_block(way, s), cols)]
        return remote(own.at[f, i] if s == 0 else part, part, gs.at[f, i, way, s], gr.at[f, i, way, s], at_line[way])

    def g_arrival(f, i, way, s):
        part = gath.at[f, i, :, span(line_block(way, s + 1), cols)]
        return remote(part, part, gs.at[f, i, way, s], gr.at[f, i, way, s], at_line[way])

    def g_start(f, i):
        for way in (0, 1):
            @pl.when(line_sends(way, 0))
            def _():
                g_copy(f, i, way, 0).start()
        g_local(f, i).start()

    def g_step(f, i, s):
        for way in (0, 1):
            @pl.when(line_gets(way, s))
            def _():
                g_arrival(f, i, way, s).wait_recv()
                if s + 1 < groups - 1:
                    @pl.when(line_sends(way, s + 1))
                    def _():
                        g_copy(f, i, way, s + 1).start()
        if s == groups - 2:
            g_local(f, i).wait()

    def w_part(j, core, column):
        return wide.at[j, core, span(column, depth)]

    def w_copy(j):
        return remote(w_part(j, c, x), w_part(j, c, x), ws.at[j], wr.at[j], at_x)

    def w_arrival(j):
        return remote(w_part(j, c, 1 - x), w_part(j, c, 1 - x), ws.at[j], wr.at[j], at_x)

    def wc_copy(j, second):
        part = w_part(j, c, 1 - x if second else x)
        return remote(part, part, wcs.at[j, second], wcr.at[j, second], at_c)

    def wc_arrival(j, second):
        part = w_part(j, 1 - c, 1 - x if second else x)
        return remote(part, part, wcs.at[j, second], wcr.at[j, second], at_c)

    def w_relay(j):
        w_arrival(j).wait_recv()
        wc_copy(j, 1).start()

    def w_ready(j):
        wc_arrival(j, 0).wait_recv()
        wc_arrival(j, 1).wait_recv()

    for i in range(groups):
        g_start(0, i)
    for j in range(3):
        own_weights[j].wait()
        w_copy(j).start()
        wc_copy(j, 0).start()

    for copy in own_text:
        copy.wait()

    def norm_text(i, carry):
        these = span(i, HD)
        for h in range(heads):
            lanes = slice(h * HD, (h + 1) * HD)
            part = text[0, these, lanes].astype(F32)
            scale = lax.rsqrt(jnp.mean(part * part, axis=1, keepdims=True) + EPS)
            text[0, these, lanes] = (part * scale).astype(BF)
        return carry

    lax.fori_loop(0, text.shape[1] // HD, norm_text, 0)
    totals = jnp.sum(head[...].astype(F32), axis=0, keepdims=True)

    def y_copy(i):
        return remote(left.at[i], right.at[i], ys.at[i], yr.at[i], at_y)

    def y2_copy(i):
        return remote(left2.at[i], right2.at[i], y2s.at[i], y2r.at[i], at_y)

    def q_copy(i, d):
        return remote(asked.at[i, lax.rem(z + d, groups)], answers.at[i, z], qs.at[i, d - 1], qr.at[i, d - 1], at_z[d])

    def q_arrival(i, d):
        part = answers.at[i, from_z[d]]
        return remote(part, part, qs.at[i, d - 1], qr.at[i, d - 1], at_z[d])

    def f_copy(i, d):
        return remote(facts.at[i], facts_in.at[i, z], fs.at[i, d - 1], fr.at[i, d - 1], at_z[d])

    def f_arrival(i, d):
        part = facts_in.at[i, from_z[d]]
        return remote(part, part, fs.at[i, d - 1], fr.at[i, d - 1], at_z[d])

    def s_copy(d):
        return remote(cols_out.at[lax.rem(z + d, groups)], cols_in.at[z], ss.at[d - 1], sr.at[d - 1], at_z[d])

    def s_arrival(d):
        part = cols_in.at[from_z[d]]
        return remote(part, part, ss.at[d - 1], sr.at[d - 1], at_z[d])

    def project_out(i):
        for half in (0, 1):
            left[i, :, half * wid : (half + 1) * wid] = nt_dot(gath[0, i], wide[0, half]).astype(BF)
        y_copy(i).start()

    def sum_columns():
        ones = jnp.ones((16, wid), BF)
        for g in range(groups):
            lanes = slice(g * cols, (g + 1) * cols)
            total = jnp.dot(ones, wide[1, 0, :, lanes], preferred_element_type=F32)
            total += jnp.dot(ones, wide[1, 1, :, lanes], preferred_element_type=F32)
            cols_out[g] = total[:8]
        for d in NEAR:
            s_copy(d).start()

    def update(i):
        y_copy(i).wait_recv()
        these = slice(i * tok, (i + 1) * tok)
        shift = mean[these]
        first = second = jnp.zeros((tok, 1), F32)
        for half in (0, 1):
            lanes = slice(half * wid, (half + 1) * wid)
            both = left[i, :, lanes].astype(F32) + right[i, :, lanes].astype(F32)
            new = (raw[half, these].astype(F32) - shift) + both
            state[i, half] = new
            first += jnp.sum(new, axis=1, keepdims=True)
            second += jnp.sum(new * new, axis=1, keepdims=True)
        facts[i] = pack_columns(first, second)
        for d in NEAR:
            f_copy(i, d).start()
        for g in range(groups):
            lanes = slice(g * cols, (g + 1) * cols)
            part = jnp.dot(state[i, 0].astype(BF), wide[1, 0, :, lanes], preferred_element_type=F32)
            part += jnp.dot(state[i, 1].astype(BF), wide[1, 1, :, lanes], preferred_element_type=F32)
            asked[i, g] = part.astype(BF)
        for d in NEAR:
            q_copy(i, d).start()

    def cross(i):
        packed = facts[i]
        crossed = asked[i, z].astype(F32)
        column_sums = cols_out[z, 0:1]
        for d in NEAR:
            q_arrival(i, d).wait_recv()
            f_arrival(i, d).wait_recv()
            if i == 0:
                s_arrival(d).wait_recv()
            packed = packed + facts_in[i, from_z[d]]
            crossed = crossed + answers[i, from_z[d]].astype(F32)
            column_sums = column_sums + cols_in[from_z[d], 0:1]
        first, second = unpack_columns(packed, tok)
        average = first / width
        variance = jnp.maximum(second / width - average * average, 0.0)
        crossed = crossed - average * column_sums
        index = lax.broadcasted_iota(jnp.int32, (tok, 1), 0) + (i * 2 + x) * tok
        tenant = tenants_at(index, lengths)
        slot = lax.broadcasted_iota(jnp.int32, (1, slots), 1)
        ones = jnp.ones((slots, HD), BF)
        for h in range(heads):
            lanes = slice(h * HD, (h + 1) * HD)
            part = crossed[:, lanes]
            square = jnp.mean(part * part, axis=1, keepdims=True)
            query = (part * lax.rsqrt(square + EPS * (variance + EPS))).astype(BF)
            summed = jnp.zeros((tok, 2 * HD), F32)
            for t in range(TENANTS):
                these = slice(t * slots, (t + 1) * slots)
                scores = nt_dot(query, text[0, these, lanes]) * (1.0 / math.sqrt(HD))
                allowed = jnp.logical_and(tenant == t, slot < text_lengths[0, t])
                chances = jnp.where(allowed, jnp.exp(scores), 0.0).astype(BF)
                both = jnp.concatenate([text[1, these, lanes], ones], axis=1)
                summed += jnp.dot(chances, both, preferred_element_type=F32)
            own[1, i, :, lanes] = (summed[:, :HD] / summed[:, HD:]).astype(BF)
        g_start(1, i)

    def project_last(i):
        left2[i] = nt_dot(gath[1, i], wide[2, 1 - y]).astype(BF)
        y2_copy(i).start()
        kept[i] = nt_dot(gath[1, i], wide[2, y]).astype(BF)

    def o_remote(i):
        return remote(leaving.at[i], hidden_out.at[:, span(z, wid)], os_.at[i], or_.at[z], {"z": i})

    def o_local(i):
        return pltpu.make_async_copy(leaving.at[i], hidden_out.at[:, span(z, wid)], loc_f)

    def v_remote(i):
        return remote(vel.at[i], vel_in.at[z], vs.at[i], vr.at[z], {"z": i})

    def finish(i):
        y2_copy(i).wait_recv()
        these = slice(i * tok, (i + 1) * tok)
        final = state[i, y] + kept[i].astype(F32) + right2[i].astype(F32)
        leaving[i] = (final + mean[these]).astype(BF)

        @pl.when(z != i)
        def _():
            o_remote(i).start()

        @pl.when(z == i)
        def _():
            o_local(i).start()

        rows_here = pl.ds(pl.multiple_of((y * groups + z) * wid, wid), wid)
        some = jnp.dot(final.astype(BF), head[rows_here], preferred_element_type=F32)
        first = jnp.sum(final, axis=1, keepdims=True)
        second = jnp.sum(final * final, axis=1, keepdims=True)
        lane = lax.broadcasted_iota(jnp.int32, (tok, HD - channels), 1)
        tail = jnp.where(lane == 0, first, jnp.where(lane == 1, second, 0.0))
        vel[i] = jnp.concatenate([some, tail], axis=1)

        @pl.when(z != i)
        def _():
            v_remote(i).start()

    w_relay(0)
    g_step(0, 0, 0)
    g_step(0, 1, 0)
    g_step(0, 0, 1)
    g_step(0, 2, 0)
    g_step(0, 1, 1)
    g_step(0, 0, 2)
    w_ready(0)
    project_out(0)
    g_step(0, 3, 0)
    g_step(0, 2, 1)
    g_step(0, 1, 2)
    project_out(1)
    w_relay(1)
    g_step(0, 3, 1)
    g_step(0, 2, 2)
    project_out(2)
    w_ready(1)
    sum_columns()
    update(0)
    g_step(0, 3, 2)
    project_out(3)
    update(1)
    cross(0)
    update(2)
    w_relay(2)
    g_step(1, 0, 0)
    cross(1)
    update(3)
    g_step(1, 1, 0)
    g_step(1, 0, 1)
    cross(2)
    g_step(1, 2, 0)
    g_step(1, 1, 1)
    g_step(1, 0, 2)
    w_ready(2)
    project_last(0)
    cross(3)
    g_step(1, 3, 0)
    g_step(1, 2, 1)
    g_step(1, 1, 2)
    project_last(1)
    finish(0)
    g_step(1, 3, 1)
    g_step(1, 2, 2)
    project_last(2)
    finish(1)
    g_step(1, 3, 2)
    project_last(3)
    finish(2)
    finish(3)

    total = vel[z]
    for d in NEAR:
        part = vel_in.at[from_z[d]]
        remote(part, part, vs.at[d], vr.at[from_z[d]], at_z[d]).wait_recv()
        total = total + vel_in[from_z[d]]
    half_out[...] = total
    over_y = remote(half_out, half_in, es.at[0], er.at[0], at_y)
    over_y.start()
    over_y.wait()
    total = half_out[...] + half_in[...]
    average = total[:, channels : channels + 1] / width
    variance = jnp.maximum(total[:, channels + 1 : channels + 2] / width - average * average, 0.0)
    velocity = (total[:, :channels] - average * totals) * lax.rsqrt(variance + EPS)
    core_out[...] = jnp.concatenate([velocity, velocity], axis=1)
    over_c = remote(core_out, core_in, es.at[1], er.at[1], at_c)
    over_c.start()
    over_c.wait()
    span_out = latent.shape[1]
    mine, other = core_out[...], core_in[...]
    here = [jnp.where(c == 0, both[:, :span_out], both[:, span_out : 2 * span_out]) for both in (mine, other)]
    conditional = jnp.where(c == 0, here[0], here[1])
    null_text = jnp.where(c == 0, here[1], here[0])
    latent_out[...] = latent[...] + step_size[0] * (null_text + guidance[0] * (conditional - null_text))

    for d in NEAR:
        part = hidden_out.at[:, span(from_z[d], wid)]
        remote(part, part, os_.at[d], or_.at[from_z[d]], at_z[d]).wait_recv()
    for i in range(groups):
        @pl.when(z != i)
        def _():
            o_remote(i).wait_send()
            v_remote(i).wait_send()

        @pl.when(z == i)
        def _():
            o_local(i).wait()

        y_copy(i).wait_send()
        y2_copy(i).wait_send()
        for d in NEAR:
            q_copy(i, d).wait_send()
            f_copy(i, d).wait_send()
        for f in (0, 1):
            for way in (0, 1):
                for s in range(groups - 1):
                    @pl.when(line_sends(way, s))
                    def _():
                        g_copy(f, i, way, s).wait_send()
    for d in NEAR:
        s_copy(d).wait_send()
    for j in range(3):
        w_copy(j).wait_send()
        wc_copy(j, 0).wait_send()
        wc_copy(j, 1).wait_send()


def cross_attention_call(
    lengths, text_lengths, guidance, step_size, mixed, raw, mean, head, latent, text_kv, w_out, w_cross, w_last
):
    groups = LINE
    rows, cols = mixed.shape
    tok = rows // groups
    wid = raw.shape[2]
    depth, local_cols = w_out.shape
    padded = tok + -tok % HD
    anywhere = pl.BlockSpec(memory_space=pl.ANY)
    vmem = pl.BlockSpec(memory_space=pltpu.VMEM)
    smem = pl.BlockSpec(memory_space=pltpu.SMEM)
    dma = pltpu.SemaphoreType.DMA
    return pl.pallas_call(
        cross_attention_kernel,
        out_shape=[
            jax.ShapeDtypeStruct((tok, groups * wid), BF),
            jax.ShapeDtypeStruct(latent.shape, F32),
        ],
        in_specs=[smem] * 4 + [vmem] * 5 + [anywhere] * 4,
        out_specs=[anywhere, vmem],
        scratch_shapes=[
            pltpu.VMEM((3, 2, 2 * depth, local_cols), BF),
            pltpu.VMEM((2, text_kv.shape[2], cols), BF),
            pltpu.VMEM((2, groups, tok, local_cols), BF),
            pltpu.VMEM((2, groups, tok, cols), BF),
            pltpu.VMEM((groups, tok, 2 * wid), BF),
            pltpu.VMEM((groups, tok, 2 * wid), BF),
            pltpu.VMEM((groups, tok, wid), BF),
            pltpu.VMEM((groups, tok, wid), BF),
            pltpu.VMEM((groups, tok, wid), BF),
            pltpu.VMEM((groups, 2, tok, wid), F32),
            pltpu.VMEM((groups, groups, tok, cols), BF),
            pltpu.VMEM((groups, groups, tok, cols), BF),
            pltpu.VMEM((groups, 8, padded), F32),
            pltpu.VMEM((groups, groups, 8, padded), F32),
            pltpu.VMEM((groups, 8, cols), F32),
            pltpu.VMEM((groups, 8, cols), F32),
            pltpu.VMEM((groups, tok, wid), BF),
            pltpu.VMEM((groups, tok, HD), F32),
            pltpu.VMEM((groups, tok, HD), F32),
            pltpu.VMEM((tok, HD), F32),
            pltpu.VMEM((tok, HD), F32),
            pltpu.VMEM((tok, HD), F32),
            pltpu.VMEM((tok, HD), F32),
            dma((3,)), dma((2,)), dma((2, groups)), dma,
            dma((3,)), dma((3,)), dma((3, 2)), dma((3, 2)),
            dma((2, groups, 2, 3)), dma((2, groups, 2, 3)),
            dma((groups,)), dma((groups,)), dma((groups,)), dma((groups,)),
            dma((groups, 3)), dma((groups, 3)), dma((groups, 3)), dma((groups, 3)),
            dma((3,)), dma((3,)),
            dma((groups,)), dma((groups,)), dma((groups,)), dma((groups,)),
            dma((2,)), dma((2,)),
        ],
        compiler_params=pltpu.CompilerParams(
            collective_id=1, has_side_effects=True, vmem_limit_bytes=56 * 2**20
        ),
        cost_estimate=pl.CostEstimate(
            flops=20 * rows * wid * local_cols, bytes_accessed=20 * 2**20, transcendentals=0
        ),
    )(lengths, text_lengths, guidance, step_size, mixed, raw, mean, head, latent, text_kv, w_out, w_cross, w_last)


def on_device(
    hidden,
    latent,
    tenant_lengths,
    grid_positions,
    text_kv,
    text_lengths,
    w_query,
    w_key,
    w_value,
    w_out,
    w_cross_query,
    w_cross_out,
    w_head,
    guidance,
    step_size,
):
    halves, groups, parts, columns = (lax.axis_size(a) for a in ("cfg", "z", "t", "wt"))
    half_index, z_index, t_index, wt_index = (
        lax.axis_index(a) for a in ("cfg", "z", "t", "wt")
    )
    tok, width = hidden.shape[1:]
    rows = groups * tok
    local_cols = w_query.shape[1]
    my_cols = local_cols // groups
    heads = my_cols // HD
    paired = halves == 2 and parts == 2
    block = w_query.shape[0]
    if paired and groups == LINE and columns == 2 and tok % 16 == 0 and block % 16 == 0 and my_cols % HD == 0:
        mixed, raw, mean = self_attention_call(
            tenant_lengths, hidden[0], grid_positions, w_key, w_value, w_query
        )
        hidden_out, latent_next = cross_attention_call(
            tenant_lengths, text_lengths, guidance, step_size, mixed, raw, mean, w_head, latent,
            text_kv, w_out, w_cross_query, w_cross_out,
        )
        return (hidden_out[None], latent_next)
    ends = running_ends(tenant_lengths)

    def tenant_of(indices):
        return jnp.sum((indices[:, None] >= ends[None, :]).astype(jnp.int32), axis=1)

    def ordered(mine, other, index):
        return jnp.where(
            index == 0, jnp.concatenate([mine, other]), jnp.concatenate([other, mine])
        )

    def wide(w):
        if not paired:
            return lax.all_gather(w, ("cfg", "t"), axis=0, tiled=True)
        two = ordered(w, flip(w, "t"), t_index)
        return ordered(two, flip(two, "cfg"), half_index)

    def over_groups(x):
        return x if groups == 1 else lax.all_to_all(x, "z", 0, 0, tiled=True)

    def join_groups(x):
        if groups == 1:
            return x
        x = lax.all_gather(x, "z", axis=0)
        return jnp.swapaxes(x, 0, 1).reshape(x.shape[1], local_cols)

    def sum_at_owner(x):
        if groups == 1:
            return x[0].astype(F32)
        return jnp.sum(lax.all_to_all(x, "z", 0, 0).astype(F32), axis=0)

    def sum_groups(x):
        if groups == 1:
            return x
        return lax.psum_scatter(x, "z", scatter_dimension=0, tiled=True)

    def to_groups(x, n):
        return jnp.swapaxes(x.reshape(x.shape[0], groups, n), 0, 1)

    def both_columns(terms):
        terms = terms.astype(BF)
        if columns == 1:
            return terms.astype(F32)
        if columns == 2:
            return terms.astype(F32) + flip(terms, "wt").astype(F32)
        return lax.psum(terms, "wt").astype(F32)

    if paired:
        key_pair = ordered(w_key, flip(w_key, "t"), t_index)
        key_pair, w_query, w_value = lax.optimization_barrier((key_pair, w_query, w_value))
        wide_key = ordered(key_pair, flip(key_pair, "cfg"), half_index)
    else:
        wide_key = wide(w_key)
    wide_query, wide_value = wide(w_query), wide(w_value)
    wide_out, wide_cross, wide_cross_out = wide(w_out), wide(w_cross_query), wide(w_cross_out)

    chunks = CHUNKS if groups > 1 and tok % (CHUNKS * 16) == 0 else 1
    part = tok // chunks
    chunk_rows = rows // chunks

    def by_chunk(x):
        shape = (groups, chunks, part) + x.shape[2:]
        return jnp.swapaxes(x.reshape(shape), 0, 1).reshape((rows,) + x.shape[2:])

    def three_terms(x):
        high = lax.reduce_precision(x, 8, 7)
        middle = lax.reduce_precision(x - high, 8, 7)
        return [term.astype(BF) for term in (high, middle, x - high - middle)]

    own = hidden[0].astype(F32)
    mean = jnp.mean(own, axis=-1, keepdims=True)
    centred = own - mean
    scale = lax.rsqrt(jnp.mean(centred * centred, axis=-1, keepdims=True) + EPS)
    facts = jnp.concatenate([mean, scale, grid_positions.astype(F32)], axis=1)
    slice_width = width // groups
    if groups == 1:
        sliced = own
    else:
        extra = jnp.concatenate(three_terms(facts), axis=1)
        extra = jnp.pad(extra, ((0, 0), (0, 128 - extra.shape[1])))
        features = hidden[0].reshape(tok, halves, groups, slice_width // halves)
        features = jnp.concatenate(
            [features[:, half] for half in range(halves)]
            + [jnp.broadcast_to(extra[:, None], (tok, groups, 128))],
            axis=2,
        )
        arrived = lax.all_to_all(jnp.swapaxes(features, 0, 1), "z", 0, 0)
        arrived = by_chunk(arrived).astype(F32)
        sliced = arrived[:, :slice_width]
        extra = arrived[:, slice_width : slice_width + 15]
        facts = extra[:, 0:5] + extra[:, 5:10] + extra[:, 10:15]
    normed = ((sliced - facts[:, 0:1]) * facts[:, 1:2]).astype(BF)

    def project(w):
        return to_groups(jnp.dot(normed, w, preferred_element_type=F32).astype(BF), my_cols)

    projected_keys = sum_at_owner(project(wide_key)).astype(BF)
    projected = jnp.concatenate([project(wide_query), project(wide_value)], axis=2)
    projected = sum_groups(projected.reshape(groups * rows, 2 * my_cols))

    table, swap = rotary_tables()
    angles = (
        facts[:, 2:3] * table[0][None] + facts[:, 3:4] * table[1][None] + facts[:, 4:5] * table[2][None]
    )
    cosine, sinus = jnp.cos(angles)[:, None, :], jnp.sin(angles)[:, None, :]

    def rotated(x):
        shaped = x.reshape(rows, heads, HD)
        swapped = jnp.einsum("thd,de->the", shaped, jnp.asarray(swap, BF), preferred_element_type=F32)
        shaped = shaped.astype(F32)
        return ((shaped * cosine + swapped * sinus) * head_scale(shaped)).astype(BF)

    keys = rotated(projected_keys).reshape(rows, my_cols)
    queries = rotated(projected[:, :my_cols])
    values = projected[:, my_cols:]

    base = jnp.arange(groups, dtype=jnp.int32)[:, None] * (parts * tok)
    base = by_chunk(base + jnp.arange(tok, dtype=jnp.int32)[None])
    my_tenant = tenant_of(base + t_index * tok)
    if parts == 2:
        keys = jnp.concatenate([keys, flip(keys, "t")], axis=0)
        values = jnp.concatenate([values, flip(values, "t")], axis=0)
        key_tenant = jnp.concatenate([my_tenant, tenant_of(base + (1 - t_index) * tok)])
    else:
        keys = lax.all_gather(keys, "t", axis=0, tiled=True)
        values = lax.all_gather(values, "t", axis=0, tiled=True)
        key_tenant = tenant_of(
            (jnp.arange(parts, dtype=jnp.int32)[:, None] * tok + base[None]).reshape(-1)
        )
    keys = keys.reshape(-1, heads, HD)
    values = values.reshape(-1, heads, HD)

    spans = [slice(i * chunk_rows, (i + 1) * chunk_rows) for i in range(chunks)]
    mixed = [
        attend(queries[i], keys, values, my_tenant[i][:, None] == key_tenant[None, :])
        for i in spans
    ]

    def project_out(mixed, weight):
        return lax.dot_general(
            join_groups(mixed), weight, (((1,), (1,)), ((), ())), preferred_element_type=F32
        )

    column_sums = jnp.dot(jnp.ones((8, slice_width), BF), wide_cross, preferred_element_type=F32)
    column_sums = column_sums[0].reshape(groups, 1, my_cols)
    riding = groups > 1 and chunk_rows <= my_cols

    text = lax.dynamic_slice_in_dim(text_kv[:, 0], z_index * my_cols, my_cols, 2)
    text_keys = text[0].reshape(-1, heads, HD).astype(F32)
    text_keys = (text_keys * head_scale(text_keys)).astype(BF)
    text_values = text[1].reshape(-1, heads, HD)
    text_index = jnp.arange(text_kv.shape[2], dtype=jnp.int32)
    text_tenant = text_index // TEXT
    slots = text_tenant[:, None] == jnp.arange(TENANTS, dtype=jnp.int32)[None, :]
    live_length = jnp.sum(jnp.where(slots, text_lengths[0][None, :], 0), axis=1)
    live = text_index % TEXT < live_length

    states, cross_mixed = [], []
    for i, block_mixed in zip(spans, mixed):
        shifted = (sliced[i] - facts[i, 0:1]) + both_columns(project_out(block_mixed, wide_out))
        states.append(shifted)
        sums = jnp.stack([jnp.sum(shifted, axis=1), jnp.sum(shifted * shifted, axis=1)])
        crossed = jnp.dot(shifted.astype(BF), wide_cross, preferred_element_type=F32).astype(BF)
        crossed = to_groups(crossed, my_cols)
        if riding:
            sums = jnp.concatenate(three_terms(sums))
            sums = jnp.pad(sums, ((0, 0), (0, my_cols - chunk_rows)))
            sums = jnp.broadcast_to(sums[None], (groups,) + sums.shape)
            below = jnp.concatenate([sums] + three_terms(column_sums), axis=1)
            below = jnp.pad(below, ((0, 0), (0, 16 - below.shape[1]), (0, 0)))
            arrived = sum_at_owner(jnp.concatenate([crossed, below], axis=1))
            crossed, below = arrived[:chunk_rows], arrived[chunk_rows:]
            sums = (below[0:2] + below[2:4] + below[4:6])[:, :chunk_rows]
            all_columns = below[6:7] + below[7:8] + below[8:9]
        else:
            sums = sum_at_owner(jnp.broadcast_to(sums[None], (groups,) + sums.shape))
            all_columns = sum_at_owner(column_sums)
            crossed = sum_at_owner(crossed)
        sums = sums / width
        variance = jnp.maximum(sums[1] - sums[0] * sums[0], 0.0)[:, None, None]
        shaped = (crossed - sums[0][:, None] * all_columns).reshape(chunk_rows, heads, HD)
        square = jnp.mean(shaped * shaped, axis=-1, keepdims=True)
        cross_queries = (shaped * lax.rsqrt(square + EPS * (variance + EPS))).astype(BF)
        allowed = (my_tenant[i][:, None] == text_tenant[None, :]) & live[None]
        cross_mixed.append(attend(cross_queries, text_keys, text_values, allowed))

    channels = w_head.shape[1]
    head_rows = lax.dynamic_index_in_dim(
        w_head.reshape(halves, groups, parts * block, channels), z_index, 1, keepdims=False
    ).reshape(-1, channels)
    totals = jnp.sum(w_head.astype(F32), axis=0)[None]
    out_width = width // columns

    leaving, sums = [], []
    for i, shifted, block_mixed in zip(spans, states, cross_mixed):
        shifted = shifted + both_columns(project_out(block_mixed, wide_cross_out))
        final = (shifted + facts[i, 0:1]).astype(BF)
        if groups > 1 and columns == halves:
            span = slice_width // halves
            final = lax.dynamic_slice_in_dim(final, wt_index * span, span, 1)
        leaving.append(final.reshape(groups, part, -1))
        some = jnp.concatenate(
            [
                jnp.dot(shifted.astype(BF), head_rows, preferred_element_type=F32),
                jnp.sum(shifted, axis=1, keepdims=True),
                jnp.sum(shifted * shifted, axis=1, keepdims=True),
            ],
            axis=1,
        )
        sums.append(some.reshape(groups, part, channels + 2))
    sums = sum_at_owner(jnp.concatenate(sums, axis=1))
    mean = sums[:, channels : channels + 1] / width
    variance = jnp.maximum(sums[:, channels + 1 :] / width - mean * mean, 0.0)
    velocity = (sums[:, :channels] - mean * totals) * lax.rsqrt(variance + EPS)

    leaving = jnp.concatenate(leaving, axis=1)
    if groups == 1:
        hidden_out = lax.dynamic_slice_in_dim(leaving[0], wt_index * out_width, out_width, 1)
    else:
        leaving = jnp.swapaxes(lax.all_to_all(leaving, "z", 0, 0), 0, 1)
        if columns == halves:
            hidden_out = leaving.reshape(tok, out_width)
        else:
            leaving = jnp.swapaxes(leaving.reshape(tok, groups, halves, -1), 1, 2)
            hidden_out = lax.dynamic_slice_in_dim(
                leaving.reshape(tok, width), wt_index * out_width, out_width, 1
            )

    channel_half = latent.shape[1]
    outgoing = lax.dynamic_slice_in_dim(velocity, (1 - half_index) * channel_half, channel_half, 1)
    partner = flip(outgoing, "cfg")
    own_part = lax.dynamic_slice_in_dim(velocity, half_index * channel_half, channel_half, 1)
    conditional = jnp.where(half_index == 0, own_part, partner)
    null_text = jnp.where(half_index == 0, partner, own_part)
    latent_next = latent + step_size[0] * (null_text + guidance[0] * (conditional - null_text))
    return (hidden_out[None], latent_next)


def solution(mesh):
    halves, seq, columns = (mesh.shape[a] for a in ("cfg", "seq", "wt"))

    def run(*args):
        heads_here = args[6].shape[1] // columns // HD
        groups = math.gcd(heads_here, seq)
        fine = Mesh(
            mesh.devices.reshape(halves, groups, seq // groups, columns), ("cfg", "z", "t", "wt")
        )
        seq_axes = ("z", "t")
        weight = P(("cfg", "z", "t"), "wt")
        return jax.shard_map(
            on_device,
            mesh=fine,
            in_specs=(
                P("cfg", seq_axes, None),
                P(seq_axes, "cfg"),
                P(),
                P(seq_axes, None),
                P(None, "cfg", None, "wt"),
                P("cfg", None),
                weight,
                weight,
                weight,
                weight,
                weight,
                weight,
                P(),
                P(),
                P(),
            ),
            out_specs=(P("cfg", seq_axes, "wt"), P(seq_axes, "cfg")),
            check_vma=False,
        )(*args)

    return run
```

```python
import math

import jax
import jax.numpy as jnp
import numpy as np
from jax import lax
from jax.experimental import pallas as pl
from jax.experimental.pallas import tpu as pltpu
from jax.sharding import Mesh
from jax.sharding import PartitionSpec as P

HD = 128
TEXT = 512
TENANTS = 4
EPS = 1e-06
CHUNKS = 2
BF = jnp.bfloat16
F32 = jnp.float32


def flip(block, axis):
    return lax.ppermute(block, axis, [(0, 1), (1, 0)])


def rotary_tables():
    sixth = HD // 6
    table = np.zeros((3, HD), np.float32)
    lane = 0
    for column, span in enumerate((HD - 4 * sixth, 2 * sixth, 2 * sixth)):
        exponent = np.arange(0, span, 2).astype(np.float32) / np.float32(span)
        frequency = (1.0 / 10000.0**exponent).astype(np.float32)
        table[column, lane : lane + span] = np.repeat(frequency, 2)
        lane += span
    swap = np.zeros((HD, HD), np.float32)
    for pair in range(0, HD, 2):
        swap[pair + 1, pair] = -1.0
        swap[pair, pair + 1] = 1.0
    return table, swap


def running_ends(lengths):
    upto = np.tril(np.ones((TENANTS, TENANTS), np.int32))
    return jnp.sum(jnp.asarray(upto) * lengths[None, :], axis=1)


def head_scale(shaped):
    return lax.rsqrt(jnp.mean(shaped * shaped, axis=-1, keepdims=True) + EPS)


def attend(queries, keys, values, allowed):
    scores = jnp.einsum("qhd,khd->hqk", queries, keys, preferred_element_type=F32)
    scores = scores * (1.0 / math.sqrt(queries.shape[-1]))
    weights = jnp.where(allowed[None], jnp.exp(scores), 0.0).astype(BF)
    summed = jnp.einsum("hqk,khd->qhd", weights, values, preferred_element_type=F32)
    totals = jnp.sum(weights.astype(F32), axis=2).T
    return (summed / totals[..., None]).astype(BF).reshape(queries.shape[0], -1)


MESH = pl.DeviceIdType.MESH
NEAR = (1, 3, 2)
LINE = 4


def remote(src, dst, sent, got, device):
    return pltpu.make_async_remote_copy(
        src_ref=src, dst_ref=dst, send_sem=sent, recv_sem=got, device_id=device, device_id_type=MESH
    )


def meet(devices):
    barrier = pltpu.get_barrier_semaphore()
    for device in devices:
        pl.semaphore_signal(barrier, inc=1, device_id=device, device_id_type=MESH)
    pl.semaphore_wait(barrier, len(devices))


def span(index, size):
    return pl.ds(pl.multiple_of(index * size, size), size)


def nt_dot(a, b):
    return lax.dot_general(a, b, (((1,), (1,)), ((), ())), preferred_element_type=F32)


def tenants_at(index, lengths):
    found, end = jnp.zeros(index.shape, jnp.int32), 0
    for tenant in range(TENANTS):
        end = end + lengths[tenant]
        found = found + (index >= end).astype(jnp.int32)
    return found


def self_attention_kernel(
    lengths, pos, table, key_index, hid, wk, wv, wq, mixed_out, raw_out, mean_out,
    wide, rows, normed, pairs, queries, pos_all, rot,
    loc_w, loc_h, raw_sem, zs, zr, hs, hr, ps, pr, xs, xr, cs, cr, ys, yr, ks, kr,
):
    c, z, x, y = (lax.axis_index(a) for a in ("cfg", "z", "t", "wt"))
    groups = LINE
    tok = hid.shape[0]
    depth = wk.shape[0]
    wid = rows.shape[2]
    cols = wide.shape[3]
    heads = cols // HD
    at_z = [{"z": lax.rem(z + d, groups)} for d in range(groups)]
    from_z = [lax.rem(z + groups - d, groups) for d in range(groups)]
    at_x, at_c, at_y = {"t": 1 - x}, {"cfg": 1 - c}, {"wt": 1 - y}
    weights = (wk, wv, wq)
    mine = c * groups + z

    own_rows = [
        pltpu.make_async_copy(hid.at[:, kb * wid : (kb + 1) * wid], rows.at[kb, span(z, tok)], loc_h.at[kb])
        for kb in range(2 * groups)
    ]
    own_weights = [
        pltpu.make_async_copy(w.at[:, span(z, cols)], wide.at[j, mine, span(x, depth)], loc_w.at[j])
        for j, w in enumerate(weights)
    ]
    own_pos = pltpu.make_async_copy(pos, pos_all.at[z], loc_w.at[3])
    for copy in own_rows + [own_pos] + own_weights:
        copy.start()
    meet([at_z[1], at_z[2], at_z[3], at_x, at_c, at_y])

    def block(j, d, column):
        return wide.at[j, c * groups + from_z[d], span(column, depth)]

    def x_copy(j, d):
        return remote(block(j, d, x), block(j, d, x), xs.at[d, j], xr.at[d, j], at_x)

    def x_arrival(j, d):
        return remote(block(j, d, 1 - x), block(j, d, 1 - x), xs.at[d, j], xr.at[d, j], at_x)

    def c_copy(j, d, second):
        part = block(j, d, 1 - x if second else x)
        return remote(part, part, cs.at[second, d, j], cr.at[second, d, j], at_c)

    def c_arrival(j, d, second):
        part = wide.at[j, (1 - c) * groups + from_z[d], span(1 - x if second else x, depth)]
        return remote(part, part, cs.at[second, d, j], cr.at[second, d, j], at_c)

    def z_copy(j, d):
        target = lax.rem(z + d, groups)
        return remote(
            weights[j].at[:, span(target, cols)], wide.at[j, mine, span(x, depth)], zs.at[d - 1, j], zr.at[d - 1, j], at_z[d]
        )

    def z_arrival(j, d):
        return remote(block(j, d, x), block(j, d, x), zs.at[d - 1, j], zr.at[d - 1, j], at_z[d])

    def rows_of(b, column, piece):
        return rows.at[column * groups + piece, span(b, tok)]

    def by_z(*choices):
        return jnp.where(z == 0, choices[0], jnp.where(z == 1, choices[1], jnp.where(z == 2, choices[2], choices[3])))

    inner = jnp.logical_and(z > 0, z < groups - 1)
    way_of = [None, by_z(1, 0, 1, 0), by_z(1, 1, 0, 0), by_z(1, 1, 0, 0)]
    step_of = [None, by_z(0, 0, 0, 0), by_z(1, 0, 0, 1), by_z(2, 1, 1, 2)]
    block_of = [z, by_z(1, 0, 3, 2), by_z(2, 2, 1, 1), by_z(3, 3, 0, 0)]

    def h_own(way, p):
        part = rows_of(z, y, p)
        return remote(part, part, hs.at[way, 0, p], hr.at[way, 0, p], {"z": z + 1 - 2 * way})

    def h_arrival(e, p):
        part = rows_of(block_of[e], y, p)
        return remote(part, part, hs.at[way_of[e], step_of[e], p], hr.at[way_of[e], step_of[e], p], at_y)

    def h_onward(e, p):
        part = rows_of(block_of[e], y, p)
        at = step_of[e] + 1
        return remote(part, part, hs.at[way_of[e], at, p], hr.at[way_of[e], at, p], {"z": z + 1 - 2 * way_of[e]})

    def y_copy(e, p):
        part = rows_of(block_of[e], y, p)
        return remote(part, part, ys.at[e - 1, p], yr.at[e - 1, p], at_y)

    def y_arrival(e, p):
        part = rows_of(block_of[e], 1 - y, p)
        return remote(part, part, ys.at[e - 1, p], yr.at[e - 1, p], at_y)

    def up(p):
        @pl.when(z < groups - 1)
        def _():
            h_own(0, p).start()

        @pl.when(z > 0)
        def _():
            h_own(1, p).start()

    def arrive(e):
        for p in range(groups):
            h_arrival(e, p).wait_recv()

            @pl.when(inner)
            def _():
                h_onward(e, p).start()

            y_copy(e, p).start()

    def p_copy(d):
        return remote(pos_all.at[z], pos_all.at[z], ps.at[d - 1], pr.at[d - 1], at_z[d])

    def p_arrival(d):
        part = pos_all.at[from_z[d]]
        return remote(part, part, ps.at[d - 1], pr.at[d - 1], at_z[d])

    some = 16
    width = 2 * groups * wid

    def norm_block(b):
        def norm(i, carry):
            these = pl.ds(pl.multiple_of(b * tok + i * some, some), some)
            total = jnp.zeros((some, wid), F32)
            for kb in range(2 * groups):
                total += rows[kb, these].astype(F32)
            mean = jnp.sum(total, axis=1, keepdims=True) / width
            total = jnp.zeros((some, wid), F32)
            for kb in range(2 * groups):
                centred = rows[kb, these].astype(F32) - mean
                total += centred * centred
            scale = lax.rsqrt(jnp.sum(total, axis=1, keepdims=True) / width + EPS)
            for kb in range(2 * groups):
                normed[kb, these] = ((rows[kb, these].astype(F32) - mean) * scale).astype(BF)
            mean_out[these] = mean
            return carry

        lax.fori_loop(0, tok // some, norm, 0)

    for copy in own_rows + [own_pos]:
        copy.wait()
    for d in NEAR:
        p_copy(d).start()
    for d in NEAR:
        z_copy(0, d).start()
    for j in range(3):
        own_weights[j].wait()
        x_copy(j, 0).start()
        c_copy(j, 0, 0).start()
    norm_block(z)

    def relay(j, d):
        z_arrival(j, d).wait_recv()
        x_copy(j, d).start()
        c_copy(j, d, 0).start()

    def second_relay(j, d):
        x_arrival(j, d).wait_recv()
        c_copy(j, d, 1).start()

    for j in range(3):
        second_relay(j, 0)
    relay(0, 1)
    for d in NEAR:
        z_copy(1, d).start()
    relay(0, 3)
    relay(0, 2)
    for p in range(groups):
        up(p)
    for d in NEAR:
        second_relay(0, d)
    relay(1, 1)
    for d in NEAR:
        z_copy(2, d).start()
    relay(1, 3)
    relay(1, 2)
    for d in NEAR:
        second_relay(1, d)
    arrive(1)

    @pl.when(inner)
    def _():
        arrive(2)

    for d in NEAR:
        relay(2, d)
    for d in NEAR:
        second_relay(2, d)
    for d in NEAR:
        p_arrival(d).wait_recv()
    lane = lax.broadcasted_iota(jnp.int32, (tok, HD), 1)
    even = lax.rem(lane, 2) == 0
    for m in range(groups):
        held = pos_all[m]
        full = jnp.concatenate([held, jnp.zeros((HD - held.shape[0], held.shape[1]), F32)], axis=0)
        column = jnp.transpose(full)[:tok]
        angles = sum(column[:, a : a + 1] * table[a : a + 1, :] for a in range(3))
        rot[0, m * tok : (m + 1) * tok] = jnp.cos(angles)
        sinus = jnp.sin(angles)
        rot[1, m * tok : (m + 1) * tok] = jnp.where(even, -sinus, sinus)

    def rotated(these, total):
        turned = []
        for h in range(heads):
            part = total[:, h * HD : (h + 1) * HD]
            scale = lax.rsqrt(jnp.mean(part * part, axis=1, keepdims=True) + EPS)
            swapped = jnp.where(even, pltpu.roll(part, HD - 1, 1), pltpu.roll(part, 1, 1))
            turned.append((part * rot[0, these] + swapped * rot[1, these]) * scale)
        return jnp.concatenate(turned, axis=1).astype(BF)

    def pair_copy(e):
        part = pairs.at[x, :, span(block_of[e], tok)]
        return remote(part, part, ks.at[e], kr.at[e], at_x)

    def pair_arrival(e):
        part = pairs.at[1 - x, :, span(block_of[e], tok)]
        return remote(part, part, ks.at[e], kr.at[e], at_x)

    def project(e):
        these = span(block_of[e], tok)
        for j in range(3):
            total = jnp.dot(normed[0, these], wide[j, 0], preferred_element_type=F32)
            for kb in range(1, 2 * groups):
                total += jnp.dot(normed[kb, these], wide[j, kb], preferred_element_type=F32)
            if j == 0:
                pairs[x, 0, these] = rotated(these, total)
            elif j == 1:
                pairs[x, 1, these] = total.astype(BF)
                pair_copy(e).start()
            else:
                queries[these] = rotated(these, total)

    def finish(e):
        for p in range(groups):
            y_arrival(e, p).wait_recv()
        norm_block(block_of[e])
        project(e)

    for j in range(3):
        for d in range(groups):
            c_arrival(j, d, 0).wait_recv()
            c_arrival(j, d, 1).wait_recv()
    project(0)

    @pl.when(inner)
    def _():
        arrive(3)

    @pl.when(jnp.logical_not(inner))
    def _():
        arrive(2)

    finish(1)

    @pl.when(jnp.logical_not(inner))
    def _():
        arrive(3)

    raws = [
        pltpu.make_async_copy(rows.at[half * groups + z], raw_out.at[half], raw_sem.at[half]) for half in (0, 1)
    ]
    finish(2)
    finish(3)
    for copy in raws:
        copy.start()
    for e in range(groups):
        pair_arrival(e).wait_recv()

    key_tenant = tenants_at(key_index[0:1], lengths)
    ones = jnp.ones((groups * tok, HD), BF)

    def attend_block(m, carry):
        these = span(m, tok)
        index = lax.broadcasted_iota(jnp.int32, (tok, 1), 0) + (m * 2 + x) * tok
        allowed = tenants_at(index, lengths) == key_tenant
        for h in range(heads):
            lanes = slice(h * HD, (h + 1) * HD)
            summed = jnp.zeros((tok, 2 * HD), F32)
            for part in (0, 1):
                scores = nt_dot(queries[these, lanes], pairs[part, 0, :, lanes]) * (1.0 / math.sqrt(HD))
                here = allowed[:, part * groups * tok : (part + 1) * groups * tok]
                chances = jnp.where(here, jnp.exp(scores), 0.0).astype(BF)
                both = jnp.concatenate([pairs[part, 1, :, lanes], ones], axis=1)
                summed += jnp.dot(chances, both, preferred_element_type=F32)
            mixed_out[these, lanes] = (summed[:, :HD] / summed[:, HD:]).astype(BF)
        return carry

    lax.fori_loop(0, groups, attend_block, 0)

    for copy in raws:
        copy.wait()
    for p in range(groups):
        @pl.when(z < groups - 1)
        def _():
            h_own(0, p).wait_send()

        @pl.when(z > 0)
        def _():
            h_own(1, p).wait_send()

        for e in (1, 2, 3):
            @pl.when(inner)
            def _():
                h_onward(e, p).wait_send()

            y_copy(e, p).wait_send()
    for d in NEAR:
        p_copy(d).wait_send()
        for j in range(3):
            z_copy(j, d).wait_send()
    for d in range(groups):
        for j in range(3):
            x_copy(j, d).wait_send()
            c_copy(j, d, 0).wait_send()
            c_copy(j, d, 1).wait_send()
    for e in range(groups):
        pair_copy(e).wait_send()


def self_attention_call(lengths, hidden, positions, wk, wv, wq):
    tok, width = hidden.shape
    groups = LINE
    depth, local_cols = wk.shape
    cols = local_cols // groups
    rows = groups * tok
    wid = width // (2 * groups)
    anywhere = pl.BlockSpec(memory_space=pl.ANY)
    vmem = pl.BlockSpec(memory_space=pltpu.VMEM)
    smem = pl.BlockSpec(memory_space=pltpu.SMEM)
    dma = pltpu.SemaphoreType.DMA
    made = [
        jax.ShapeDtypeStruct((rows, cols), BF),
        jax.ShapeDtypeStruct((2, rows, wid), BF),
        jax.ShapeDtypeStruct((rows, 1), F32),
    ]
    table = np.zeros((8, HD), np.float32)
    table[:3] = rotary_tables()[0]
    place = np.arange(2 * rows)
    place = (place % rows // tok * 2 + place // rows) * tok + place % tok
    place = np.broadcast_to(place.astype(np.int32), (8, 2 * rows))
    pos = jnp.pad(positions.T.astype(F32), ((0, 5), (0, -tok % 128)))
    return pl.pallas_call(
        self_attention_kernel,
        out_shape=made,
        in_specs=[smem, vmem, vmem, vmem] + [anywhere] * 4,
        out_specs=[vmem] * 3,
        scratch_shapes=[
            pltpu.VMEM((3, 2 * groups, 2 * depth, cols), BF),
            pltpu.VMEM((2 * groups, rows, wid), BF),
            pltpu.VMEM((2 * groups, rows, wid), BF),
            pltpu.VMEM((2, 2, rows, cols), BF),
            pltpu.VMEM((rows, cols), BF),
            pltpu.VMEM((groups,) + pos.shape, F32),
            pltpu.VMEM((2, rows, HD), F32),
            dma((4,)), dma((2 * groups,)), dma((2,)),
            dma((3, 3)), dma((3, 3)),
            dma((2, 3, 4)), dma((2, 3, 4)),
            dma((3,)), dma((3,)),
            dma((4, 3)), dma((4, 3)),
            dma((2, 4, 3)), dma((2, 4, 3)),
            dma((3, 4)), dma((3, 4)),
            dma((4,)), dma((4,)),
        ],
        compiler_params=pltpu.CompilerParams(
            collective_id=0, has_side_effects=True, vmem_limit_bytes=56 * 2**20
        ),
        cost_estimate=pl.CostEstimate(
            flops=6 * rows * width * cols, bytes_accessed=20 * 2**20, transcendentals=0
        ),
    )(lengths, pos, jnp.asarray(table), jnp.asarray(place), hidden, wk, wv, wq)


def line_places(z):
    def block(way, s):
        return z - s if way == 0 else z + s

    def sends(way, s):
        if way == 0:
            return jnp.logical_and(z - s >= 0, z + 1 < LINE)
        return jnp.logical_and(z + s < LINE, z >= 1)

    def gets(way, s):
        return z - 1 - s >= 0 if way == 0 else z + 1 + s < LINE

    return block, sends, gets


def pack_columns(first, second):
    tok = first.shape[0]
    lane = lax.broadcasted_iota(jnp.int32, (tok, HD), 1)
    both = jnp.where(lane == 0, first, jnp.where(lane == 1, second, 0.0))
    both = jnp.concatenate([both, jnp.zeros((-tok % HD, HD), F32)], axis=0)
    return jnp.transpose(both)[:8]


def unpack_columns(packed, tok):
    full = jnp.concatenate([packed, jnp.zeros((HD - packed.shape[0], packed.shape[1]), F32)], axis=0)
    column = jnp.transpose(full)[:tok]
    return column[:, 0:1], column[:, 1:2]


def cross_attention_kernel(
    lengths, text_lengths, guidance, step_size, mixed, raw, mean, head, latent, text_kv, w_out, w_cross, w_last,
    hidden_out, latent_out,
    wide, text, gath, own, left, right, left2, right2, kept, state, asked, answers, facts, facts_in, cols_out, cols_in,
    leaving, vel, vel_in, half_out, half_in, core_out, core_in,
    loc_w, loc_t, loc_g, loc_f, ws, wr, wcs, wcr, gs, gr, ys, yr, y2s, y2r, qs, qr, fs, fr, ss, sr, os_, or_, vs, vr, es, er,
):
    c, z, x, y = (lax.axis_index(a) for a in ("cfg", "z", "t", "wt"))
    groups = LINE
    rows, cols = mixed.shape
    tok = rows // groups
    depth = w_out.shape[0]
    wid = raw.shape[2]
    width = 2 * groups * wid
    heads = cols // HD
    channels = head.shape[1]
    slots = text.shape[1] // TENANTS
    at_z = [{"z": lax.rem(z + d, groups)} for d in range(groups)]
    from_z = [lax.rem(z + groups - d, groups) for d in range(groups)]
    at_x, at_c, at_y = {"t": 1 - x}, {"cfg": 1 - c}, {"wt": 1 - y}
    at_line = ({"z": jnp.minimum(z + 1, groups - 1)}, {"z": jnp.maximum(z - 1, 0)})
    line_block, line_sends, line_gets = line_places(z)
    weights = (w_out, w_cross, w_last)

    own_weights = [
        pltpu.make_async_copy(w, wide.at[j, c, span(x, depth)], loc_w.at[j]) for j, w in enumerate(weights)
    ]
    own_text = [pltpu.make_async_copy(text_kv.at[k, 0, :, span(z, cols)], text.at[k], loc_t.at[k]) for k in (0, 1)]
    for copy in own_weights + own_text:
        copy.start()
    own[0] = mixed[...].reshape(groups, tok, cols)
    meet([at_z[1], at_z[2], at_z[3], at_x, at_c, at_y])

    def g_local(f, i):
        return pltpu.make_async_copy(own.at[f, i], gath.at[f, i, :, span(z, cols)], loc_g.at[f, i])

    def g_copy(f, i, way, s):
        part = gath.at[f, i, :, span(line_block(way, s), cols)]
        return remote(own.at[f, i] if s == 0 else part, part, gs.at[f, i, way, s], gr.at[f, i, way, s], at_line[way])

    def g_arrival(f, i, way, s):
        part = gath.at[f, i, :, span(line_block(way, s + 1), cols)]
        return remote(part, part, gs.at[f, i, way, s], gr.at[f, i, way, s], at_line[way])

    def g_start(f, i):
        for way in (0, 1):
            @pl.when(line_sends(way, 0))
            def _():
                g_copy(f, i, way, 0).start()
        g_local(f, i).start()

    def g_step(f, i, s):
        for way in (0, 1):
            @pl.when(line_gets(way, s))
            def _():
                g_arrival(f, i, way, s).wait_recv()
                if s + 1 < groups - 1:
                    @pl.when(line_sends(way, s + 1))
                    def _():
                        g_copy(f, i, way, s + 1).start()
        if s == groups - 2:
            g_local(f, i).wait()

    def w_part(j, core, column):
        return wide.at[j, core, span(column, depth)]

    def w_copy(j):
        return remote(w_part(j, c, x), w_part(j, c, x), ws.at[j], wr.at[j], at_x)

    def w_arrival(j):
        return remote(w_part(j, c, 1 - x), w_part(j, c, 1 - x), ws.at[j], wr.at[j], at_x)

    def wc_copy(j, second):
        part = w_part(j, c, 1 - x if second else x)
        return remote(part, part, wcs.at[j, second], wcr.at[j, second], at_c)

    def wc_arrival(j, second):
        part = w_part(j, 1 - c, 1 - x if second else x)
        return remote(part, part, wcs.at[j, second], wcr.at[j, second], at_c)

    def w_relay(j):
        w_arrival(j).wait_recv()
        wc_copy(j, 1).start()

    def w_ready(j):
        wc_arrival(j, 0).wait_recv()
        wc_arrival(j, 1).wait_recv()

    for i in range(groups):
        g_start(0, i)
    for j in range(3):
        own_weights[j].wait()
        w_copy(j).start()
        wc_copy(j, 0).start()

    for copy in own_text:
        copy.wait()

    def norm_text(i, carry):
        these = span(i, HD)
        for h in range(heads):
            lanes = slice(h * HD, (h + 1) * HD)
            part = text[0, these, lanes].astype(F32)
            scale = lax.rsqrt(jnp.mean(part * part, axis=1, keepdims=True) + EPS)
            text[0, these, lanes] = (part * scale).astype(BF)
        return carry

    lax.fori_loop(0, text.shape[1] // HD, norm_text, 0)
    totals = jnp.sum(head[...].astype(F32), axis=0, keepdims=True)

    def y_copy(i):
        return remote(left.at[i], right.at[i], ys.at[i], yr.at[i], at_y)

    def y2_copy(i):
        return remote(left2.at[i], right2.at[i], y2s.at[i], y2r.at[i], at_y)

    def q_copy(i, d):
        return remote(asked.at[i, lax.rem(z + d, groups)], answers.at[i, z], qs.at[i, d - 1], qr.at[i, d - 1], at_z[d])

    def q_arrival(i, d):
        part = answers.at[i, from_z[d]]
        return remote(part, part, qs.at[i, d - 1], qr.at[i, d - 1], at_z[d])

    def f_copy(i, d):
        return remote(facts.at[i], facts_in.at[i, z], fs.at[i, d - 1], fr.at[i, d - 1], at_z[d])

    def f_arrival(i, d):
        part = facts_in.at[i, from_z[d]]
        return remote(part, part, fs.at[i, d - 1], fr.at[i, d - 1], at_z[d])

    def s_copy(d):
        return remote(cols_out.at[lax.rem(z + d, groups)], cols_in.at[z], ss.at[d - 1], sr.at[d - 1], at_z[d])

    def s_arrival(d):
        part = cols_in.at[from_z[d]]
        return remote(part, part, ss.at[d - 1], sr.at[d - 1], at_z[d])

    def project_out(i):
        for half in (0, 1):
            left[i, :, half * wid : (half + 1) * wid] = nt_dot(gath[0, i], wide[0, half]).astype(BF)
        y_copy(i).start()

    def sum_columns():
        ones = jnp.ones((16, wid), BF)
        for g in range(groups):
            lanes = slice(g * cols, (g + 1) * cols)
            total = jnp.dot(ones, wide[1, 0, :, lanes], preferred_element_type=F32)
            total += jnp.dot(ones, wide[1, 1, :, lanes], preferred_element_type=F32)
            cols_out[g] = total[:8]
        for d in NEAR:
            s_copy(d).start()

    def update(i):
        y_copy(i).wait_recv()
        these = slice(i * tok, (i + 1) * tok)
        shift = mean[these]
        first = second = jnp.zeros((tok, 1), F32)
        for half in (0, 1):
            lanes = slice(half * wid, (half + 1) * wid)
            both = left[i, :, lanes].astype(F32) + right[i, :, lanes].astype(F32)
            new = (raw[half, these].astype(F32) - shift) + both
            state[i, half] = new
            first += jnp.sum(new, axis=1, keepdims=True)
            second += jnp.sum(new * new, axis=1, keepdims=True)
        facts[i] = pack_columns(first, second)
        for d in NEAR:
            f_copy(i, d).start()
        for g in range(groups):
            lanes = slice(g * cols, (g + 1) * cols)
            part = jnp.dot(state[i, 0].astype(BF), wide[1, 0, :, lanes], preferred_element_type=F32)
            part += jnp.dot(state[i, 1].astype(BF), wide[1, 1, :, lanes], preferred_element_type=F32)
            asked[i, g] = part.astype(BF)
        for d in NEAR:
            q_copy(i, d).start()

    def cross(i):
        packed = facts[i]
        crossed = asked[i, z].astype(F32)
        column_sums = cols_out[z, 0:1]
        for d in NEAR:
            q_arrival(i, d).wait_recv()
            f_arrival(i, d).wait_recv()
            if i == 0:
                s_arrival(d).wait_recv()
            packed = packed + facts_in[i, from_z[d]]
            crossed = crossed + answers[i, from_z[d]].astype(F32)
            column_sums = column_sums + cols_in[from_z[d], 0:1]
        first, second = unpack_columns(packed, tok)
        average = first / width
        variance = jnp.maximum(second / width - average * average, 0.0)
        crossed = crossed - average * column_sums
        index = lax.broadcasted_iota(jnp.int32, (tok, 1), 0) + (i * 2 + x) * tok
        tenant = tenants_at(index, lengths)
        slot = lax.broadcasted_iota(jnp.int32, (1, slots), 1)
        ones = jnp.ones((slots, HD), BF)
        for h in range(heads):
            lanes = slice(h * HD, (h + 1) * HD)
            part = crossed[:, lanes]
            square = jnp.mean(part * part, axis=1, keepdims=True)
            query = (part * lax.rsqrt(square + EPS * (variance + EPS))).astype(BF)
            summed = jnp.zeros((tok, 2 * HD), F32)
            for t in range(TENANTS):
                these = slice(t * slots, (t + 1) * slots)
                scores = nt_dot(query, text[0, these, lanes]) * (1.0 / math.sqrt(HD))
                allowed = jnp.logical_and(tenant == t, slot < text_lengths[0, t])
                chances = jnp.where(allowed, jnp.exp(scores), 0.0).astype(BF)
                both = jnp.concatenate([text[1, these, lanes], ones], axis=1)
                summed += jnp.dot(chances, both, preferred_element_type=F32)
            own[1, i, :, lanes] = (summed[:, :HD] / summed[:, HD:]).astype(BF)
        g_start(1, i)

    def project_last(i):
        left2[i] = nt_dot(gath[1, i], wide[2, 1 - y]).astype(BF)
        y2_copy(i).start()
        kept[i] = nt_dot(gath[1, i], wide[2, y]).astype(BF)

    def o_remote(i):
        return remote(leaving.at[i], hidden_out.at[:, span(z, wid)], os_.at[i], or_.at[z], {"z": i})

    def o_local(i):
        return pltpu.make_async_copy(leaving.at[i], hidden_out.at[:, span(z, wid)], loc_f)

    def v_remote(i):
        return remote(vel.at[i], vel_in.at[z], vs.at[i], vr.at[z], {"z": i})

    def finish(i):
        y2_copy(i).wait_recv()
        these = slice(i * tok, (i + 1) * tok)
        final = state[i, y] + kept[i].astype(F32) + right2[i].astype(F32)
        leaving[i] = (final + mean[these]).astype(BF)

        @pl.when(z != i)
        def _():
            o_remote(i).start()

        @pl.when(z == i)
        def _():
            o_local(i).start()

        rows_here = pl.ds(pl.multiple_of((y * groups + z) * wid, wid), wid)
        some = jnp.dot(final.astype(BF), head[rows_here], preferred_element_type=F32)
        first = jnp.sum(final, axis=1, keepdims=True)
        second = jnp.sum(final * final, axis=1, keepdims=True)
        lane = lax.broadcasted_iota(jnp.int32, (tok, HD - channels), 1)
        tail = jnp.where(lane == 0, first, jnp.where(lane == 1, second, 0.0))
        vel[i] = jnp.concatenate([some, tail], axis=1)

        @pl.when(z != i)
        def _():
            v_remote(i).start()

    w_relay(0)
    g_step(0, 0, 0)
    g_step(0, 1, 0)
    g_step(0, 0, 1)
    g_step(0, 2, 0)
    g_step(0, 1, 1)
    g_step(0, 0, 2)
    w_ready(0)
    project_out(0)
    g_step(0, 3, 0)
    g_step(0, 2, 1)
    g_step(0, 1, 2)
    project_out(1)
    w_relay(1)
    g_step(0, 3, 1)
    g_step(0, 2, 2)
    project_out(2)
    w_ready(1)
    sum_columns()
    update(0)
    g_step(0, 3, 2)
    project_out(3)
    update(1)
    cross(0)
    update(2)
    w_relay(2)
    g_step(1, 0, 0)
    cross(1)
    update(3)
    g_step(1, 1, 0)
    g_step(1, 0, 1)
    cross(2)
    g_step(1, 2, 0)
    g_step(1, 1, 1)
    g_step(1, 0, 2)
    w_ready(2)
    project_last(0)
    cross(3)
    g_step(1, 3, 0)
    g_step(1, 2, 1)
    g_step(1, 1, 2)
    project_last(1)
    finish(0)
    g_step(1, 3, 1)
    g_step(1, 2, 2)
    project_last(2)
    finish(1)
    g_step(1, 3, 2)
    project_last(3)
    finish(2)
    finish(3)

    total = vel[z]
    for d in NEAR:
        part = vel_in.at[from_z[d]]
        remote(part, part, vs.at[d], vr.at[from_z[d]], at_z[d]).wait_recv()
        total = total + vel_in[from_z[d]]
    half_out[...] = total
    over_y = remote(half_out, half_in, es.at[0], er.at[0], at_y)
    over_y.start()
    over_y.wait()
    total = half_out[...] + half_in[...]
    average = total[:, channels : channels + 1] / width
    variance = jnp.maximum(total[:, channels + 1 : channels + 2] / width - average * average, 0.0)
    velocity = (total[:, :channels] - average * totals) * lax.rsqrt(variance + EPS)
    core_out[...] = jnp.concatenate([velocity, velocity], axis=1)
    over_c = remote(core_out, core_in, es.at[1], er.at[1], at_c)
    over_c.start()
    over_c.wait()
    span_out = latent.shape[1]
    mine, other = core_out[...], core_in[...]
    here = [jnp.where(c == 0, both[:, :span_out], both[:, span_out : 2 * span_out]) for both in (mine, other)]
    conditional = jnp.where(c == 0, here[0], here[1])
    null_text = jnp.where(c == 0, here[1], here[0])
    latent_out[...] = latent[...] + step_size[0] * (null_text + guidance[0] * (conditional - null_text))

    for d in NEAR:
        part = hidden_out.at[:, span(from_z[d], wid)]
        remote(part, part, os_.at[d], or_.at[from_z[d]], at_z[d]).wait_recv()
    for i in range(groups):
        @pl.when(z != i)
        def _():
            o_remote(i).wait_send()
            v_remote(i).wait_send()

        @pl.when(z == i)
        def _():
            o_local(i).wait()

        y_copy(i).wait_send()
        y2_copy(i).wait_send()
        for d in NEAR:
            q_copy(i, d).wait_send()
            f_copy(i, d).wait_send()
        for f in (0, 1):
            for way in (0, 1):
                for s in range(groups - 1):
                    @pl.when(line_sends(way, s))
                    def _():
                        g_copy(f, i, way, s).wait_send()
    for d in NEAR:
        s_copy(d).wait_send()
    for j in range(3):
        w_copy(j).wait_send()
        wc_copy(j, 0).wait_send()
        wc_copy(j, 1).wait_send()


def cross_attention_call(
    lengths, text_lengths, guidance, step_size, mixed, raw, mean, head, latent, text_kv, w_out, w_cross, w_last
):
    groups = LINE
    rows, cols = mixed.shape
    tok = rows // groups
    wid = raw.shape[2]
    depth, local_cols = w_out.shape
    padded = tok + -tok % HD
    anywhere = pl.BlockSpec(memory_space=pl.ANY)
    vmem = pl.BlockSpec(memory_space=pltpu.VMEM)
    smem = pl.BlockSpec(memory_space=pltpu.SMEM)
    dma = pltpu.SemaphoreType.DMA
    return pl.pallas_call(
        cross_attention_kernel,
        out_shape=[
            jax.ShapeDtypeStruct((tok, groups * wid), BF),
            jax.ShapeDtypeStruct(latent.shape, F32),
        ],
        in_specs=[smem] * 4 + [vmem] * 5 + [anywhere] * 4,
        out_specs=[anywhere, vmem],
        scratch_shapes=[
            pltpu.VMEM((3, 2, 2 * depth, local_cols), BF),
            pltpu.VMEM((2, text_kv.shape[2], cols), BF),
            pltpu.VMEM((2, groups, tok, local_cols), BF),
            pltpu.VMEM((2, groups, tok, cols), BF),
            pltpu.VMEM((groups, tok, 2 * wid), BF),
            pltpu.VMEM((groups, tok, 2 * wid), BF),
            pltpu.VMEM((groups, tok, wid), BF),
            pltpu.VMEM((groups, tok, wid), BF),
            pltpu.VMEM((groups, tok, wid), BF),
            pltpu.VMEM((groups, 2, tok, wid), F32),
            pltpu.VMEM((groups, groups, tok, cols), BF),
            pltpu.VMEM((groups, groups, tok, cols), BF),
            pltpu.VMEM((groups, 8, padded), F32),
            pltpu.VMEM((groups, groups, 8, padded), F32),
            pltpu.VMEM((groups, 8, cols), F32),
            pltpu.VMEM((groups, 8, cols), F32),
            pltpu.VMEM((groups, tok, wid), BF),
            pltpu.VMEM((groups, tok, HD), F32),
            pltpu.VMEM((groups, tok, HD), F32),
            pltpu.VMEM((tok, HD), F32),
            pltpu.VMEM((tok, HD), F32),
            pltpu.VMEM((tok, HD), F32),
            pltpu.VMEM((tok, HD), F32),
            dma((3,)), dma((2,)), dma((2, groups)), dma,
            dma((3,)), dma((3,)), dma((3, 2)), dma((3, 2)),
            dma((2, groups, 2, 3)), dma((2, groups, 2, 3)),
            dma((groups,)), dma((groups,)), dma((groups,)), dma((groups,)),
            dma((groups, 3)), dma((groups, 3)), dma((groups, 3)), dma((groups, 3)),
            dma((3,)), dma((3,)),
            dma((groups,)), dma((groups,)), dma((groups,)), dma((groups,)),
            dma((2,)), dma((2,)),
        ],
        compiler_params=pltpu.CompilerParams(
            collective_id=1, has_side_effects=True, vmem_limit_bytes=56 * 2**20
        ),
        cost_estimate=pl.CostEstimate(
            flops=20 * rows * wid * local_cols, bytes_accessed=20 * 2**20, transcendentals=0
        ),
    )(lengths, text_lengths, guidance, step_size, mixed, raw, mean, head, latent, text_kv, w_out, w_cross, w_last)


def on_device(
    hidden,
    latent,
    tenant_lengths,
    grid_positions,
    text_kv,
    text_lengths,
    w_query,
    w_key,
    w_value,
    w_out,
    w_cross_query,
    w_cross_out,
    w_head,
    guidance,
    step_size,
):
    halves, groups, parts, columns = (lax.axis_size(a) for a in ("cfg", "z", "t", "wt"))
    half_index, z_index, t_index, wt_index = (
        lax.axis_index(a) for a in ("cfg", "z", "t", "wt")
    )
    tok, width = hidden.shape[1:]
    rows = groups * tok
    local_cols = w_query.shape[1]
    my_cols = local_cols // groups
    heads = my_cols // HD
    paired = halves == 2 and parts == 2
    block = w_query.shape[0]
    if paired and groups == LINE and columns == 2 and tok % 16 == 0 and block % 16 == 0 and my_cols % HD == 0:
        mixed, raw, mean = self_attention_call(
            tenant_lengths, hidden[0], grid_positions, w_key, w_value, w_query
        )
        hidden_out, latent_next = cross_attention_call(
            tenant_lengths, text_lengths, guidance, step_size, mixed, raw, mean, w_head, latent,
            text_kv, w_out, w_cross_query, w_cross_out,
        )
        return (hidden_out[None], latent_next)
    ends = running_ends(tenant_lengths)

    def tenant_of(indices):
        return jnp.sum((indices[:, None] >= ends[None, :]).astype(jnp.int32), axis=1)

    def ordered(mine, other, index):
        return jnp.where(
            index == 0, jnp.concatenate([mine, other]), jnp.concatenate([other, mine])
        )

    def wide(w):
        if not paired:
            return lax.all_gather(w, ("cfg", "t"), axis=0, tiled=True)
        two = ordered(w, flip(w, "t"), t_index)
        return ordered(two, flip(two, "cfg"), half_index)

    def over_groups(x):
        return x if groups == 1 else lax.all_to_all(x, "z", 0, 0, tiled=True)

    def join_groups(x):
        if groups == 1:
            return x
        x = lax.all_gather(x, "z", axis=0)
        return jnp.swapaxes(x, 0, 1).reshape(x.shape[1], local_cols)

    def sum_at_owner(x):
        if groups == 1:
            return x[0].astype(F32)
        return jnp.sum(lax.all_to_all(x, "z", 0, 0).astype(F32), axis=0)

    def sum_groups(x):
        if groups == 1:
            return x
        return lax.psum_scatter(x, "z", scatter_dimension=0, tiled=True)

    def to_groups(x, n):
        return jnp.swapaxes(x.reshape(x.shape[0], groups, n), 0, 1)

    def both_columns(terms):
        terms = terms.astype(BF)
        if columns == 1:
            return terms.astype(F32)
        if columns == 2:
            return terms.astype(F32) + flip(terms, "wt").astype(F32)
        return lax.psum(terms, "wt").astype(F32)

    if paired:
        key_pair = ordered(w_key, flip(w_key, "t"), t_index)
        key_pair, w_query, w_value = lax.optimization_barrier((key_pair, w_query, w_value))
        wide_key = ordered(key_pair, flip(key_pair, "cfg"), half_index)
    else:
        wide_key = wide(w_key)
    wide_query, wide_value = wide(w_query), wide(w_value)
    wide_out, wide_cross, wide_cross_out = wide(w_out), wide(w_cross_query), wide(w_cross_out)

    chunks = CHUNKS if groups > 1 and tok % (CHUNKS * 16) == 0 else 1
    part = tok // chunks
    chunk_rows = rows // chunks

    def by_chunk(x):
        shape = (groups, chunks, part) + x.shape[2:]
        return jnp.swapaxes(x.reshape(shape), 0, 1).reshape((rows,) + x.shape[2:])

    def three_terms(x):
        high = lax.reduce_precision(x, 8, 7)
        middle = lax.reduce_precision(x - high, 8, 7)
        return [term.astype(BF) for term in (high, middle, x - high - middle)]

    own = hidden[0].astype(F32)
    mean = jnp.mean(own, axis=-1, keepdims=True)
    centred = own - mean
    scale = lax.rsqrt(jnp.mean(centred * centred, axis=-1, keepdims=True) + EPS)
    facts = jnp.concatenate([mean, scale, grid_positions.astype(F32)], axis=1)
    slice_width = width // groups
    if groups == 1:
        sliced = own
    else:
        extra = jnp.concatenate(three_terms(facts), axis=1)
        extra = jnp.pad(extra, ((0, 0), (0, 128 - extra.shape[1])))
        features = hidden[0].reshape(tok, halves, groups, slice_width // halves)
        features = jnp.concatenate(
            [features[:, half] for half in range(halves)]
            + [jnp.broadcast_to(extra[:, None], (tok, groups, 128))],
            axis=2,
        )
        arrived = lax.all_to_all(jnp.swapaxes(features, 0, 1), "z", 0, 0)
        arrived = by_chunk(arrived).astype(F32)
        sliced = arrived[:, :slice_width]
        extra = arrived[:, slice_width : slice_width + 15]
        facts = extra[:, 0:5] + extra[:, 5:10] + extra[:, 10:15]
    normed = ((sliced - facts[:, 0:1]) * facts[:, 1:2]).astype(BF)

    def project(w):
        return to_groups(jnp.dot(normed, w, preferred_element_type=F32).astype(BF), my_cols)

    projected_keys = sum_at_owner(project(wide_key)).astype(BF)
    projected = jnp.concatenate([project(wide_query), project(wide_value)], axis=2)
    projected = sum_groups(projected.reshape(groups * rows, 2 * my_cols))

    table, swap = rotary_tables()
    angles = (
        facts[:, 2:3] * table[0][None] + facts[:, 3:4] * table[1][None] + facts[:, 4:5] * table[2][None]
    )
    cosine, sinus = jnp.cos(angles)[:, None, :], jnp.sin(angles)[:, None, :]

    def rotated(x):
        shaped = x.reshape(rows, heads, HD)
        swapped = jnp.einsum("thd,de->the", shaped, jnp.asarray(swap, BF), preferred_element_type=F32)
        shaped = shaped.astype(F32)
        return ((shaped * cosine + swapped * sinus) * head_scale(shaped)).astype(BF)

    keys = rotated(projected_keys).reshape(rows, my_cols)
    queries = rotated(projected[:, :my_cols])
    values = projected[:, my_cols:]

    base = jnp.arange(groups, dtype=jnp.int32)[:, None] * (parts * tok)
    base = by_chunk(base + jnp.arange(tok, dtype=jnp.int32)[None])
    my_tenant = tenant_of(base + t_index * tok)
    if parts == 2:
        keys = jnp.concatenate([keys, flip(keys, "t")], axis=0)
        values = jnp.concatenate([values, flip(values, "t")], axis=0)
        key_tenant = jnp.concatenate([my_tenant, tenant_of(base + (1 - t_index) * tok)])
    else:
        keys = lax.all_gather(keys, "t", axis=0, tiled=True)
        values = lax.all_gather(values, "t", axis=0, tiled=True)
        key_tenant = tenant_of(
            (jnp.arange(parts, dtype=jnp.int32)[:, None] * tok + base[None]).reshape(-1)
        )
    keys = keys.reshape(-1, heads, HD)
    values = values.reshape(-1, heads, HD)

    spans = [slice(i * chunk_rows, (i + 1) * chunk_rows) for i in range(chunks)]
    mixed = [
        attend(queries[i], keys, values, my_tenant[i][:, None] == key_tenant[None, :])
        for i in spans
    ]

    def project_out(mixed, weight):
        return lax.dot_general(
            join_groups(mixed), weight, (((1,), (1,)), ((), ())), preferred_element_type=F32
        )

    column_sums = jnp.dot(jnp.ones((8, slice_width), BF), wide_cross, preferred_element_type=F32)
    column_sums = column_sums[0].reshape(groups, 1, my_cols)
    riding = groups > 1 and chunk_rows <= my_cols

    text = lax.dynamic_slice_in_dim(text_kv[:, 0], z_index * my_cols, my_cols, 2)
    text_keys = text[0].reshape(-1, heads, HD).astype(F32)
    text_keys = (text_keys * head_scale(text_keys)).astype(BF)
    text_values = text[1].reshape(-1, heads, HD)
    text_index = jnp.arange(text_kv.shape[2], dtype=jnp.int32)
    text_tenant = text_index // TEXT
    slots = text_tenant[:, None] == jnp.arange(TENANTS, dtype=jnp.int32)[None, :]
    live_length = jnp.sum(jnp.where(slots, text_lengths[0][None, :], 0), axis=1)
    live = text_index % TEXT < live_length

    states, cross_mixed = [], []
    for i, block_mixed in zip(spans, mixed):
        shifted = (sliced[i] - facts[i, 0:1]) + both_columns(project_out(block_mixed, wide_out))
        states.append(shifted)
        sums = jnp.stack([jnp.sum(shifted, axis=1), jnp.sum(shifted * shifted, axis=1)])
        crossed = jnp.dot(shifted.astype(BF), wide_cross, preferred_element_type=F32).astype(BF)
        crossed = to_groups(crossed, my_cols)
        if riding:
            sums = jnp.concatenate(three_terms(sums))
            sums = jnp.pad(sums, ((0, 0), (0, my_cols - chunk_rows)))
            sums = jnp.broadcast_to(sums[None], (groups,) + sums.shape)
            below = jnp.concatenate([sums] + three_terms(column_sums), axis=1)
            below = jnp.pad(below, ((0, 0), (0, 16 - below.shape[1]), (0, 0)))
            arrived = sum_at_owner(jnp.concatenate([crossed, below], axis=1))
            crossed, below = arrived[:chunk_rows], arrived[chunk_rows:]
            sums = (below[0:2] + below[2:4] + below[4:6])[:, :chunk_rows]
            all_columns = below[6:7] + below[7:8] + below[8:9]
        else:
            sums = sum_at_owner(jnp.broadcast_to(sums[None], (groups,) + sums.shape))
            all_columns = sum_at_owner(column_sums)
            crossed = sum_at_owner(crossed)
        sums = sums / width
        variance = jnp.maximum(sums[1] - sums[0] * sums[0], 0.0)[:, None, None]
        shaped = (crossed - sums[0][:, None] * all_columns).reshape(chunk_rows, heads, HD)
        square = jnp.mean(shaped * shaped, axis=-1, keepdims=True)
        cross_queries = (shaped * lax.rsqrt(square + EPS * (variance + EPS))).astype(BF)
        allowed = (my_tenant[i][:, None] == text_tenant[None, :]) & live[None]
        cross_mixed.append(attend(cross_queries, text_keys, text_values, allowed))

    channels = w_head.shape[1]
    head_rows = lax.dynamic_index_in_dim(
        w_head.reshape(halves, groups, parts * block, channels), z_index, 1, keepdims=False
    ).reshape(-1, channels)
    totals = jnp.sum(w_head.astype(F32), axis=0)[None]
    out_width = width // columns

    leaving, sums = [], []
    for i, shifted, block_mixed in zip(spans, states, cross_mixed):
        shifted = shifted + both_columns(project_out(block_mixed, wide_cross_out))
        final = (shifted + facts[i, 0:1]).astype(BF)
        if groups > 1 and columns == halves:
            span = slice_width // halves
            final = lax.dynamic_slice_in_dim(final, wt_index * span, span, 1)
        leaving.append(final.reshape(groups, part, -1))
        some = jnp.concatenate(
            [
                jnp.dot(shifted.astype(BF), head_rows, preferred_element_type=F32),
                jnp.sum(shifted, axis=1, keepdims=True),
                jnp.sum(shifted * shifted, axis=1, keepdims=True),
            ],
            axis=1,
        )
        sums.append(some.reshape(groups, part, channels + 2))
    sums = sum_at_owner(jnp.concatenate(sums, axis=1))
    mean = sums[:, channels : channels + 1] / width
    variance = jnp.maximum(sums[:, channels + 1 :] / width - mean * mean, 0.0)
    velocity = (sums[:, :channels] - mean * totals) * lax.rsqrt(variance + EPS)

    leaving = jnp.concatenate(leaving, axis=1)
    if groups == 1:
        hidden_out = lax.dynamic_slice_in_dim(leaving[0], wt_index * out_width, out_width, 1)
    else:
        leaving = jnp.swapaxes(lax.all_to_all(leaving, "z", 0, 0), 0, 1)
        if columns == halves:
            hidden_out = leaving.reshape(tok, out_width)
        else:
            leaving = jnp.swapaxes(leaving.reshape(tok, groups, halves, -1), 1, 2)
            hidden_out = lax.dynamic_slice_in_dim(
                leaving.reshape(tok, width), wt_index * out_width, out_width, 1
            )

    channel_half = latent.shape[1]
    outgoing = lax.dynamic_slice_in_dim(velocity, (1 - half_index) * channel_half, channel_half, 1)
    partner = flip(outgoing, "cfg")
    own_part = lax.dynamic_slice_in_dim(velocity, half_index * channel_half, channel_half, 1)
    conditional = jnp.where(half_index == 0, own_part, partner)
    null_text = jnp.where(half_index == 0, partner, own_part)
    latent_next = latent + step_size[0] * (null_text + guidance[0] * (conditional - null_text))
    return (hidden_out[None], latent_next)


def solution(mesh):
    halves, seq, columns = (mesh.shape[a] for a in ("cfg", "seq", "wt"))

    def run(*args):
        heads_here = args[6].shape[1] // columns // HD
        groups = math.gcd(heads_here, seq)
        fine = Mesh(
            mesh.devices.reshape(halves, groups, seq // groups, columns), ("cfg", "z", "t", "wt")
        )
        seq_axes = ("z", "t")
        weight = P(("cfg", "z", "t"), "wt")
        return jax.shard_map(
            on_device,
            mesh=fine,
            in_specs=(
                P("cfg", seq_axes, None),
                P(seq_axes, "cfg"),
                P(),
                P(seq_axes, None),
                P(None, "cfg", None, "wt"),
                P("cfg", None),
                weight,
                weight,
                weight,
                weight,
                weight,
                weight,
                P(),
                P(),
                P(),
            ),
            out_specs=(P("cfg", seq_axes, "wt"), P(seq_axes, "cfg")),
            check_vma=False,
        )(*args)

    return run
```

```python
import math

import jax
import jax.numpy as jnp
import numpy as np
from jax import lax
from jax.experimental import pallas as pl
from jax.experimental.pallas import tpu as pltpu
from jax.sharding import Mesh
from jax.sharding import PartitionSpec as P

HD = 128
TEXT = 512
TENANTS = 4
EPS = 1e-06
CHUNKS = 2
BF = jnp.bfloat16
F32 = jnp.float32


def flip(block, axis):
    return lax.ppermute(block, axis, [(0, 1), (1, 0)])


def rotary_tables():
    sixth = HD // 6
    table = np.zeros((3, HD), np.float32)
    lane = 0
    for column, span in enumerate((HD - 4 * sixth, 2 * sixth, 2 * sixth)):
        exponent = np.arange(0, span, 2).astype(np.float32) / np.float32(span)
        frequency = (1.0 / 10000.0**exponent).astype(np.float32)
        table[column, lane : lane + span] = np.repeat(frequency, 2)
        lane += span
    swap = np.zeros((HD, HD), np.float32)
    for pair in range(0, HD, 2):
        swap[pair + 1, pair] = -1.0
        swap[pair, pair + 1] = 1.0
    return table, swap


def running_ends(lengths):
    upto = np.tril(np.ones((TENANTS, TENANTS), np.int32))
    return jnp.sum(jnp.asarray(upto) * lengths[None, :], axis=1)


def head_scale(shaped):
    return lax.rsqrt(jnp.mean(shaped * shaped, axis=-1, keepdims=True) + EPS)


def attend(queries, keys, values, allowed):
    scores = jnp.einsum("qhd,khd->hqk", queries, keys, preferred_element_type=F32)
    scores = scores * (1.0 / math.sqrt(queries.shape[-1]))
    weights = jnp.where(allowed[None], jnp.exp(scores), 0.0).astype(BF)
    summed = jnp.einsum("hqk,khd->qhd", weights, values, preferred_element_type=F32)
    totals = jnp.sum(weights.astype(F32), axis=2).T
    return (summed / totals[..., None]).astype(BF).reshape(queries.shape[0], -1)


MESH = pl.DeviceIdType.MESH
NEAR = (1, 3, 2)
LINE = 4


def remote(src, dst, sent, got, device):
    return pltpu.make_async_remote_copy(
        src_ref=src, dst_ref=dst, send_sem=sent, recv_sem=got, device_id=device, device_id_type=MESH
    )


def meet(devices):
    barrier = pltpu.get_barrier_semaphore()
    for device in devices:
        pl.semaphore_signal(barrier, inc=1, device_id=device, device_id_type=MESH)
    pl.semaphore_wait(barrier, len(devices))


def span(index, size):
    return pl.ds(pl.multiple_of(index * size, size), size)


def nt_dot(a, b):
    return lax.dot_general(a, b, (((1,), (1,)), ((), ())), preferred_element_type=F32)


def tenants_at(index, lengths):
    found, end = jnp.zeros(index.shape, jnp.int32), 0
    for tenant in range(TENANTS):
        end = end + lengths[tenant]
        found = found + (index >= end).astype(jnp.int32)
    return found


def self_attention_kernel(
    lengths, pos, table, key_index, hid, wk, wv, wq, w_out, mixed_out, raw_out, mean_out, out_wide,
    wide, rows, normed, pairs, queries, pos_all, rot,
    loc_w, loc_h, raw_sem, zs, zr, hs, hr, ps, pr, xs, xr, cs, cr, ys, yr, ks, kr, us, ur,
):
    c, z, x, y = (lax.axis_index(a) for a in ("cfg", "z", "t", "wt"))
    groups = LINE
    tok = hid.shape[0]
    depth = wk.shape[0]
    wid = rows.shape[2]
    cols = wide.shape[3]
    heads = cols // HD
    at_z = [{"z": lax.rem(z + d, groups)} for d in range(groups)]
    from_z = [lax.rem(z + groups - d, groups) for d in range(groups)]
    at_x, at_c, at_y = {"t": 1 - x}, {"cfg": 1 - c}, {"wt": 1 - y}
    weights = (wk, wv, wq)
    mine = c * groups + z

    own_rows = [
        pltpu.make_async_copy(hid.at[:, kb * wid : (kb + 1) * wid], rows.at[kb, span(z, tok)], loc_h.at[kb])
        for kb in range(2 * groups)
    ]
    own_weights = [
        pltpu.make_async_copy(w.at[:, span(z, cols)], wide.at[j, mine, span(x, depth)], loc_w.at[j])
        for j, w in enumerate(weights)
    ]
    own_pos = pltpu.make_async_copy(pos, pos_all.at[z], loc_w.at[3])
    for copy in own_rows + [own_pos] + own_weights:
        copy.start()
    meet([at_z[1], at_z[2], at_z[3], at_x, at_c, at_y])

    def block(j, d, column):
        return wide.at[j, c * groups + from_z[d], span(column, depth)]

    def x_copy(j, d):
        return remote(block(j, d, x), block(j, d, x), xs.at[d, j], xr.at[d, j], at_x)

    def x_arrival(j, d):
        return remote(block(j, d, 1 - x), block(j, d, 1 - x), xs.at[d, j], xr.at[d, j], at_x)

    def c_copy(j, d, second):
        part = block(j, d, 1 - x if second else x)
        return remote(part, part, cs.at[second, d, j], cr.at[second, d, j], at_c)

    def c_arrival(j, d, second):
        part = wide.at[j, (1 - c) * groups + from_z[d], span(1 - x if second else x, depth)]
        return remote(part, part, cs.at[second, d, j], cr.at[second, d, j], at_c)

    def z_copy(j, d):
        target = lax.rem(z + d, groups)
        return remote(
            weights[j].at[:, span(target, cols)], wide.at[j, mine, span(x, depth)], zs.at[d - 1, j], zr.at[d - 1, j], at_z[d]
        )

    def z_arrival(j, d):
        return remote(block(j, d, x), block(j, d, x), zs.at[d - 1, j], zr.at[d - 1, j], at_z[d])

    def rows_of(b, column, piece):
        return rows.at[column * groups + piece, span(b, tok)]

    def by_z(*choices):
        return jnp.where(z == 0, choices[0], jnp.where(z == 1, choices[1], jnp.where(z == 2, choices[2], choices[3])))

    inner = jnp.logical_and(z > 0, z < groups - 1)
    way_of = [None, by_z(1, 0, 1, 0), by_z(1, 1, 0, 0), by_z(1, 1, 0, 0)]
    step_of = [None, by_z(0, 0, 0, 0), by_z(1, 0, 0, 1), by_z(2, 1, 1, 2)]
    block_of = [z, by_z(1, 0, 3, 2), by_z(2, 2, 1, 1), by_z(3, 3, 0, 0)]

    def out_part(core, column):
        return out_wide.at[core, span(column, depth)]

    own_out = pltpu.make_async_copy(w_out, out_part(c, x), loc_w.at[4])
    own_out.start()
    out_x = remote(w_out, out_part(c, x), us.at[0], ur.at[0], at_x)
    out_c = remote(w_out, out_part(c, x), us.at[1], ur.at[1], at_c)
    out_on = remote(out_part(c, 1 - x), out_part(c, 1 - x), us.at[2], ur.at[2], at_c)

    def h_own(way, p):
        part = rows_of(z, y, p)
        return remote(part, part, hs.at[way, 0, p], hr.at[way, 0, p], {"z": z + 1 - 2 * way})

    def h_arrival(e, p):
        part = rows_of(block_of[e], y, p)
        return remote(part, part, hs.at[way_of[e], step_of[e], p], hr.at[way_of[e], step_of[e], p], at_y)

    def h_onward(e, p):
        part = rows_of(block_of[e], y, p)
        at = step_of[e] + 1
        return remote(part, part, hs.at[way_of[e], at, p], hr.at[way_of[e], at, p], {"z": z + 1 - 2 * way_of[e]})

    def y_copy(e, p):
        part = rows_of(block_of[e], y, p)
        return remote(part, part, ys.at[e - 1, p], yr.at[e - 1, p], at_y)

    def y_arrival(e, p):
        part = rows_of(block_of[e], 1 - y, p)
        return remote(part, part, ys.at[e - 1, p], yr.at[e - 1, p], at_y)

    def up(p):
        @pl.when(z < groups - 1)
        def _():
            h_own(0, p).start()

        @pl.when(z > 0)
        def _():
            h_own(1, p).start()

    def arrive(e):
        for p in range(groups):
            h_arrival(e, p).wait_recv()

            @pl.when(inner)
            def _():
                h_onward(e, p).start()

            y_copy(e, p).start()

    def p_copy(d):
        return remote(pos_all.at[z], pos_all.at[z], ps.at[d - 1], pr.at[d - 1], at_z[d])

    def p_arrival(d):
        part = pos_all.at[from_z[d]]
        return remote(part, part, ps.at[d - 1], pr.at[d - 1], at_z[d])

    some = 16
    width = 2 * groups * wid

    def norm_block(b):
        def norm(i, carry):
            these = pl.ds(pl.multiple_of(b * tok + i * some, some), some)
            total = jnp.zeros((some, wid), F32)
            for kb in range(2 * groups):
                total += rows[kb, these].astype(F32)
            mean = jnp.sum(total, axis=1, keepdims=True) / width
            total = jnp.zeros((some, wid), F32)
            for kb in range(2 * groups):
                centred = rows[kb, these].astype(F32) - mean
                total += centred * centred
            scale = lax.rsqrt(jnp.sum(total, axis=1, keepdims=True) / width + EPS)
            for kb in range(2 * groups):
                normed[kb, these] = ((rows[kb, these].astype(F32) - mean) * scale).astype(BF)
            mean_out[these] = mean
            return carry

        lax.fori_loop(0, tok // some, norm, 0)

    for copy in own_rows + [own_pos]:
        copy.wait()
    for d in NEAR:
        p_copy(d).start()
    for d in NEAR:
        z_copy(0, d).start()
    for j in range(3):
        own_weights[j].wait()
        x_copy(j, 0).start()
        c_copy(j, 0, 0).start()
    norm_block(z)

    def relay(j, d):
        z_arrival(j, d).wait_recv()
        x_copy(j, d).start()
        c_copy(j, d, 0).start()

    def second_relay(j, d):
        x_arrival(j, d).wait_recv()
        c_copy(j, d, 1).start()

    for j in range(3):
        second_relay(j, 0)
    relay(0, 1)
    for d in NEAR:
        z_copy(1, d).start()
    relay(0, 3)
    relay(0, 2)
    for p in range(groups):
        up(p)
    for d in NEAR:
        second_relay(0, d)
    relay(1, 1)
    relay(1, 3)
    relay(1, 2)
    for d in NEAR:
        second_relay(1, d)
    out_x.start()
    out_c.start()
    arrive(1)

    @pl.when(inner)
    def _():
        arrive(2)

    for d in NEAR:
        p_arrival(d).wait_recv()
    lane = lax.broadcasted_iota(jnp.int32, (tok, HD), 1)
    even = lax.rem(lane, 2) == 0
    for m in range(groups):
        held = pos_all[m]
        full = jnp.concatenate([held, jnp.zeros((HD - held.shape[0], held.shape[1]), F32)], axis=0)
        column = jnp.transpose(full)[:tok]
        angles = sum(column[:, a : a + 1] * table[a : a + 1, :] for a in range(3))
        rot[0, m * tok : (m + 1) * tok] = jnp.cos(angles)
        sinus = jnp.sin(angles)
        rot[1, m * tok : (m + 1) * tok] = jnp.where(even, -sinus, sinus)

    def rotated(these, total):
        turned = []
        for h in range(heads):
            part = total[:, h * HD : (h + 1) * HD]
            scale = lax.rsqrt(jnp.mean(part * part, axis=1, keepdims=True) + EPS)
            swapped = jnp.where(even, pltpu.roll(part, HD - 1, 1), pltpu.roll(part, 1, 1))
            turned.append((part * rot[0, these] + swapped * rot[1, these]) * scale)
        return jnp.concatenate(turned, axis=1).astype(BF)

    def pair_copy(e):
        part = pairs.at[x, :, span(block_of[e], tok)]
        return remote(part, part, ks.at[e], kr.at[e], at_x)

    def pair_arrival(e):
        part = pairs.at[1 - x, :, span(block_of[e], tok)]
        return remote(part, part, ks.at[e], kr.at[e], at_x)

    def project(e, j):
        these = span(block_of[e] if j < 2 else e, tok)
        total = jnp.dot(normed[0, these], wide[j, 0], preferred_element_type=F32)
        for kb in range(1, 2 * groups):
            total += jnp.dot(normed[kb, these], wide[j, kb], preferred_element_type=F32)
        if j == 0:
            pairs[x, 0, these] = rotated(these, total)
        elif j == 1:
            pairs[x, 1, these] = total.astype(BF)
            pair_copy(e).start()
        else:
            queries[these] = rotated(these, total)

    def all_here(j):
        for d in range(groups):
            c_arrival(j, d, 0).wait_recv()
            c_arrival(j, d, 1).wait_recv()

    def finish(e):
        for p in range(groups):
            y_arrival(e, p).wait_recv()
        norm_block(block_of[e])
        project(e, 0)
        project(e, 1)

    all_here(0)
    all_here(1)
    project(0, 0)
    project(0, 1)

    @pl.when(inner)
    def _():
        arrive(3)

    @pl.when(jnp.logical_not(inner))
    def _():
        arrive(2)

    for d in NEAR:
        z_copy(2, d).start()
    out_here = remote(out_part(c, 1 - x), out_part(c, 1 - x), us.at[0], ur.at[0], at_x)
    out_here.wait_recv()
    out_on.start()
    finish(1)

    @pl.when(jnp.logical_not(inner))
    def _():
        arrive(3)

    relay(2, 1)
    relay(2, 3)
    raws = [
        pltpu.make_async_copy(rows.at[half * groups + z], raw_out.at[half], raw_sem.at[half]) for half in (0, 1)
    ]
    finish(2)
    relay(2, 2)
    for d in NEAR:
        second_relay(2, d)
    finish(3)
    for copy in raws:
        copy.start()
    all_here(2)

    def ask(m, carry):
        project(m, 2)
        return carry

    lax.fori_loop(0, groups, ask, 0)
    for e in range(groups):
        pair_arrival(e).wait_recv()

    key_tenant = tenants_at(key_index[0:1], lengths)
    ones = jnp.ones((groups * tok, HD), BF)

    def attend_block(m, carry):
        these = span(m, tok)
        index = lax.broadcasted_iota(jnp.int32, (tok, 1), 0) + (m * 2 + x) * tok
        allowed = tenants_at(index, lengths) == key_tenant
        for h in range(heads):
            lanes = slice(h * HD, (h + 1) * HD)
            summed = jnp.zeros((tok, 2 * HD), F32)
            for part in (0, 1):
                scores = nt_dot(queries[these, lanes], pairs[part, 0, :, lanes]) * (1.0 / math.sqrt(HD))
                here = allowed[:, part * groups * tok : (part + 1) * groups * tok]
                chances = jnp.where(here, jnp.exp(scores), 0.0).astype(BF)
                both = jnp.concatenate([pairs[part, 1, :, lanes], ones], axis=1)
                summed += jnp.dot(chances, both, preferred_element_type=F32)
            mixed_out[these, lanes] = (summed[:, :HD] / summed[:, HD:]).astype(BF)
        return carry

    lax.fori_loop(0, groups, attend_block, 0)

    for copy in raws:
        copy.wait()
    for p in range(groups):
        @pl.when(z < groups - 1)
        def _():
            h_own(0, p).wait_send()

        @pl.when(z > 0)
        def _():
            h_own(1, p).wait_send()

        for e in (1, 2, 3):
            @pl.when(inner)
            def _():
                h_onward(e, p).wait_send()

            y_copy(e, p).wait_send()
    for d in NEAR:
        p_copy(d).wait_send()
        for j in range(3):
            z_copy(j, d).wait_send()
    for d in range(groups):
        for j in range(3):
            x_copy(j, d).wait_send()
            c_copy(j, d, 0).wait_send()
            c_copy(j, d, 1).wait_send()
    for e in range(groups):
        pair_copy(e).wait_send()
    own_out.wait()
    out_x.wait_send()
    for index, part in ((1, out_part(1 - c, x)), (2, out_part(1 - c, 1 - x))):
        remote(part, part, us.at[index], ur.at[index], at_c).wait()


def self_attention_call(lengths, hidden, positions, wk, wv, wq, w_out):
    tok, width = hidden.shape
    groups = LINE
    depth, local_cols = wk.shape
    cols = local_cols // groups
    rows = groups * tok
    wid = width // (2 * groups)
    anywhere = pl.BlockSpec(memory_space=pl.ANY)
    vmem = pl.BlockSpec(memory_space=pltpu.VMEM)
    smem = pl.BlockSpec(memory_space=pltpu.SMEM)
    dma = pltpu.SemaphoreType.DMA
    made = [
        jax.ShapeDtypeStruct((rows, cols), BF),
        jax.ShapeDtypeStruct((2, rows, wid), BF),
        jax.ShapeDtypeStruct((rows, 1), F32),
        jax.ShapeDtypeStruct((2, 2 * depth, local_cols), BF),
    ]
    table = np.zeros((8, HD), np.float32)
    table[:3] = rotary_tables()[0]
    place = np.arange(2 * rows)
    place = (place % rows // tok * 2 + place // rows) * tok + place % tok
    place = np.broadcast_to(place.astype(np.int32), (8, 2 * rows))
    pos = jnp.pad(positions.T.astype(F32), ((0, 5), (0, -tok % 128)))
    return pl.pallas_call(
        self_attention_kernel,
        out_shape=made,
        in_specs=[smem, vmem, vmem, vmem] + [anywhere] * 5,
        out_specs=[vmem] * 3 + [anywhere],
        scratch_shapes=[
            pltpu.VMEM((3, 2 * groups, 2 * depth, cols), BF),
            pltpu.VMEM((2 * groups, rows, wid), BF),
            pltpu.VMEM((2 * groups, rows, wid), BF),
            pltpu.VMEM((2, 2, rows, cols), BF),
            pltpu.VMEM((rows, cols), BF),
            pltpu.VMEM((groups,) + pos.shape, F32),
            pltpu.VMEM((2, rows, HD), F32),
            dma((5,)), dma((2 * groups,)), dma((2,)),
            dma((3, 3)), dma((3, 3)),
            dma((2, 3, 4)), dma((2, 3, 4)),
            dma((3,)), dma((3,)),
            dma((4, 3)), dma((4, 3)),
            dma((2, 4, 3)), dma((2, 4, 3)),
            dma((3, 4)), dma((3, 4)),
            dma((4,)), dma((4,)), dma((3,)), dma((3,)),
        ],
        compiler_params=pltpu.CompilerParams(
            collective_id=0, has_side_effects=True, vmem_limit_bytes=56 * 2**20
        ),
        cost_estimate=pl.CostEstimate(
            flops=6 * rows * width * cols, bytes_accessed=20 * 2**20, transcendentals=0
        ),
    )(lengths, pos, jnp.asarray(table), jnp.asarray(place), hidden, wk, wv, wq, w_out)


def line_places(z):
    def block(way, s):
        return z - s if way == 0 else z + s

    def sends(way, s):
        if way == 0:
            return jnp.logical_and(z - s >= 0, z + 1 < LINE)
        return jnp.logical_and(z + s < LINE, z >= 1)

    def gets(way, s):
        return z - 1 - s >= 0 if way == 0 else z + 1 + s < LINE

    return block, sends, gets


def pack_columns(first, second):
    tok = first.shape[0]
    lane = lax.broadcasted_iota(jnp.int32, (tok, HD), 1)
    both = jnp.where(lane == 0, first, jnp.where(lane == 1, second, 0.0))
    both = jnp.concatenate([both, jnp.zeros((-tok % HD, HD), F32)], axis=0)
    return jnp.transpose(both)[:8]


def unpack_columns(packed, tok):
    full = jnp.concatenate([packed, jnp.zeros((HD - packed.shape[0], packed.shape[1]), F32)], axis=0)
    column = jnp.transpose(full)[:tok]
    return column[:, 0:1], column[:, 1:2]


def cross_attention_kernel(
    lengths, text_lengths, guidance, step_size, mixed, raw, mean, head, latent, text_kv, w_out, w_cross, w_last,
    hidden_out, latent_out,
    wide, text, gath, own, left, right, left2, right2, kept, state, asked, answers, facts, facts_in, cols_out, cols_in,
    leaving, vel, vel_in, half_out, half_in, core_out, core_in,
    loc_w, loc_t, loc_g, loc_f, ws, wr, wcs, wcr, gs, gr, ys, yr, y2s, y2r, qs, qr, fs, fr, ss, sr, os_, or_, vs, vr, es, er,
):
    c, z, x, y = (lax.axis_index(a) for a in ("cfg", "z", "t", "wt"))
    groups = LINE
    rows, cols = mixed.shape
    tok = rows // groups
    depth = w_last.shape[0]
    wid = raw.shape[2]
    width = 2 * groups * wid
    heads = cols // HD
    channels = head.shape[1]
    slots = text.shape[1] // TENANTS
    at_z = [{"z": lax.rem(z + d, groups)} for d in range(groups)]
    from_z = [lax.rem(z + groups - d, groups) for d in range(groups)]
    at_x, at_c, at_y = {"t": 1 - x}, {"cfg": 1 - c}, {"wt": 1 - y}
    at_line = ({"z": jnp.minimum(z + 1, groups - 1)}, {"z": jnp.maximum(z - 1, 0)})
    line_block, line_sends, line_gets = line_places(z)
    own_weights = [pltpu.make_async_copy(w_out, wide.at[0], loc_w.at[0])]
    own_weights += [
        pltpu.make_async_copy(w, wide.at[j, c, span(x, depth)], loc_w.at[j]) for j, w in ((1, w_cross), (2, w_last))
    ]
    own_text = [pltpu.make_async_copy(text_kv.at[k, 0, :, span(z, cols)], text.at[k], loc_t.at[k]) for k in (0, 1)]
    for copy in own_weights + own_text:
        copy.start()
    own[0] = mixed[...].reshape(groups, tok, cols)
    meet([at_z[1], at_z[2], at_z[3], at_x, at_c, at_y])

    def g_local(f, i):
        return pltpu.make_async_copy(own.at[f, i], gath.at[f, i, :, span(z, cols)], loc_g.at[f, i])

    def g_copy(f, i, way, s):
        part = gath.at[f, i, :, span(line_block(way, s), cols)]
        return remote(own.at[f, i] if s == 0 else part, part, gs.at[f, i, way, s], gr.at[f, i, way, s], at_line[way])

    def g_arrival(f, i, way, s):
        part = gath.at[f, i, :, span(line_block(way, s + 1), cols)]
        return remote(part, part, gs.at[f, i, way, s], gr.at[f, i, way, s], at_line[way])

    def g_start(f, i):
        for way in (0, 1):
            @pl.when(line_sends(way, 0))
            def _():
                g_copy(f, i, way, 0).start()
        g_local(f, i).start()

    def g_step(f, i, s):
        for way in (0, 1):
            @pl.when(line_gets(way, s))
            def _():
                g_arrival(f, i, way, s).wait_recv()
                if s + 1 < groups - 1:
                    @pl.when(line_sends(way, s + 1))
                    def _():
                        g_copy(f, i, way, s + 1).start()
        if s == groups - 2:
            g_local(f, i).wait()

    def w_part(j, core, column):
        return wide.at[j, core, span(column, depth)]

    def w_copy(j):
        return remote(w_part(j, c, x), w_part(j, c, x), ws.at[j], wr.at[j], at_x)

    def w_arrival(j):
        return remote(w_part(j, c, 1 - x), w_part(j, c, 1 - x), ws.at[j], wr.at[j], at_x)

    def wc_copy(j, second):
        part = w_part(j, c, 1 - x if second else x)
        return remote(part, part, wcs.at[j, second], wcr.at[j, second], at_c)

    def wc_arrival(j, second):
        part = w_part(j, 1 - c, 1 - x if second else x)
        return remote(part, part, wcs.at[j, second], wcr.at[j, second], at_c)

    def w_relay(j):
        w_arrival(j).wait_recv()
        wc_copy(j, 1).start()

    def w_ready(j):
        wc_arrival(j, 0).wait_recv()
        wc_arrival(j, 1).wait_recv()

    turn = (0, 3, 1, 2)
    for i in turn:
        g_start(0, i)
    for j in (1, 2):
        own_weights[j].wait()
        w_copy(j).start()
        wc_copy(j, 0).start()

    for copy in own_text:
        copy.wait()

    def norm_text(i, carry):
        these = span(i, HD)
        for h in range(heads):
            lanes = slice(h * HD, (h + 1) * HD)
            part = text[0, these, lanes].astype(F32)
            scale = lax.rsqrt(jnp.mean(part * part, axis=1, keepdims=True) + EPS)
            text[0, these, lanes] = (part * scale).astype(BF)
        return carry

    lax.fori_loop(0, text.shape[1] // HD, norm_text, 0)
    totals = jnp.sum(head[...].astype(F32), axis=0, keepdims=True)

    def y_copy(i):
        return remote(left.at[i], right.at[i], ys.at[i], yr.at[i], at_y)

    def y2_copy(i):
        return remote(left2.at[i], right2.at[i], y2s.at[i], y2r.at[i], at_y)

    def q_copy(i, d):
        return remote(asked.at[i, lax.rem(z + d, groups)], answers.at[i, z], qs.at[i, d - 1], qr.at[i, d - 1], at_z[d])

    def q_arrival(i, d):
        part = answers.at[i, from_z[d]]
        return remote(part, part, qs.at[i, d - 1], qr.at[i, d - 1], at_z[d])

    def f_copy(i, d):
        return remote(facts.at[i], facts_in.at[i, z], fs.at[i, d - 1], fr.at[i, d - 1], at_z[d])

    def f_arrival(i, d):
        part = facts_in.at[i, from_z[d]]
        return remote(part, part, fs.at[i, d - 1], fr.at[i, d - 1], at_z[d])

    def s_copy(d):
        return remote(cols_out.at[lax.rem(z + d, groups)], cols_in.at[z], ss.at[d - 1], sr.at[d - 1], at_z[d])

    def s_arrival(d):
        part = cols_in.at[from_z[d]]
        return remote(part, part, ss.at[d - 1], sr.at[d - 1], at_z[d])

    def project_out(i):
        for half in (0, 1):
            left[i, :, half * wid : (half + 1) * wid] = nt_dot(gath[0, i], wide[0, half]).astype(BF)
        y_copy(i).start()

    def sum_columns():
        ones = jnp.ones((16, wid), BF)
        for g in range(groups):
            lanes = slice(g * cols, (g + 1) * cols)
            total = jnp.dot(ones, wide[1, 0, :, lanes], preferred_element_type=F32)
            total += jnp.dot(ones, wide[1, 1, :, lanes], preferred_element_type=F32)
            cols_out[g] = total[:8]
        for d in NEAR:
            s_copy(d).start()

    def update(i):
        y_copy(i).wait_recv()
        these = slice(i * tok, (i + 1) * tok)
        shift = mean[these]
        first = second = jnp.zeros((tok, 1), F32)
        for half in (0, 1):
            lanes = slice(half * wid, (half + 1) * wid)
            both = left[i, :, lanes].astype(F32) + right[i, :, lanes].astype(F32)
            new = (raw[half, these].astype(F32) - shift) + both
            state[i, half] = new
            first += jnp.sum(new, axis=1, keepdims=True)
            second += jnp.sum(new * new, axis=1, keepdims=True)
        facts[i] = pack_columns(first, second)
        for d in NEAR:
            f_copy(i, d).start()
        for g in range(groups):
            lanes = slice(g * cols, (g + 1) * cols)
            part = jnp.dot(state[i, 0].astype(BF), wide[1, 0, :, lanes], preferred_element_type=F32)
            part += jnp.dot(state[i, 1].astype(BF), wide[1, 1, :, lanes], preferred_element_type=F32)
            asked[i, g] = part.astype(BF)
        for d in NEAR:
            q_copy(i, d).start()

    def cross(i):
        packed = facts[i]
        crossed = asked[i, z].astype(F32)
        column_sums = cols_out[z, 0:1]
        for d in NEAR:
            q_arrival(i, d).wait_recv()
            f_arrival(i, d).wait_recv()
            if i == turn[0]:
                s_arrival(d).wait_recv()
            packed = packed + facts_in[i, from_z[d]]
            crossed = crossed + answers[i, from_z[d]].astype(F32)
            column_sums = column_sums + cols_in[from_z[d], 0:1]
        first, second = unpack_columns(packed, tok)
        average = first / width
        variance = jnp.maximum(second / width - average * average, 0.0)
        crossed = crossed - average * column_sums
        index = lax.broadcasted_iota(jnp.int32, (tok, 1), 0) + (i * 2 + x) * tok
        tenant = tenants_at(index, lengths)
        slot = lax.broadcasted_iota(jnp.int32, (1, slots), 1)
        ones = jnp.ones((slots, HD), BF)
        for h in range(heads):
            lanes = slice(h * HD, (h + 1) * HD)
            part = crossed[:, lanes]
            square = jnp.mean(part * part, axis=1, keepdims=True)
            query = (part * lax.rsqrt(square + EPS * (variance + EPS))).astype(BF)
            summed = jnp.zeros((tok, 2 * HD), F32)
            for t in range(TENANTS):
                these = slice(t * slots, (t + 1) * slots)
                scores = nt_dot(query, text[0, these, lanes]) * (1.0 / math.sqrt(HD))
                allowed = jnp.logical_and(tenant == t, slot < text_lengths[0, t])
                chances = jnp.where(allowed, jnp.exp(scores), 0.0).astype(BF)
                both = jnp.concatenate([text[1, these, lanes], ones], axis=1)
                summed += jnp.dot(chances, both, preferred_element_type=F32)
            own[1, i, :, lanes] = (summed[:, :HD] / summed[:, HD:]).astype(BF)
        g_start(1, i)

    def project_last(i):
        left2[i] = nt_dot(gath[1, i], wide[2, 1 - y]).astype(BF)
        y2_copy(i).start()
        kept[i] = nt_dot(gath[1, i], wide[2, y]).astype(BF)

    def o_remote(i):
        return remote(leaving.at[i], hidden_out.at[:, span(z, wid)], os_.at[i], or_.at[z], {"z": i})

    def o_local(i):
        return pltpu.make_async_copy(leaving.at[i], hidden_out.at[:, span(z, wid)], loc_f)

    def v_remote(i):
        return remote(vel.at[i], vel_in.at[z], vs.at[i], vr.at[z], {"z": i})

    def finish(i):
        y2_copy(i).wait_recv()
        these = slice(i * tok, (i + 1) * tok)
        final = state[i, y] + kept[i].astype(F32) + right2[i].astype(F32)
        leaving[i] = (final + mean[these]).astype(BF)

        @pl.when(z != i)
        def _():
            o_remote(i).start()

        @pl.when(z == i)
        def _():
            o_local(i).start()

        rows_here = pl.ds(pl.multiple_of((y * groups + z) * wid, wid), wid)
        some = jnp.dot(final.astype(BF), head[rows_here], preferred_element_type=F32)
        first = jnp.sum(final, axis=1, keepdims=True)
        second = jnp.sum(final * final, axis=1, keepdims=True)
        lane = lax.broadcasted_iota(jnp.int32, (tok, HD - channels), 1)
        tail = jnp.where(lane == 0, first, jnp.where(lane == 1, second, 0.0))
        vel[i] = jnp.concatenate([some, tail], axis=1)

        @pl.when(z != i)
        def _():
            v_remote(i).start()

    g_step(0, turn[0], 0)
    g_step(0, turn[1], 0)
    g_step(0, turn[0], 1)
    g_step(0, turn[2], 0)
    g_step(0, turn[1], 1)
    g_step(0, turn[0], 2)
    own_weights[0].wait()
    project_out(turn[0])
    g_step(0, turn[3], 0)
    g_step(0, turn[2], 1)
    g_step(0, turn[1], 2)
    project_out(turn[1])
    w_relay(1)
    g_step(0, turn[3], 1)
    g_step(0, turn[2], 2)
    project_out(turn[2])
    w_ready(1)
    sum_columns()
    update(turn[0])
    g_step(0, turn[3], 2)
    project_out(turn[3])
    update(turn[1])
    cross(turn[0])
    update(turn[2])
    w_relay(2)
    g_step(1, turn[0], 0)
    cross(turn[1])
    update(turn[3])
    g_step(1, turn[1], 0)
    g_step(1, turn[0], 1)
    cross(turn[2])
    g_step(1, turn[2], 0)
    g_step(1, turn[1], 1)
    g_step(1, turn[0], 2)
    w_ready(2)
    project_last(turn[0])
    cross(turn[3])
    g_step(1, turn[3], 0)
    g_step(1, turn[2], 1)
    g_step(1, turn[1], 2)
    project_last(turn[1])
    finish(turn[0])
    g_step(1, turn[3], 1)
    g_step(1, turn[2], 2)
    project_last(turn[2])
    finish(turn[1])
    g_step(1, turn[3], 2)
    project_last(turn[3])
    finish(turn[2])
    finish(turn[3])

    total = vel[z]
    for d in NEAR:
        part = vel_in.at[from_z[d]]
        remote(part, part, vs.at[d], vr.at[from_z[d]], at_z[d]).wait_recv()
        total = total + vel_in[from_z[d]]
    half_out[...] = total
    over_y = remote(half_out, half_in, es.at[0], er.at[0], at_y)
    over_y.start()
    over_y.wait()
    total = half_out[...] + half_in[...]
    average = total[:, channels : channels + 1] / width
    variance = jnp.maximum(total[:, channels + 1 : channels + 2] / width - average * average, 0.0)
    velocity = (total[:, :channels] - average * totals) * lax.rsqrt(variance + EPS)
    core_out[...] = jnp.concatenate([velocity, velocity], axis=1)
    over_c = remote(core_out, core_in, es.at[1], er.at[1], at_c)
    over_c.start()
    over_c.wait()
    span_out = latent.shape[1]
    mine, other = core_out[...], core_in[...]
    here = [jnp.where(c == 0, both[:, :span_out], both[:, span_out : 2 * span_out]) for both in (mine, other)]
    conditional = jnp.where(c == 0, here[0], here[1])
    null_text = jnp.where(c == 0, here[1], here[0])
    latent_out[...] = latent[...] + step_size[0] * (null_text + guidance[0] * (conditional - null_text))

    for d in NEAR:
        part = hidden_out.at[:, span(from_z[d], wid)]
        remote(part, part, os_.at[d], or_.at[from_z[d]], at_z[d]).wait_recv()
    for i in range(groups):
        @pl.when(z != i)
        def _():
            o_remote(i).wait_send()
            v_remote(i).wait_send()

        @pl.when(z == i)
        def _():
            o_local(i).wait()

        y_copy(i).wait_send()
        y2_copy(i).wait_send()
        for d in NEAR:
            q_copy(i, d).wait_send()
            f_copy(i, d).wait_send()
        for f in (0, 1):
            for way in (0, 1):
                for s in range(groups - 1):
                    @pl.when(line_sends(way, s))
                    def _():
                        g_copy(f, i, way, s).wait_send()
    for d in NEAR:
        s_copy(d).wait_send()
    for j in (1, 2):
        w_copy(j).wait_send()
        wc_copy(j, 0).wait_send()
        wc_copy(j, 1).wait_send()


def cross_attention_call(
    lengths, text_lengths, guidance, step_size, mixed, raw, mean, head, latent, text_kv, w_out, w_cross, w_last
):
    groups = LINE
    rows, cols = mixed.shape
    tok = rows // groups
    wid = raw.shape[2]
    depth, local_cols = w_last.shape
    padded = tok + -tok % HD
    anywhere = pl.BlockSpec(memory_space=pl.ANY)
    vmem = pl.BlockSpec(memory_space=pltpu.VMEM)
    smem = pl.BlockSpec(memory_space=pltpu.SMEM)
    dma = pltpu.SemaphoreType.DMA
    return pl.pallas_call(
        cross_attention_kernel,
        out_shape=[
            jax.ShapeDtypeStruct((tok, groups * wid), BF),
            jax.ShapeDtypeStruct(latent.shape, F32),
        ],
        in_specs=[smem] * 4 + [vmem] * 5 + [anywhere] * 4,
        out_specs=[anywhere, vmem],
        scratch_shapes=[
            pltpu.VMEM((3, 2, 2 * depth, local_cols), BF),
            pltpu.VMEM((2, text_kv.shape[2], cols), BF),
            pltpu.VMEM((2, groups, tok, local_cols), BF),
            pltpu.VMEM((2, groups, tok, cols), BF),
            pltpu.VMEM((groups, tok, 2 * wid), BF),
            pltpu.VMEM((groups, tok, 2 * wid), BF),
            pltpu.VMEM((groups, tok, wid), BF),
            pltpu.VMEM((groups, tok, wid), BF),
            pltpu.VMEM((groups, tok, wid), BF),
            pltpu.VMEM((groups, 2, tok, wid), F32),
            pltpu.VMEM((groups, groups, tok, cols), BF),
            pltpu.VMEM((groups, groups, tok, cols), BF),
            pltpu.VMEM((groups, 8, padded), F32),
            pltpu.VMEM((groups, groups, 8, padded), F32),
            pltpu.VMEM((groups, 8, cols), F32),
            pltpu.VMEM((groups, 8, cols), F32),
            pltpu.VMEM((groups, tok, wid), BF),
            pltpu.VMEM((groups, tok, HD), F32),
            pltpu.VMEM((groups, tok, HD), F32),
            pltpu.VMEM((tok, HD), F32),
            pltpu.VMEM((tok, HD), F32),
            pltpu.VMEM((tok, HD), F32),
            pltpu.VMEM((tok, HD), F32),
            dma((3,)), dma((2,)), dma((2, groups)), dma,
            dma((3,)), dma((3,)), dma((3, 2)), dma((3, 2)),
            dma((2, groups, 2, 3)), dma((2, groups, 2, 3)),
            dma((groups,)), dma((groups,)), dma((groups,)), dma((groups,)),
            dma((groups, 3)), dma((groups, 3)), dma((groups, 3)), dma((groups, 3)),
            dma((3,)), dma((3,)),
            dma((groups,)), dma((groups,)), dma((groups,)), dma((groups,)),
            dma((2,)), dma((2,)),
        ],
        compiler_params=pltpu.CompilerParams(
            collective_id=1, has_side_effects=True, vmem_limit_bytes=56 * 2**20
        ),
        cost_estimate=pl.CostEstimate(
            flops=20 * rows * wid * local_cols, bytes_accessed=20 * 2**20, transcendentals=0
        ),
    )(lengths, text_lengths, guidance, step_size, mixed, raw, mean, head, latent, text_kv, w_out, w_cross, w_last)


def on_device(
    hidden,
    latent,
    tenant_lengths,
    grid_positions,
    text_kv,
    text_lengths,
    w_query,
    w_key,
    w_value,
    w_out,
    w_cross_query,
    w_cross_out,
    w_head,
    guidance,
    step_size,
):
    halves, groups, parts, columns = (lax.axis_size(a) for a in ("cfg", "z", "t", "wt"))
    half_index, z_index, t_index, wt_index = (
        lax.axis_index(a) for a in ("cfg", "z", "t", "wt")
    )
    tok, width = hidden.shape[1:]
    rows = groups * tok
    local_cols = w_query.shape[1]
    my_cols = local_cols // groups
    heads = my_cols // HD
    paired = halves == 2 and parts == 2
    block = w_query.shape[0]
    if paired and groups == LINE and columns == 2 and tok % 16 == 0 and block % 16 == 0 and my_cols % HD == 0:
        mixed, raw, mean, out_wide = self_attention_call(
            tenant_lengths, hidden[0], grid_positions, w_key, w_value, w_query, w_out
        )
        hidden_out, latent_next = cross_attention_call(
            tenant_lengths, text_lengths, guidance, step_size, mixed, raw, mean, w_head, latent,
            text_kv, out_wide, w_cross_query, w_cross_out,
        )
        return (hidden_out[None], latent_next)
    ends = running_ends(tenant_lengths)

    def tenant_of(indices):
        return jnp.sum((indices[:, None] >= ends[None, :]).astype(jnp.int32), axis=1)

    def ordered(mine, other, index):
        return jnp.where(
            index == 0, jnp.concatenate([mine, other]), jnp.concatenate([other, mine])
        )

    def wide(w):
        if not paired:
            return lax.all_gather(w, ("cfg", "t"), axis=0, tiled=True)
        two = ordered(w, flip(w, "t"), t_index)
        return ordered(two, flip(two, "cfg"), half_index)

    def over_groups(x):
        return x if groups == 1 else lax.all_to_all(x, "z", 0, 0, tiled=True)

    def join_groups(x):
        if groups == 1:
            return x
        x = lax.all_gather(x, "z", axis=0)
        return jnp.swapaxes(x, 0, 1).reshape(x.shape[1], local_cols)

    def sum_at_owner(x):
        if groups == 1:
            return x[0].astype(F32)
        return jnp.sum(lax.all_to_all(x, "z", 0, 0).astype(F32), axis=0)

    def sum_groups(x):
        if groups == 1:
            return x
        return lax.psum_scatter(x, "z", scatter_dimension=0, tiled=True)

    def to_groups(x, n):
        return jnp.swapaxes(x.reshape(x.shape[0], groups, n), 0, 1)

    def both_columns(terms):
        terms = terms.astype(BF)
        if columns == 1:
            return terms.astype(F32)
        if columns == 2:
            return terms.astype(F32) + flip(terms, "wt").astype(F32)
        return lax.psum(terms, "wt").astype(F32)

    if paired:
        key_pair = ordered(w_key, flip(w_key, "t"), t_index)
        key_pair, w_query, w_value = lax.optimization_barrier((key_pair, w_query, w_value))
        wide_key = ordered(key_pair, flip(key_pair, "cfg"), half_index)
    else:
        wide_key = wide(w_key)
    wide_query, wide_value = wide(w_query), wide(w_value)
    wide_out, wide_cross, wide_cross_out = wide(w_out), wide(w_cross_query), wide(w_cross_out)

    chunks = CHUNKS if groups > 1 and tok % (CHUNKS * 16) == 0 else 1
    part = tok // chunks
    chunk_rows = rows // chunks

    def by_chunk(x):
        shape = (groups, chunks, part) + x.shape[2:]
        return jnp.swapaxes(x.reshape(shape), 0, 1).reshape((rows,) + x.shape[2:])

    def three_terms(x):
        high = lax.reduce_precision(x, 8, 7)
        middle = lax.reduce_precision(x - high, 8, 7)
        return [term.astype(BF) for term in (high, middle, x - high - middle)]

    own = hidden[0].astype(F32)
    mean = jnp.mean(own, axis=-1, keepdims=True)
    centred = own - mean
    scale = lax.rsqrt(jnp.mean(centred * centred, axis=-1, keepdims=True) + EPS)
    facts = jnp.concatenate([mean, scale, grid_positions.astype(F32)], axis=1)
    slice_width = width // groups
    if groups == 1:
        sliced = own
    else:
        extra = jnp.concatenate(three_terms(facts), axis=1)
        extra = jnp.pad(extra, ((0, 0), (0, 128 - extra.shape[1])))
        features = hidden[0].reshape(tok, halves, groups, slice_width // halves)
        features = jnp.concatenate(
            [features[:, half] for half in range(halves)]
            + [jnp.broadcast_to(extra[:, None], (tok, groups, 128))],
            axis=2,
        )
        arrived = lax.all_to_all(jnp.swapaxes(features, 0, 1), "z", 0, 0)
        arrived = by_chunk(arrived).astype(F32)
        sliced = arrived[:, :slice_width]
        extra = arrived[:, slice_width : slice_width + 15]
        facts = extra[:, 0:5] + extra[:, 5:10] + extra[:, 10:15]
    normed = ((sliced - facts[:, 0:1]) * facts[:, 1:2]).astype(BF)

    def project(w):
        return to_groups(jnp.dot(normed, w, preferred_element_type=F32).astype(BF), my_cols)

    projected_keys = sum_at_owner(project(wide_key)).astype(BF)
    projected = jnp.concatenate([project(wide_query), project(wide_value)], axis=2)
    projected = sum_groups(projected.reshape(groups * rows, 2 * my_cols))

    table, swap = rotary_tables()
    angles = (
        facts[:, 2:3] * table[0][None] + facts[:, 3:4] * table[1][None] + facts[:, 4:5] * table[2][None]
    )
    cosine, sinus = jnp.cos(angles)[:, None, :], jnp.sin(angles)[:, None, :]

    def rotated(x):
        shaped = x.reshape(rows, heads, HD)
        swapped = jnp.einsum("thd,de->the", shaped, jnp.asarray(swap, BF), preferred_element_type=F32)
        shaped = shaped.astype(F32)
        return ((shaped * cosine + swapped * sinus) * head_scale(shaped)).astype(BF)

    keys = rotated(projected_keys).reshape(rows, my_cols)
    queries = rotated(projected[:, :my_cols])
    values = projected[:, my_cols:]

    base = jnp.arange(groups, dtype=jnp.int32)[:, None] * (parts * tok)
    base = by_chunk(base + jnp.arange(tok, dtype=jnp.int32)[None])
    my_tenant = tenant_of(base + t_index * tok)
    if parts == 2:
        keys = jnp.concatenate([keys, flip(keys, "t")], axis=0)
        values = jnp.concatenate([values, flip(values, "t")], axis=0)
        key_tenant = jnp.concatenate([my_tenant, tenant_of(base + (1 - t_index) * tok)])
    else:
        keys = lax.all_gather(keys, "t", axis=0, tiled=True)
        values = lax.all_gather(values, "t", axis=0, tiled=True)
        key_tenant = tenant_of(
            (jnp.arange(parts, dtype=jnp.int32)[:, None] * tok + base[None]).reshape(-1)
        )
    keys = keys.reshape(-1, heads, HD)
    values = values.reshape(-1, heads, HD)

    spans = [slice(i * chunk_rows, (i + 1) * chunk_rows) for i in range(chunks)]
    mixed = [
        attend(queries[i], keys, values, my_tenant[i][:, None] == key_tenant[None, :])
        for i in spans
    ]

    def project_out(mixed, weight):
        return lax.dot_general(
            join_groups(mixed), weight, (((1,), (1,)), ((), ())), preferred_element_type=F32
        )

    column_sums = jnp.dot(jnp.ones((8, slice_width), BF), wide_cross, preferred_element_type=F32)
    column_sums = column_sums[0].reshape(groups, 1, my_cols)
    riding = groups > 1 and chunk_rows <= my_cols

    text = lax.dynamic_slice_in_dim(text_kv[:, 0], z_index * my_cols, my_cols, 2)
    text_keys = text[0].reshape(-1, heads, HD).astype(F32)
    text_keys = (text_keys * head_scale(text_keys)).astype(BF)
    text_values = text[1].reshape(-1, heads, HD)
    text_index = jnp.arange(text_kv.shape[2], dtype=jnp.int32)
    text_tenant = text_index // TEXT
    slots = text_tenant[:, None] == jnp.arange(TENANTS, dtype=jnp.int32)[None, :]
    live_length = jnp.sum(jnp.where(slots, text_lengths[0][None, :], 0), axis=1)
    live = text_index % TEXT < live_length

    states, cross_mixed = [], []
    for i, block_mixed in zip(spans, mixed):
        shifted = (sliced[i] - facts[i, 0:1]) + both_columns(project_out(block_mixed, wide_out))
        states.append(shifted)
        sums = jnp.stack([jnp.sum(shifted, axis=1), jnp.sum(shifted * shifted, axis=1)])
        crossed = jnp.dot(shifted.astype(BF), wide_cross, preferred_element_type=F32).astype(BF)
        crossed = to_groups(crossed, my_cols)
        if riding:
            sums = jnp.concatenate(three_terms(sums))
            sums = jnp.pad(sums, ((0, 0), (0, my_cols - chunk_rows)))
            sums = jnp.broadcast_to(sums[None], (groups,) + sums.shape)
            below = jnp.concatenate([sums] + three_terms(column_sums), axis=1)
            below = jnp.pad(below, ((0, 0), (0, 16 - below.shape[1]), (0, 0)))
            arrived = sum_at_owner(jnp.concatenate([crossed, below], axis=1))
            crossed, below = arrived[:chunk_rows], arrived[chunk_rows:]
            sums = (below[0:2] + below[2:4] + below[4:6])[:, :chunk_rows]
            all_columns = below[6:7] + below[7:8] + below[8:9]
        else:
            sums = sum_at_owner(jnp.broadcast_to(sums[None], (groups,) + sums.shape))
            all_columns = sum_at_owner(column_sums)
            crossed = sum_at_owner(crossed)
        sums = sums / width
        variance = jnp.maximum(sums[1] - sums[0] * sums[0], 0.0)[:, None, None]
        shaped = (crossed - sums[0][:, None] * all_columns).reshape(chunk_rows, heads, HD)
        square = jnp.mean(shaped * shaped, axis=-1, keepdims=True)
        cross_queries = (shaped * lax.rsqrt(square + EPS * (variance + EPS))).astype(BF)
        allowed = (my_tenant[i][:, None] == text_tenant[None, :]) & live[None]
        cross_mixed.append(attend(cross_queries, text_keys, text_values, allowed))

    channels = w_head.shape[1]
    head_rows = lax.dynamic_index_in_dim(
        w_head.reshape(halves, groups, parts * block, channels), z_index, 1, keepdims=False
    ).reshape(-1, channels)
    totals = jnp.sum(w_head.astype(F32), axis=0)[None]
    out_width = width // columns

    leaving, sums = [], []
    for i, shifted, block_mixed in zip(spans, states, cross_mixed):
        shifted = shifted + both_columns(project_out(block_mixed, wide_cross_out))
        final = (shifted + facts[i, 0:1]).astype(BF)
        if groups > 1 and columns == halves:
            span = slice_width // halves
            final = lax.dynamic_slice_in_dim(final, wt_index * span, span, 1)
        leaving.append(final.reshape(groups, part, -1))
        some = jnp.concatenate(
            [
                jnp.dot(shifted.astype(BF), head_rows, preferred_element_type=F32),
                jnp.sum(shifted, axis=1, keepdims=True),
                jnp.sum(shifted * shifted, axis=1, keepdims=True),
            ],
            axis=1,
        )
        sums.append(some.reshape(groups, part, channels + 2))
    sums = sum_at_owner(jnp.concatenate(sums, axis=1))
    mean = sums[:, channels : channels + 1] / width
    variance = jnp.maximum(sums[:, channels + 1 :] / width - mean * mean, 0.0)
    velocity = (sums[:, :channels] - mean * totals) * lax.rsqrt(variance + EPS)

    leaving = jnp.concatenate(leaving, axis=1)
    if groups == 1:
        hidden_out = lax.dynamic_slice_in_dim(leaving[0], wt_index * out_width, out_width, 1)
    else:
        leaving = jnp.swapaxes(lax.all_to_all(leaving, "z", 0, 0), 0, 1)
        if columns == halves:
            hidden_out = leaving.reshape(tok, out_width)
        else:
            leaving = jnp.swapaxes(leaving.reshape(tok, groups, halves, -1), 1, 2)
            hidden_out = lax.dynamic_slice_in_dim(
                leaving.reshape(tok, width), wt_index * out_width, out_width, 1
            )

    channel_half = latent.shape[1]
    outgoing = lax.dynamic_slice_in_dim(velocity, (1 - half_index) * channel_half, channel_half, 1)
    partner = flip(outgoing, "cfg")
    own_part = lax.dynamic_slice_in_dim(velocity, half_index * channel_half, channel_half, 1)
    conditional = jnp.where(half_index == 0, own_part, partner)
    null_text = jnp.where(half_index == 0, partner, own_part)
    latent_next = latent + step_size[0] * (null_text + guidance[0] * (conditional - null_text))
    return (hidden_out[None], latent_next)


def solution(mesh):
    halves, seq, columns = (mesh.shape[a] for a in ("cfg", "seq", "wt"))

    def run(*args):
        heads_here = args[6].shape[1] // columns // HD
        groups = math.gcd(heads_here, seq)
        fine = Mesh(
            mesh.devices.reshape(halves, groups, seq // groups, columns), ("cfg", "z", "t", "wt")
        )
        seq_axes = ("z", "t")
        weight = P(("cfg", "z", "t"), "wt")
        return jax.shard_map(
            on_device,
            mesh=fine,
            in_specs=(
                P("cfg", seq_axes, None),
                P(seq_axes, "cfg"),
                P(),
                P(seq_axes, None),
                P(None, "cfg", None, "wt"),
                P("cfg", None),
                weight,
                weight,
                weight,
                weight,
                weight,
                weight,
                P(),
                P(),
                P(),
            ),
            out_specs=(P("cfg", seq_axes, "wt"), P(seq_axes, "cfg")),
            check_vma=False,
        )(*args)

    return run
```

```python
import math

import jax
import jax.numpy as jnp
import numpy as np
from jax import lax
from jax.experimental import pallas as pl
from jax.experimental.pallas import tpu as pltpu
from jax.sharding import Mesh
from jax.sharding import PartitionSpec as P

HD = 128
TEXT = 512
TENANTS = 4
EPS = 1e-06
CHUNKS = 2
BF = jnp.bfloat16
F32 = jnp.float32


def flip(block, axis):
    return lax.ppermute(block, axis, [(0, 1), (1, 0)])


def rotary_tables():
    sixth = HD // 6
    table = np.zeros((3, HD), np.float32)
    lane = 0
    for column, span in enumerate((HD - 4 * sixth, 2 * sixth, 2 * sixth)):
        exponent = np.arange(0, span, 2).astype(np.float32) / np.float32(span)
        frequency = (1.0 / 10000.0**exponent).astype(np.float32)
        table[column, lane : lane + span] = np.repeat(frequency, 2)
        lane += span
    swap = np.zeros((HD, HD), np.float32)
    for pair in range(0, HD, 2):
        swap[pair + 1, pair] = -1.0
        swap[pair, pair + 1] = 1.0
    return table, swap


def running_ends(lengths):
    upto = np.tril(np.ones((TENANTS, TENANTS), np.int32))
    return jnp.sum(jnp.asarray(upto) * lengths[None, :], axis=1)


def head_scale(shaped):
    return lax.rsqrt(jnp.mean(shaped * shaped, axis=-1, keepdims=True) + EPS)


def attend(queries, keys, values, allowed):
    scores = jnp.einsum("qhd,khd->hqk", queries, keys, preferred_element_type=F32)
    scores = scores * (1.0 / math.sqrt(queries.shape[-1]))
    weights = jnp.where(allowed[None], jnp.exp(scores), 0.0).astype(BF)
    summed = jnp.einsum("hqk,khd->qhd", weights, values, preferred_element_type=F32)
    totals = jnp.sum(weights.astype(F32), axis=2).T
    return (summed / totals[..., None]).astype(BF).reshape(queries.shape[0], -1)


MESH = pl.DeviceIdType.MESH
NEAR = (1, 3, 2)
LINE = 4


def remote(src, dst, sent, got, device):
    return pltpu.make_async_remote_copy(
        src_ref=src, dst_ref=dst, send_sem=sent, recv_sem=got, device_id=device, device_id_type=MESH
    )


def meet(devices):
    barrier = pltpu.get_barrier_semaphore()
    for device in devices:
        pl.semaphore_signal(barrier, inc=1, device_id=device, device_id_type=MESH)
    pl.semaphore_wait(barrier, len(devices))


def span(index, size):
    return pl.ds(pl.multiple_of(index * size, size), size)


def nt_dot(a, b):
    return lax.dot_general(a, b, (((1,), (1,)), ((), ())), preferred_element_type=F32)


def tenants_at(index, lengths):
    found, end = jnp.zeros(index.shape, jnp.int32), 0
    for tenant in range(TENANTS):
        end = end + lengths[tenant]
        found = found + (index >= end).astype(jnp.int32)
    return found


def self_attention_kernel(
    lengths, pos, table, key_index, hid, wk, wv, wq, w_out, mixed_out, raw_out, mean_out, out_wide,
    wide, rows, normed, pairs, queries, pos_all, rot,
    loc_w, loc_h, raw_sem, zs, zr, hs, hr, ps, pr, xs, xr, cs, cr, ys, yr, ks, kr, us, ur,
):
    c, z, x, y = (lax.axis_index(a) for a in ("cfg", "z", "t", "wt"))
    groups = LINE
    tok = hid.shape[0]
    depth = wk.shape[0]
    wid = rows.shape[2]
    cols = wide.shape[3]
    heads = cols // HD
    at_z = [{"z": lax.rem(z + d, groups)} for d in range(groups)]
    from_z = [lax.rem(z + groups - d, groups) for d in range(groups)]
    at_x, at_c, at_y = {"t": 1 - x}, {"cfg": 1 - c}, {"wt": 1 - y}
    weights = (wk, wv, wq)
    mine = c * groups + z

    own_rows = [
        pltpu.make_async_copy(hid.at[:, kb * wid : (kb + 1) * wid], rows.at[kb, span(z, tok)], loc_h.at[kb])
        for kb in range(2 * groups)
    ]
    own_weights = [
        pltpu.make_async_copy(w.at[:, span(z, cols)], wide.at[j, mine, span(x, depth)], loc_w.at[j])
        for j, w in enumerate(weights)
    ]
    own_pos = pltpu.make_async_copy(pos, pos_all.at[z], loc_w.at[3])
    for copy in own_rows + [own_pos] + own_weights:
        copy.start()
    meet([at_z[1], at_z[2], at_z[3], at_x, at_c, at_y])

    def block(j, d, column):
        return wide.at[j, c * groups + from_z[d], span(column, depth)]

    def x_copy(j, d):
        return remote(block(j, d, x), block(j, d, x), xs.at[d, j], xr.at[d, j], at_x)

    def x_arrival(j, d):
        return remote(block(j, d, 1 - x), block(j, d, 1 - x), xs.at[d, j], xr.at[d, j], at_x)

    def c_copy(j, d, second):
        part = block(j, d, 1 - x if second else x)
        return remote(part, part, cs.at[second, d, j], cr.at[second, d, j], at_c)

    def c_arrival(j, d, second):
        part = wide.at[j, (1 - c) * groups + from_z[d], span(1 - x if second else x, depth)]
        return remote(part, part, cs.at[second, d, j], cr.at[second, d, j], at_c)

    def z_copy(j, d):
        target = lax.rem(z + d, groups)
        return remote(
            weights[j].at[:, span(target, cols)], wide.at[j, mine, span(x, depth)], zs.at[d - 1, j], zr.at[d - 1, j], at_z[d]
        )

    def z_arrival(j, d):
        return remote(block(j, d, x), block(j, d, x), zs.at[d - 1, j], zr.at[d - 1, j], at_z[d])

    def rows_of(b, column, piece):
        return rows.at[column * groups + piece, span(b, tok)]

    def by_z(*choices):
        return jnp.where(z == 0, choices[0], jnp.where(z == 1, choices[1], jnp.where(z == 2, choices[2], choices[3])))

    inner = jnp.logical_and(z > 0, z < groups - 1)
    way_of = [None, by_z(1, 0, 1, 0), by_z(1, 1, 0, 0), by_z(1, 1, 0, 0)]
    step_of = [None, by_z(0, 0, 0, 0), by_z(1, 0, 0, 1), by_z(2, 1, 1, 2)]
    block_of = [z, by_z(1, 0, 3, 2), by_z(2, 2, 1, 1), by_z(3, 3, 0, 0)]

    def out_part(core, column):
        return out_wide.at[core, span(column, depth)]

    own_out = pltpu.make_async_copy(w_out, out_part(c, x), loc_w.at[4])
    own_out.start()
    out_x = remote(w_out, out_part(c, x), us.at[0], ur.at[0], at_x)
    out_c = remote(w_out, out_part(c, x), us.at[1], ur.at[1], at_c)
    out_on = remote(out_part(c, 1 - x), out_part(c, 1 - x), us.at[2], ur.at[2], at_c)

    def h_own(way, p):
        part = rows_of(z, y, p)
        return remote(part, part, hs.at[way, 0, p], hr.at[way, 0, p], {"z": z + 1 - 2 * way})

    def h_arrival(e, p):
        part = rows_of(block_of[e], y, p)
        return remote(part, part, hs.at[way_of[e], step_of[e], p], hr.at[way_of[e], step_of[e], p], at_y)

    def h_onward(e, p):
        part = rows_of(block_of[e], y, p)
        at = step_of[e] + 1
        return remote(part, part, hs.at[way_of[e], at, p], hr.at[way_of[e], at, p], {"z": z + 1 - 2 * way_of[e]})

    def y_copy(e, p):
        part = rows_of(block_of[e], y, p)
        return remote(part, part, ys.at[e - 1, p], yr.at[e - 1, p], at_y)

    def y_arrival(e, p):
        part = rows_of(block_of[e], 1 - y, p)
        return remote(part, part, ys.at[e - 1, p], yr.at[e - 1, p], at_y)

    def up(p):
        @pl.when(z < groups - 1)
        def _():
            h_own(0, p).start()

        @pl.when(z > 0)
        def _():
            h_own(1, p).start()

    def arrive(e):
        for p in range(groups):
            h_arrival(e, p).wait_recv()

            @pl.when(inner)
            def _():
                h_onward(e, p).start()

            y_copy(e, p).start()

    def p_copy(d):
        return remote(pos_all.at[z], pos_all.at[z], ps.at[d - 1], pr.at[d - 1], at_z[d])

    def p_arrival(d):
        part = pos_all.at[from_z[d]]
        return remote(part, part, ps.at[d - 1], pr.at[d - 1], at_z[d])

    some = 16
    width = 2 * groups * wid

    def norm_block(b):
        def norm(i, carry):
            these = pl.ds(pl.multiple_of(b * tok + i * some, some), some)
            total = jnp.zeros((some, wid), F32)
            for kb in range(2 * groups):
                total += rows[kb, these].astype(F32)
            mean = jnp.sum(total, axis=1, keepdims=True) / width
            total = jnp.zeros((some, wid), F32)
            for kb in range(2 * groups):
                centred = rows[kb, these].astype(F32) - mean
                total += centred * centred
            scale = lax.rsqrt(jnp.sum(total, axis=1, keepdims=True) / width + EPS)
            for kb in range(2 * groups):
                normed[kb, these] = ((rows[kb, these].astype(F32) - mean) * scale).astype(BF)
            mean_out[these] = mean
            return carry

        lax.fori_loop(0, tok // some, norm, 0)

    for copy in own_rows + [own_pos]:
        copy.wait()
    for d in NEAR:
        p_copy(d).start()
    for d in NEAR:
        z_copy(0, d).start()
    for j in range(3):
        own_weights[j].wait()
        x_copy(j, 0).start()
        c_copy(j, 0, 0).start()
    norm_block(z)

    def relay(j, d):
        z_arrival(j, d).wait_recv()
        x_copy(j, d).start()
        c_copy(j, d, 0).start()

    def second_relay(j, d):
        x_arrival(j, d).wait_recv()
        c_copy(j, d, 1).start()

    for j in range(3):
        second_relay(j, 0)
    relay(0, 1)
    for d in NEAR:
        z_copy(1, d).start()
    relay(0, 3)
    relay(0, 2)
    for p in range(groups):
        up(p)
    for d in NEAR:
        second_relay(0, d)
    relay(1, 1)
    relay(1, 3)
    relay(1, 2)
    for d in NEAR:
        second_relay(1, d)
    out_x.start()
    out_c.start()
    arrive(1)

    @pl.when(inner)
    def _():
        arrive(2)

    for d in NEAR:
        p_arrival(d).wait_recv()
    lane = lax.broadcasted_iota(jnp.int32, (tok, HD), 1)
    even = lax.rem(lane, 2) == 0
    for m in range(groups):
        held = pos_all[m]
        full = jnp.concatenate([held, jnp.zeros((HD - held.shape[0], held.shape[1]), F32)], axis=0)
        column = jnp.transpose(full)[:tok]
        angles = sum(column[:, a : a + 1] * table[a : a + 1, :] for a in range(3))
        rot[0, m * tok : (m + 1) * tok] = jnp.cos(angles)
        sinus = jnp.sin(angles)
        rot[1, m * tok : (m + 1) * tok] = jnp.where(even, -sinus, sinus)

    def rotated(these, total):
        turned = []
        for h in range(heads):
            part = total[:, h * HD : (h + 1) * HD]
            scale = lax.rsqrt(jnp.mean(part * part, axis=1, keepdims=True) + EPS)
            swapped = jnp.where(even, pltpu.roll(part, HD - 1, 1), pltpu.roll(part, 1, 1))
            turned.append((part * rot[0, these] + swapped * rot[1, these]) * scale)
        return jnp.concatenate(turned, axis=1).astype(BF)

    def pair_copy(e):
        part = pairs.at[x, :, span(block_of[e], tok)]
        return remote(part, part, ks.at[e], kr.at[e], at_x)

    def pair_arrival(e):
        part = pairs.at[1 - x, :, span(block_of[e], tok)]
        return remote(part, part, ks.at[e], kr.at[e], at_x)

    def project(e, j):
        these = span(block_of[e] if j < 2 else e, tok)
        total = jnp.dot(normed[0, these], wide[j, 0], preferred_element_type=F32)
        for kb in range(1, 2 * groups):
            total += jnp.dot(normed[kb, these], wide[j, kb], preferred_element_type=F32)
        if j == 0:
            pairs[x, 0, these] = rotated(these, total)
        elif j == 1:
            pairs[x, 1, these] = total.astype(BF)
            pair_copy(e).start()
        else:
            queries[these] = rotated(these, total)

    def all_here(j):
        for d in range(groups):
            c_arrival(j, d, 0).wait_recv()
            c_arrival(j, d, 1).wait_recv()

    def finish(e):
        for p in range(groups):
            y_arrival(e, p).wait_recv()
        norm_block(block_of[e])
        project(e, 0)
        project(e, 1)

    all_here(0)
    all_here(1)
    project(0, 0)
    project(0, 1)

    @pl.when(inner)
    def _():
        arrive(3)

    @pl.when(jnp.logical_not(inner))
    def _():
        arrive(2)

    for d in NEAR:
        z_copy(2, d).start()
    out_here = remote(out_part(c, 1 - x), out_part(c, 1 - x), us.at[0], ur.at[0], at_x)
    out_here.wait_recv()
    out_on.start()
    finish(1)

    @pl.when(jnp.logical_not(inner))
    def _():
        arrive(3)

    relay(2, 1)
    relay(2, 3)
    raws = [
        pltpu.make_async_copy(rows.at[half * groups + z], raw_out.at[half], raw_sem.at[half]) for half in (0, 1)
    ]
    finish(2)
    relay(2, 2)
    for d in NEAR:
        second_relay(2, d)
    finish(3)
    for copy in raws:
        copy.start()
    all_here(2)

    def ask(m, carry):
        project(m, 2)
        return carry

    lax.fori_loop(0, groups, ask, 0)
    for e in range(groups):
        pair_arrival(e).wait_recv()

    key_tenant = tenants_at(key_index[0:1], lengths)
    ones = jnp.ones((groups * tok, HD), BF)

    def attend_block(m, carry):
        these = span(m, tok)
        index = lax.broadcasted_iota(jnp.int32, (tok, 1), 0) + (m * 2 + x) * tok
        allowed = tenants_at(index, lengths) == key_tenant
        for h in range(heads):
            lanes = slice(h * HD, (h + 1) * HD)
            summed = jnp.zeros((tok, 2 * HD), F32)
            for part in (0, 1):
                scores = nt_dot(queries[these, lanes], pairs[part, 0, :, lanes]) * (1.0 / math.sqrt(HD))
                here = allowed[:, part * groups * tok : (part + 1) * groups * tok]
                chances = jnp.where(here, jnp.exp(scores), 0.0).astype(BF)
                both = jnp.concatenate([pairs[part, 1, :, lanes], ones], axis=1)
                summed += jnp.dot(chances, both, preferred_element_type=F32)
            mixed_out[these, lanes] = (summed[:, :HD] / summed[:, HD:]).astype(BF)
        return carry

    lax.fori_loop(0, groups, attend_block, 0)

    for copy in raws:
        copy.wait()
    for p in range(groups):
        @pl.when(z < groups - 1)
        def _():
            h_own(0, p).wait_send()

        @pl.when(z > 0)
        def _():
            h_own(1, p).wait_send()

        for e in (1, 2, 3):
            @pl.when(inner)
            def _():
                h_onward(e, p).wait_send()

            y_copy(e, p).wait_send()
    for d in NEAR:
        p_copy(d).wait_send()
        for j in range(3):
            z_copy(j, d).wait_send()
    for d in range(groups):
        for j in range(3):
            x_copy(j, d).wait_send()
            c_copy(j, d, 0).wait_send()
            c_copy(j, d, 1).wait_send()
    for e in range(groups):
        pair_copy(e).wait_send()
    own_out.wait()
    out_x.wait_send()
    for index, part in ((1, out_part(1 - c, x)), (2, out_part(1 - c, 1 - x))):
        remote(part, part, us.at[index], ur.at[index], at_c).wait()


def self_attention_call(lengths, hidden, positions, wk, wv, wq, w_out):
    tok, width = hidden.shape
    groups = LINE
    depth, local_cols = wk.shape
    cols = local_cols // groups
    rows = groups * tok
    wid = width // (2 * groups)
    anywhere = pl.BlockSpec(memory_space=pl.ANY)
    vmem = pl.BlockSpec(memory_space=pltpu.VMEM)
    smem = pl.BlockSpec(memory_space=pltpu.SMEM)
    dma = pltpu.SemaphoreType.DMA
    made = [
        jax.ShapeDtypeStruct((rows, cols), BF),
        jax.ShapeDtypeStruct((2, rows, wid), BF),
        jax.ShapeDtypeStruct((rows, 1), F32),
        jax.ShapeDtypeStruct((2, 2 * depth, local_cols), BF),
    ]
    table = np.zeros((8, HD), np.float32)
    table[:3] = rotary_tables()[0]
    place = np.arange(2 * rows)
    place = (place % rows // tok * 2 + place // rows) * tok + place % tok
    place = np.broadcast_to(place.astype(np.int32), (8, 2 * rows))
    pos = jnp.pad(positions.T.astype(F32), ((0, 5), (0, -tok % 128)))
    return pl.pallas_call(
        self_attention_kernel,
        out_shape=made,
        in_specs=[smem, vmem, vmem, vmem] + [anywhere] * 5,
        out_specs=[vmem] * 3 + [anywhere],
        scratch_shapes=[
            pltpu.VMEM((3, 2 * groups, 2 * depth, cols), BF),
            pltpu.VMEM((2 * groups, rows, wid), BF),
            pltpu.VMEM((2 * groups, rows, wid), BF),
            pltpu.VMEM((2, 2, rows, cols), BF),
            pltpu.VMEM((rows, cols), BF),
            pltpu.VMEM((groups,) + pos.shape, F32),
            pltpu.VMEM((2, rows, HD), F32),
            dma((5,)), dma((2 * groups,)), dma((2,)),
            dma((3, 3)), dma((3, 3)),
            dma((2, 3, 4)), dma((2, 3, 4)),
            dma((3,)), dma((3,)),
            dma((4, 3)), dma((4, 3)),
            dma((2, 4, 3)), dma((2, 4, 3)),
            dma((3, 4)), dma((3, 4)),
            dma((4,)), dma((4,)), dma((3,)), dma((3,)),
        ],
        compiler_params=pltpu.CompilerParams(
            collective_id=0, has_side_effects=True, vmem_limit_bytes=56 * 2**20
        ),
        cost_estimate=pl.CostEstimate(
            flops=6 * rows * width * cols, bytes_accessed=20 * 2**20, transcendentals=0
        ),
    )(lengths, pos, jnp.asarray(table), jnp.asarray(place), hidden, wk, wv, wq, w_out)


def line_places(z):
    def block(way, s):
        return z - s if way == 0 else z + s

    def sends(way, s):
        if way == 0:
            return jnp.logical_and(z - s >= 0, z + 1 < LINE)
        return jnp.logical_and(z + s < LINE, z >= 1)

    def gets(way, s):
        return z - 1 - s >= 0 if way == 0 else z + 1 + s < LINE

    return block, sends, gets


def pack_columns(first, second):
    tok = first.shape[0]
    lane = lax.broadcasted_iota(jnp.int32, (tok, HD), 1)
    both = jnp.where(lane == 0, first, jnp.where(lane == 1, second, 0.0))
    both = jnp.concatenate([both, jnp.zeros((-tok % HD, HD), F32)], axis=0)
    return jnp.transpose(both)[:8]


def unpack_columns(packed, tok):
    full = jnp.concatenate([packed, jnp.zeros((HD - packed.shape[0], packed.shape[1]), F32)], axis=0)
    column = jnp.transpose(full)[:tok]
    return column[:, 0:1], column[:, 1:2]


def cross_attention_kernel(
    lengths, text_lengths, guidance, step_size, mixed, raw, mean, head, latent, text_kv, w_out, w_cross, w_last,
    hidden_out, latent_out,
    wide, text, gath, own, left, right, left2, right2, kept, state, asked, answers, facts, facts_in, cols_out, cols_in,
    leaving, vel, vel_in, half_out, half_in, core_out, core_in,
    loc_w, loc_t, loc_g, loc_f, ws, wr, wcs, wcr, gs, gr, ys, yr, y2s, y2r, qs, qr, fs, fr, ss, sr, os_, or_, vs, vr, es, er,
):
    c, z, x, y = (lax.axis_index(a) for a in ("cfg", "z", "t", "wt"))
    groups = LINE
    rows, cols = mixed.shape
    tok = rows // groups
    depth = w_last.shape[0]
    wid = raw.shape[2]
    width = 2 * groups * wid
    heads = cols // HD
    channels = head.shape[0]
    slots = text.shape[1] // TENANTS
    at_z = [{"z": lax.rem(z + d, groups)} for d in range(groups)]
    from_z = [lax.rem(z + groups - d, groups) for d in range(groups)]
    at_x, at_c, at_y = {"t": 1 - x}, {"cfg": 1 - c}, {"wt": 1 - y}
    at_line = ({"z": jnp.minimum(z + 1, groups - 1)}, {"z": jnp.maximum(z - 1, 0)})
    line_block, line_sends, line_gets = line_places(z)
    own_weights = [pltpu.make_async_copy(w_out, wide.at[0], loc_w.at[0])]
    own_weights += [
        pltpu.make_async_copy(w, wide.at[j, c, span(x, depth)], loc_w.at[j]) for j, w in ((1, w_cross), (2, w_last))
    ]
    own_text = [pltpu.make_async_copy(text_kv.at[k, 0, :, span(z, cols)], text.at[k], loc_t.at[k]) for k in (0, 1)]
    for copy in own_weights + own_text:
        copy.start()
    own[0] = mixed[...].reshape(groups, tok, cols)
    meet([at_z[1], at_z[2], at_z[3], at_x, at_c, at_y])

    def g_local(f, i):
        return pltpu.make_async_copy(own.at[f, i], gath.at[f, i, :, span(z, cols)], loc_g.at[f, i])

    def g_copy(f, i, way, s):
        part = gath.at[f, i, :, span(line_block(way, s), cols)]
        return remote(own.at[f, i] if s == 0 else part, part, gs.at[f, i, way, s], gr.at[f, i, way, s], at_line[way])

    def g_arrival(f, i, way, s):
        part = gath.at[f, i, :, span(line_block(way, s + 1), cols)]
        return remote(part, part, gs.at[f, i, way, s], gr.at[f, i, way, s], at_line[way])

    def g_start(f, i):
        for way in (0, 1):
            @pl.when(line_sends(way, 0))
            def _():
                g_copy(f, i, way, 0).start()
        g_local(f, i).start()

    def g_step(f, i, s):
        for way in (0, 1):
            @pl.when(line_gets(way, s))
            def _():
                g_arrival(f, i, way, s).wait_recv()
                if s + 1 < groups - 1:
                    @pl.when(line_sends(way, s + 1))
                    def _():
                        g_copy(f, i, way, s + 1).start()
        if s == groups - 2:
            g_local(f, i).wait()

    def w_part(j, core, column):
        return wide.at[j, core, span(column, depth)]

    def w_copy(j):
        return remote(w_part(j, c, x), w_part(j, c, x), ws.at[j], wr.at[j], at_x)

    def w_arrival(j):
        return remote(w_part(j, c, 1 - x), w_part(j, c, 1 - x), ws.at[j], wr.at[j], at_x)

    def wc_copy(j, second):
        part = w_part(j, c, 1 - x if second else x)
        return remote(part, part, wcs.at[j, second], wcr.at[j, second], at_c)

    def wc_arrival(j, second):
        part = w_part(j, 1 - c, 1 - x if second else x)
        return remote(part, part, wcs.at[j, second], wcr.at[j, second], at_c)

    def w_relay(j):
        w_arrival(j).wait_recv()
        wc_copy(j, 1).start()

    def w_ready(j):
        wc_arrival(j, 0).wait_recv()
        wc_arrival(j, 1).wait_recv()

    turn = (0, 3, 1, 2)
    for i in turn:
        g_start(0, i)
    for j in (1, 2):
        own_weights[j].wait()
        w_copy(j).start()
        wc_copy(j, 0).start()

    for copy in own_text:
        copy.wait()

    def norm_text(i, carry):
        these = span(i, HD)
        for h in range(heads):
            lanes = slice(h * HD, (h + 1) * HD)
            part = text[0, these, lanes].astype(F32)
            scale = lax.rsqrt(jnp.mean(part * part, axis=1, keepdims=True) + EPS)
            text[0, these, lanes] = (part * scale).astype(BF)
        return carry

    lax.fori_loop(0, text.shape[1] // HD, norm_text, 0)
    totals = nt_dot(jnp.ones((16, width), BF), head[...])[0:1]

    def y_copy(i):
        return remote(left.at[i], right.at[i], ys.at[i], yr.at[i], at_y)

    def y2_copy(i):
        return remote(left2.at[i], right2.at[i], y2s.at[i], y2r.at[i], at_y)

    def q_copy(i, d):
        return remote(asked.at[i, lax.rem(z + d, groups)], answers.at[i, z], qs.at[i, d - 1], qr.at[i, d - 1], at_z[d])

    def q_arrival(i, d):
        part = answers.at[i, from_z[d]]
        return remote(part, part, qs.at[i, d - 1], qr.at[i, d - 1], at_z[d])

    def f_copy(i, d):
        return remote(facts.at[i], facts_in.at[i, z], fs.at[i, d - 1], fr.at[i, d - 1], at_z[d])

    def f_arrival(i, d):
        part = facts_in.at[i, from_z[d]]
        return remote(part, part, fs.at[i, d - 1], fr.at[i, d - 1], at_z[d])

    def s_copy(d):
        return remote(cols_out.at[lax.rem(z + d, groups)], cols_in.at[z], ss.at[d - 1], sr.at[d - 1], at_z[d])

    def s_arrival(d):
        part = cols_in.at[from_z[d]]
        return remote(part, part, ss.at[d - 1], sr.at[d - 1], at_z[d])

    def project_out(i):
        for half in (0, 1):
            left[i, :, half * wid : (half + 1) * wid] = nt_dot(gath[0, i], wide[0, half]).astype(BF)
        y_copy(i).start()

    def sum_columns():
        ones = jnp.ones((16, wid), BF)
        for g in range(groups):
            lanes = slice(g * cols, (g + 1) * cols)
            total = jnp.dot(ones, wide[1, 0, :, lanes], preferred_element_type=F32)
            total += jnp.dot(ones, wide[1, 1, :, lanes], preferred_element_type=F32)
            cols_out[g] = total[:8]
        for d in NEAR:
            s_copy(d).start()

    def update(i):
        y_copy(i).wait_recv()
        these = slice(i * tok, (i + 1) * tok)
        shift = mean[these]
        first = second = jnp.zeros((tok, 1), F32)
        for half in (0, 1):
            lanes = slice(half * wid, (half + 1) * wid)
            both = left[i, :, lanes].astype(F32) + right[i, :, lanes].astype(F32)
            new = (raw[half, these].astype(F32) - shift) + both
            state[i, half] = new
            first += jnp.sum(new, axis=1, keepdims=True)
            second += jnp.sum(new * new, axis=1, keepdims=True)
        facts[i] = pack_columns(first, second)
        for d in NEAR:
            f_copy(i, d).start()
        for g in range(groups):
            lanes = slice(g * cols, (g + 1) * cols)
            part = jnp.dot(state[i, 0].astype(BF), wide[1, 0, :, lanes], preferred_element_type=F32)
            part += jnp.dot(state[i, 1].astype(BF), wide[1, 1, :, lanes], preferred_element_type=F32)
            asked[i, g] = part.astype(BF)
        for d in NEAR:
            q_copy(i, d).start()

    def cross(i):
        packed = facts[i]
        crossed = asked[i, z].astype(F32)
        column_sums = cols_out[z, 0:1]
        for d in NEAR:
            q_arrival(i, d).wait_recv()
            f_arrival(i, d).wait_recv()
            if i == turn[0]:
                s_arrival(d).wait_recv()
            packed = packed + facts_in[i, from_z[d]]
            crossed = crossed + answers[i, from_z[d]].astype(F32)
            column_sums = column_sums + cols_in[from_z[d], 0:1]
        first, second = unpack_columns(packed, tok)
        average = first / width
        variance = jnp.maximum(second / width - average * average, 0.0)
        crossed = crossed - average * column_sums
        index = lax.broadcasted_iota(jnp.int32, (tok, 1), 0) + (i * 2 + x) * tok
        tenant = tenants_at(index, lengths)
        slot = lax.broadcasted_iota(jnp.int32, (1, slots), 1)
        ones = jnp.ones((slots, HD), BF)
        for h in range(heads):
            lanes = slice(h * HD, (h + 1) * HD)
            part = crossed[:, lanes]
            square = jnp.mean(part * part, axis=1, keepdims=True)
            query = (part * lax.rsqrt(square + EPS * (variance + EPS))).astype(BF)
            summed = jnp.zeros((tok, 2 * HD), F32)
            for t in range(TENANTS):
                these = slice(t * slots, (t + 1) * slots)
                scores = nt_dot(query, text[0, these, lanes]) * (1.0 / math.sqrt(HD))
                allowed = jnp.logical_and(tenant == t, slot < text_lengths[0, t])
                chances = jnp.where(allowed, jnp.exp(scores), 0.0).astype(BF)
                both = jnp.concatenate([text[1, these, lanes], ones], axis=1)
                summed += jnp.dot(chances, both, preferred_element_type=F32)
            own[1, i, :, lanes] = (summed[:, :HD] / summed[:, HD:]).astype(BF)
        g_start(1, i)

    def project_last(i):
        left2[i] = nt_dot(gath[1, i], wide[2, 1 - y]).astype(BF)
        y2_copy(i).start()
        kept[i] = nt_dot(gath[1, i], wide[2, y]).astype(BF)

    def o_remote(i):
        return remote(leaving.at[i], hidden_out.at[:, span(z, wid)], os_.at[i], or_.at[z], {"z": i})

    def o_local(i):
        return pltpu.make_async_copy(leaving.at[i], hidden_out.at[:, span(z, wid)], loc_f)

    def v_remote(i):
        return remote(vel.at[i], vel_in.at[z], vs.at[i], vr.at[z], {"z": i})

    def finish(i):
        y2_copy(i).wait_recv()
        these = slice(i * tok, (i + 1) * tok)
        final = state[i, y] + kept[i].astype(F32) + right2[i].astype(F32)
        leaving[i] = (final + mean[these]).astype(BF)

        @pl.when(z != i)
        def _():
            o_remote(i).start()

        @pl.when(z == i)
        def _():
            o_local(i).start()

        rows_here = pl.ds(pl.multiple_of((y * groups + z) * wid, wid), wid)
        some = nt_dot(final.astype(BF), head[:, rows_here])
        first = jnp.sum(final, axis=1, keepdims=True)
        second = jnp.sum(final * final, axis=1, keepdims=True)
        lane = lax.broadcasted_iota(jnp.int32, (tok, HD - channels), 1)
        tail = jnp.where(lane == 0, first, jnp.where(lane == 1, second, 0.0))
        vel[i] = jnp.concatenate([some, tail], axis=1)

        @pl.when(z != i)
        def _():
            v_remote(i).start()

    g_step(0, turn[0], 0)
    g_step(0, turn[1], 0)
    g_step(0, turn[0], 1)
    g_step(0, turn[2], 0)
    g_step(0, turn[1], 1)
    g_step(0, turn[0], 2)
    own_weights[0].wait()
    project_out(turn[0])
    g_step(0, turn[3], 0)
    g_step(0, turn[2], 1)
    g_step(0, turn[1], 2)
    project_out(turn[1])
    w_relay(1)
    g_step(0, turn[3], 1)
    g_step(0, turn[2], 2)
    project_out(turn[2])
    w_ready(1)
    sum_columns()
    update(turn[0])
    g_step(0, turn[3], 2)
    project_out(turn[3])
    update(turn[1])
    cross(turn[0])
    update(turn[2])
    w_relay(2)
    g_step(1, turn[0], 0)
    cross(turn[1])
    update(turn[3])
    g_step(1, turn[1], 0)
    g_step(1, turn[0], 1)
    cross(turn[2])
    g_step(1, turn[2], 0)
    g_step(1, turn[1], 1)
    g_step(1, turn[0], 2)
    w_ready(2)
    project_last(turn[0])
    cross(turn[3])
    g_step(1, turn[3], 0)
    g_step(1, turn[2], 1)
    g_step(1, turn[1], 2)
    project_last(turn[1])
    finish(turn[0])
    g_step(1, turn[3], 1)
    g_step(1, turn[2], 2)
    project_last(turn[2])
    finish(turn[1])
    g_step(1, turn[3], 2)
    project_last(turn[3])
    finish(turn[2])
    finish(turn[3])

    total = vel[z]
    for d in NEAR:
        part = vel_in.at[from_z[d]]
        remote(part, part, vs.at[d], vr.at[from_z[d]], at_z[d]).wait_recv()
        total = total + vel_in[from_z[d]]
    half_out[...] = total
    over_y = remote(half_out, half_in, es.at[0], er.at[0], at_y)
    over_y.start()
    over_y.wait()
    total = half_out[...] + half_in[...]
    average = total[:, channels : channels + 1] / width
    variance = jnp.maximum(total[:, channels + 1 : channels + 2] / width - average * average, 0.0)
    velocity = (total[:, :channels] - average * totals) * lax.rsqrt(variance + EPS)
    core_out[...] = jnp.concatenate([velocity, velocity], axis=1)
    over_c = remote(core_out, core_in, es.at[1], er.at[1], at_c)
    over_c.start()
    over_c.wait()
    span_out = latent.shape[0]
    turned = []
    for held in (core_out, core_in):
        full = jnp.concatenate([held[...], jnp.zeros((-tok % HD, HD), F32)], axis=0)
        both = jnp.transpose(full)[:, :tok]
        turned.append(jnp.where(c == 0, both[:span_out], both[span_out : 2 * span_out]))
    conditional = jnp.where(c == 0, turned[0], turned[1])
    null_text = jnp.where(c == 0, turned[1], turned[0])
    latent_out[...] = latent[...] + step_size[0] * (null_text + guidance[0] * (conditional - null_text))

    for d in NEAR:
        part = hidden_out.at[:, span(from_z[d], wid)]
        remote(part, part, os_.at[d], or_.at[from_z[d]], at_z[d]).wait_recv()
    for i in range(groups):
        @pl.when(z != i)
        def _():
            o_remote(i).wait_send()
            v_remote(i).wait_send()

        @pl.when(z == i)
        def _():
            o_local(i).wait()

        y_copy(i).wait_send()
        y2_copy(i).wait_send()
        for d in NEAR:
            q_copy(i, d).wait_send()
            f_copy(i, d).wait_send()
        for f in (0, 1):
            for way in (0, 1):
                for s in range(groups - 1):
                    @pl.when(line_sends(way, s))
                    def _():
                        g_copy(f, i, way, s).wait_send()
    for d in NEAR:
        s_copy(d).wait_send()
    for j in (1, 2):
        w_copy(j).wait_send()
        wc_copy(j, 0).wait_send()
        wc_copy(j, 1).wait_send()


def cross_attention_call(
    lengths, text_lengths, guidance, step_size, mixed, raw, mean, head, latent, text_kv, w_out, w_cross, w_last
):
    groups = LINE
    rows, cols = mixed.shape
    tok = rows // groups
    wid = raw.shape[2]
    depth, local_cols = w_last.shape
    padded = tok + -tok % HD
    anywhere = pl.BlockSpec(memory_space=pl.ANY)
    vmem = pl.BlockSpec(memory_space=pltpu.VMEM)
    smem = pl.BlockSpec(memory_space=pltpu.SMEM)
    dma = pltpu.SemaphoreType.DMA
    return pl.pallas_call(
        cross_attention_kernel,
        out_shape=[
            jax.ShapeDtypeStruct((tok, groups * wid), BF),
            jax.ShapeDtypeStruct(latent.shape, F32),
        ],
        in_specs=[smem] * 4 + [vmem] * 5 + [anywhere] * 4,
        out_specs=[anywhere, vmem],
        scratch_shapes=[
            pltpu.VMEM((3, 2, 2 * depth, local_cols), BF),
            pltpu.VMEM((2, text_kv.shape[2], cols), BF),
            pltpu.VMEM((2, groups, tok, local_cols), BF),
            pltpu.VMEM((2, groups, tok, cols), BF),
            pltpu.VMEM((groups, tok, 2 * wid), BF),
            pltpu.VMEM((groups, tok, 2 * wid), BF),
            pltpu.VMEM((groups, tok, wid), BF),
            pltpu.VMEM((groups, tok, wid), BF),
            pltpu.VMEM((groups, tok, wid), BF),
            pltpu.VMEM((groups, 2, tok, wid), F32),
            pltpu.VMEM((groups, groups, tok, cols), BF),
            pltpu.VMEM((groups, groups, tok, cols), BF),
            pltpu.VMEM((groups, 8, padded), F32),
            pltpu.VMEM((groups, groups, 8, padded), F32),
            pltpu.VMEM((groups, 8, cols), F32),
            pltpu.VMEM((groups, 8, cols), F32),
            pltpu.VMEM((groups, tok, wid), BF),
            pltpu.VMEM((groups, tok, HD), F32),
            pltpu.VMEM((groups, tok, HD), F32),
            pltpu.VMEM((tok, HD), F32),
            pltpu.VMEM((tok, HD), F32),
            pltpu.VMEM((tok, HD), F32),
            pltpu.VMEM((tok, HD), F32),
            dma((3,)), dma((2,)), dma((2, groups)), dma,
            dma((3,)), dma((3,)), dma((3, 2)), dma((3, 2)),
            dma((2, groups, 2, 3)), dma((2, groups, 2, 3)),
            dma((groups,)), dma((groups,)), dma((groups,)), dma((groups,)),
            dma((groups, 3)), dma((groups, 3)), dma((groups, 3)), dma((groups, 3)),
            dma((3,)), dma((3,)),
            dma((groups,)), dma((groups,)), dma((groups,)), dma((groups,)),
            dma((2,)), dma((2,)),
        ],
        compiler_params=pltpu.CompilerParams(
            collective_id=1, has_side_effects=True, vmem_limit_bytes=56 * 2**20
        ),
        cost_estimate=pl.CostEstimate(
            flops=20 * rows * wid * local_cols, bytes_accessed=20 * 2**20, transcendentals=0
        ),
    )(lengths, text_lengths, guidance, step_size, mixed, raw, mean, head, latent, text_kv, w_out, w_cross, w_last)


def on_device(
    hidden,
    latent,
    tenant_lengths,
    grid_positions,
    text_kv,
    text_lengths,
    w_query,
    w_key,
    w_value,
    w_out,
    w_cross_query,
    w_cross_out,
    w_head,
    guidance,
    step_size,
):
    halves, groups, parts, columns = (lax.axis_size(a) for a in ("cfg", "z", "t", "wt"))
    half_index, z_index, t_index, wt_index = (
        lax.axis_index(a) for a in ("cfg", "z", "t", "wt")
    )
    tok, width = hidden.shape[1:]
    rows = groups * tok
    local_cols = w_query.shape[1]
    my_cols = local_cols // groups
    heads = my_cols // HD
    paired = halves == 2 and parts == 2
    block = w_query.shape[0]
    if paired and groups == LINE and columns == 2 and tok % 16 == 0 and block % 16 == 0 and my_cols % HD == 0:
        mixed, raw, mean, out_wide = self_attention_call(
            tenant_lengths, hidden[0], grid_positions, w_key, w_value, w_query, w_out
        )
        hidden_out, latent_next = cross_attention_call(
            tenant_lengths, text_lengths, guidance, step_size, mixed, raw, mean, w_head.T, latent.T,
            text_kv, out_wide, w_cross_query, w_cross_out,
        )
        return (hidden_out[None], latent_next.T)
    ends = running_ends(tenant_lengths)

    def tenant_of(indices):
        return jnp.sum((indices[:, None] >= ends[None, :]).astype(jnp.int32), axis=1)

    def ordered(mine, other, index):
        return jnp.where(
            index == 0, jnp.concatenate([mine, other]), jnp.concatenate([other, mine])
        )

    def wide(w):
        if not paired:
            return lax.all_gather(w, ("cfg", "t"), axis=0, tiled=True)
        two = ordered(w, flip(w, "t"), t_index)
        return ordered(two, flip(two, "cfg"), half_index)

    def over_groups(x):
        return x if groups == 1 else lax.all_to_all(x, "z", 0, 0, tiled=True)

    def join_groups(x):
        if groups == 1:
            return x
        x = lax.all_gather(x, "z", axis=0)
        return jnp.swapaxes(x, 0, 1).reshape(x.shape[1], local_cols)

    def sum_at_owner(x):
        if groups == 1:
            return x[0].astype(F32)
        return jnp.sum(lax.all_to_all(x, "z", 0, 0).astype(F32), axis=0)

    def sum_groups(x):
        if groups == 1:
            return x
        return lax.psum_scatter(x, "z", scatter_dimension=0, tiled=True)

    def to_groups(x, n):
        return jnp.swapaxes(x.reshape(x.shape[0], groups, n), 0, 1)

    def both_columns(terms):
        terms = terms.astype(BF)
        if columns == 1:
            return terms.astype(F32)
        if columns == 2:
            return terms.astype(F32) + flip(terms, "wt").astype(F32)
        return lax.psum(terms, "wt").astype(F32)

    if paired:
        key_pair = ordered(w_key, flip(w_key, "t"), t_index)
        key_pair, w_query, w_value = lax.optimization_barrier((key_pair, w_query, w_value))
        wide_key = ordered(key_pair, flip(key_pair, "cfg"), half_index)
    else:
        wide_key = wide(w_key)
    wide_query, wide_value = wide(w_query), wide(w_value)
    wide_out, wide_cross, wide_cross_out = wide(w_out), wide(w_cross_query), wide(w_cross_out)

    chunks = CHUNKS if groups > 1 and tok % (CHUNKS * 16) == 0 else 1
    part = tok // chunks
    chunk_rows = rows // chunks

    def by_chunk(x):
        shape = (groups, chunks, part) + x.shape[2:]
        return jnp.swapaxes(x.reshape(shape), 0, 1).reshape((rows,) + x.shape[2:])

    def three_terms(x):
        high = lax.reduce_precision(x, 8, 7)
        middle = lax.reduce_precision(x - high, 8, 7)
        return [term.astype(BF) for term in (high, middle, x - high - middle)]

    own = hidden[0].astype(F32)
    mean = jnp.mean(own, axis=-1, keepdims=True)
    centred = own - mean
    scale = lax.rsqrt(jnp.mean(centred * centred, axis=-1, keepdims=True) + EPS)
    facts = jnp.concatenate([mean, scale, grid_positions.astype(F32)], axis=1)
    slice_width = width // groups
    if groups == 1:
        sliced = own
    else:
        extra = jnp.concatenate(three_terms(facts), axis=1)
        extra = jnp.pad(extra, ((0, 0), (0, 128 - extra.shape[1])))
        features = hidden[0].reshape(tok, halves, groups, slice_width // halves)
        features = jnp.concatenate(
            [features[:, half] for half in range(halves)]
            + [jnp.broadcast_to(extra[:, None], (tok, groups, 128))],
            axis=2,
        )
        arrived = lax.all_to_all(jnp.swapaxes(features, 0, 1), "z", 0, 0)
        arrived = by_chunk(arrived).astype(F32)
        sliced = arrived[:, :slice_width]
        extra = arrived[:, slice_width : slice_width + 15]
        facts = extra[:, 0:5] + extra[:, 5:10] + extra[:, 10:15]
    normed = ((sliced - facts[:, 0:1]) * facts[:, 1:2]).astype(BF)

    def project(w):
        return to_groups(jnp.dot(normed, w, preferred_element_type=F32).astype(BF), my_cols)

    projected_keys = sum_at_owner(project(wide_key)).astype(BF)
    projected = jnp.concatenate([project(wide_query), project(wide_value)], axis=2)
    projected = sum_groups(projected.reshape(groups * rows, 2 * my_cols))

    table, swap = rotary_tables()
    angles = (
        facts[:, 2:3] * table[0][None] + facts[:, 3:4] * table[1][None] + facts[:, 4:5] * table[2][None]
    )
    cosine, sinus = jnp.cos(angles)[:, None, :], jnp.sin(angles)[:, None, :]

    def rotated(x):
        shaped = x.reshape(rows, heads, HD)
        swapped = jnp.einsum("thd,de->the", shaped, jnp.asarray(swap, BF), preferred_element_type=F32)
        shaped = shaped.astype(F32)
        return ((shaped * cosine + swapped * sinus) * head_scale(shaped)).astype(BF)

    keys = rotated(projected_keys).reshape(rows, my_cols)
    queries = rotated(projected[:, :my_cols])
    values = projected[:, my_cols:]

    base = jnp.arange(groups, dtype=jnp.int32)[:, None] * (parts * tok)
    base = by_chunk(base + jnp.arange(tok, dtype=jnp.int32)[None])
    my_tenant = tenant_of(base + t_index * tok)
    if parts == 2:
        keys = jnp.concatenate([keys, flip(keys, "t")], axis=0)
        values = jnp.concatenate([values, flip(values, "t")], axis=0)
        key_tenant = jnp.concatenate([my_tenant, tenant_of(base + (1 - t_index) * tok)])
    else:
        keys = lax.all_gather(keys, "t", axis=0, tiled=True)
        values = lax.all_gather(values, "t", axis=0, tiled=True)
        key_tenant = tenant_of(
            (jnp.arange(parts, dtype=jnp.int32)[:, None] * tok + base[None]).reshape(-1)
        )
    keys = keys.reshape(-1, heads, HD)
    values = values.reshape(-1, heads, HD)

    spans = [slice(i * chunk_rows, (i + 1) * chunk_rows) for i in range(chunks)]
    mixed = [
        attend(queries[i], keys, values, my_tenant[i][:, None] == key_tenant[None, :])
        for i in spans
    ]

    def project_out(mixed, weight):
        return lax.dot_general(
            join_groups(mixed), weight, (((1,), (1,)), ((), ())), preferred_element_type=F32
        )

    column_sums = jnp.dot(jnp.ones((8, slice_width), BF), wide_cross, preferred_element_type=F32)
    column_sums = column_sums[0].reshape(groups, 1, my_cols)
    riding = groups > 1 and chunk_rows <= my_cols

    text = lax.dynamic_slice_in_dim(text_kv[:, 0], z_index * my_cols, my_cols, 2)
    text_keys = text[0].reshape(-1, heads, HD).astype(F32)
    text_keys = (text_keys * head_scale(text_keys)).astype(BF)
    text_values = text[1].reshape(-1, heads, HD)
    text_index = jnp.arange(text_kv.shape[2], dtype=jnp.int32)
    text_tenant = text_index // TEXT
    slots = text_tenant[:, None] == jnp.arange(TENANTS, dtype=jnp.int32)[None, :]
    live_length = jnp.sum(jnp.where(slots, text_lengths[0][None, :], 0), axis=1)
    live = text_index % TEXT < live_length

    states, cross_mixed = [], []
    for i, block_mixed in zip(spans, mixed):
        shifted = (sliced[i] - facts[i, 0:1]) + both_columns(project_out(block_mixed, wide_out))
        states.append(shifted)
        sums = jnp.stack([jnp.sum(shifted, axis=1), jnp.sum(shifted * shifted, axis=1)])
        crossed = jnp.dot(shifted.astype(BF), wide_cross, preferred_element_type=F32).astype(BF)
        crossed = to_groups(crossed, my_cols)
        if riding:
            sums = jnp.concatenate(three_terms(sums))
            sums = jnp.pad(sums, ((0, 0), (0, my_cols - chunk_rows)))
            sums = jnp.broadcast_to(sums[None], (groups,) + sums.shape)
            below = jnp.concatenate([sums] + three_terms(column_sums), axis=1)
            below = jnp.pad(below, ((0, 0), (0, 16 - below.shape[1]), (0, 0)))
            arrived = sum_at_owner(jnp.concatenate([crossed, below], axis=1))
            crossed, below = arrived[:chunk_rows], arrived[chunk_rows:]
            sums = (below[0:2] + below[2:4] + below[4:6])[:, :chunk_rows]
            all_columns = below[6:7] + below[7:8] + below[8:9]
        else:
            sums = sum_at_owner(jnp.broadcast_to(sums[None], (groups,) + sums.shape))
            all_columns = sum_at_owner(column_sums)
            crossed = sum_at_owner(crossed)
        sums = sums / width
        variance = jnp.maximum(sums[1] - sums[0] * sums[0], 0.0)[:, None, None]
        shaped = (crossed - sums[0][:, None] * all_columns).reshape(chunk_rows, heads, HD)
        square = jnp.mean(shaped * shaped, axis=-1, keepdims=True)
        cross_queries = (shaped * lax.rsqrt(square + EPS * (variance + EPS))).astype(BF)
        allowed = (my_tenant[i][:, None] == text_tenant[None, :]) & live[None]
        cross_mixed.append(attend(cross_queries, text_keys, text_values, allowed))

    channels = w_head.shape[1]
    head_rows = lax.dynamic_index_in_dim(
        w_head.reshape(halves, groups, parts * block, channels), z_index, 1, keepdims=False
    ).reshape(-1, channels)
    totals = jnp.sum(w_head.astype(F32), axis=0)[None]
    out_width = width // columns

    leaving, sums = [], []
    for i, shifted, block_mixed in zip(spans, states, cross_mixed):
        shifted = shifted + both_columns(project_out(block_mixed, wide_cross_out))
        final = (shifted + facts[i, 0:1]).astype(BF)
        if groups > 1 and columns == halves:
            span = slice_width // halves
            final = lax.dynamic_slice_in_dim(final, wt_index * span, span, 1)
        leaving.append(final.reshape(groups, part, -1))
        some = jnp.concatenate(
            [
                jnp.dot(shifted.astype(BF), head_rows, preferred_element_type=F32),
                jnp.sum(shifted, axis=1, keepdims=True),
                jnp.sum(shifted * shifted, axis=1, keepdims=True),
            ],
            axis=1,
        )
        sums.append(some.reshape(groups, part, channels + 2))
    sums = sum_at_owner(jnp.concatenate(sums, axis=1))
    mean = sums[:, channels : channels + 1] / width
    variance = jnp.maximum(sums[:, channels + 1 :] / width - mean * mean, 0.0)
    velocity = (sums[:, :channels] - mean * totals) * lax.rsqrt(variance + EPS)

    leaving = jnp.concatenate(leaving, axis=1)
    if groups == 1:
        hidden_out = lax.dynamic_slice_in_dim(leaving[0], wt_index * out_width, out_width, 1)
    else:
        leaving = jnp.swapaxes(lax.all_to_all(leaving, "z", 0, 0), 0, 1)
        if columns == halves:
            hidden_out = leaving.reshape(tok, out_width)
        else:
            leaving = jnp.swapaxes(leaving.reshape(tok, groups, halves, -1), 1, 2)
            hidden_out = lax.dynamic_slice_in_dim(
                leaving.reshape(tok, width), wt_index * out_width, out_width, 1
            )

    channel_half = latent.shape[1]
    outgoing = lax.dynamic_slice_in_dim(velocity, (1 - half_index) * channel_half, channel_half, 1)
    partner = flip(outgoing, "cfg")
    own_part = lax.dynamic_slice_in_dim(velocity, half_index * channel_half, channel_half, 1)
    conditional = jnp.where(half_index == 0, own_part, partner)
    null_text = jnp.where(half_index == 0, partner, own_part)
    latent_next = latent + step_size[0] * (null_text + guidance[0] * (conditional - null_text))
    return (hidden_out[None], latent_next)


def solution(mesh):
    halves, seq, columns = (mesh.shape[a] for a in ("cfg", "seq", "wt"))

    def run(*args):
        heads_here = args[6].shape[1] // columns // HD
        groups = math.gcd(heads_here, seq)
        fine = Mesh(
            mesh.devices.reshape(halves, groups, seq // groups, columns), ("cfg", "z", "t", "wt")
        )
        seq_axes = ("z", "t")
        weight = P(("cfg", "z", "t"), "wt")
        return jax.shard_map(
            on_device,
            mesh=fine,
            in_specs=(
                P("cfg", seq_axes, None),
                P(seq_axes, "cfg"),
                P(),
                P(seq_axes, None),
                P(None, "cfg", None, "wt"),
                P("cfg", None),
                weight,
                weight,
                weight,
                weight,
                weight,
                weight,
                P(),
                P(),
                P(),
            ),
            out_specs=(P("cfg", seq_axes, "wt"), P(seq_axes, "cfg")),
            check_vma=False,
        )(*args)

    return run
```

```python
import math

import jax
import jax.numpy as jnp
import numpy as np
from jax import lax
from jax.experimental import pallas as pl
from jax.experimental.pallas import tpu as pltpu
from jax.sharding import Mesh
from jax.sharding import PartitionSpec as P

HD = 128
TEXT = 512
TENANTS = 4
EPS = 1e-06
CHUNKS = 2
BF = jnp.bfloat16
F32 = jnp.float32


def flip(block, axis):
    return lax.ppermute(block, axis, [(0, 1), (1, 0)])


def rotary_tables():
    sixth = HD // 6
    table = np.zeros((3, HD), np.float32)
    lane = 0
    for column, span in enumerate((HD - 4 * sixth, 2 * sixth, 2 * sixth)):
        exponent = np.arange(0, span, 2).astype(np.float32) / np.float32(span)
        frequency = (1.0 / 10000.0**exponent).astype(np.float32)
        table[column, lane : lane + span] = np.repeat(frequency, 2)
        lane += span
    swap = np.zeros((HD, HD), np.float32)
    for pair in range(0, HD, 2):
        swap[pair + 1, pair] = -1.0
        swap[pair, pair + 1] = 1.0
    return table, swap


def running_ends(lengths):
    upto = np.tril(np.ones((TENANTS, TENANTS), np.int32))
    return jnp.sum(jnp.asarray(upto) * lengths[None, :], axis=1)


def head_scale(shaped):
    return lax.rsqrt(jnp.mean(shaped * shaped, axis=-1, keepdims=True) + EPS)


def attend(queries, keys, values, allowed):
    scores = jnp.einsum("qhd,khd->hqk", queries, keys, preferred_element_type=F32)
    scores = scores * (1.0 / math.sqrt(queries.shape[-1]))
    weights = jnp.where(allowed[None], jnp.exp(scores), 0.0).astype(BF)
    summed = jnp.einsum("hqk,khd->qhd", weights, values, preferred_element_type=F32)
    totals = jnp.sum(weights.astype(F32), axis=2).T
    return (summed / totals[..., None]).astype(BF).reshape(queries.shape[0], -1)


MESH = pl.DeviceIdType.MESH
NEAR = (1, 3, 2)
LINE = 4


def remote(src, dst, sent, got, device):
    return pltpu.make_async_remote_copy(
        src_ref=src, dst_ref=dst, send_sem=sent, recv_sem=got, device_id=device, device_id_type=MESH
    )


def meet(devices):
    barrier = pltpu.get_barrier_semaphore()
    for device in devices:
        pl.semaphore_signal(barrier, inc=1, device_id=device, device_id_type=MESH)
    pl.semaphore_wait(barrier, len(devices))


def span(index, size):
    return pl.ds(pl.multiple_of(index * size, size), size)


def nt_dot(a, b):
    return lax.dot_general(a, b, (((1,), (1,)), ((), ())), preferred_element_type=F32)


def tenants_at(index, lengths):
    found, end = jnp.zeros(index.shape, jnp.int32), 0
    for tenant in range(TENANTS):
        end = end + lengths[tenant]
        found = found + (index >= end).astype(jnp.int32)
    return found


def self_attention_kernel(
    lengths, pos, table, hid, wk, wv, wq, w_out, mixed_out, raw_out, mean_out, out_wide,
    wide, rows, normed, pairs, queries, pos_all, rot,
    loc_w, loc_h, raw_sem, zs, zr, hs, hr, ps, pr, xs, xr, cs, cr, ys, yr, ks, kr, us, ur,
):
    c, z, x, y = (lax.axis_index(a) for a in ("cfg", "z", "t", "wt"))
    groups = LINE
    tok = hid.shape[0]
    depth = wk.shape[0]
    wid = rows.shape[2]
    cols = wide.shape[3]
    heads = cols // HD
    at_z = [{"z": lax.rem(z + d, groups)} for d in range(groups)]
    from_z = [lax.rem(z + groups - d, groups) for d in range(groups)]
    at_x, at_c, at_y = {"t": 1 - x}, {"cfg": 1 - c}, {"wt": 1 - y}
    weights = (wk, wv, wq)
    mine = c * groups + z

    own_rows = [
        pltpu.make_async_copy(hid.at[:, kb * wid : (kb + 1) * wid], rows.at[kb, span(z, tok)], loc_h.at[kb])
        for kb in range(2 * groups)
    ]
    own_weights = [
        pltpu.make_async_copy(w.at[:, span(z, cols)], wide.at[j, mine, span(x, depth)], loc_w.at[j])
        for j, w in enumerate(weights)
    ]
    for copy in own_rows + own_weights:
        copy.start()
    high, long = pos_all.shape[1:]
    held = jnp.concatenate([pos[...].astype(F32), jnp.zeros((pos.shape[0], long - tok), F32)], axis=1)
    pos_all[z] = jnp.concatenate([held, jnp.zeros((high - pos.shape[0], long), F32)], axis=0)
    meet([at_z[1], at_z[2], at_z[3], at_x, at_c, at_y])

    def block(j, d, column):
        return wide.at[j, c * groups + from_z[d], span(column, depth)]

    def x_copy(j, d):
        return remote(block(j, d, x), block(j, d, x), xs.at[d, j], xr.at[d, j], at_x)

    def x_arrival(j, d):
        return remote(block(j, d, 1 - x), block(j, d, 1 - x), xs.at[d, j], xr.at[d, j], at_x)

    def c_copy(j, d, second):
        part = block(j, d, 1 - x if second else x)
        return remote(part, part, cs.at[second, d, j], cr.at[second, d, j], at_c)

    def c_arrival(j, d, second):
        part = wide.at[j, (1 - c) * groups + from_z[d], span(1 - x if second else x, depth)]
        return remote(part, part, cs.at[second, d, j], cr.at[second, d, j], at_c)

    def z_copy(j, d):
        target = lax.rem(z + d, groups)
        return remote(
            weights[j].at[:, span(target, cols)], wide.at[j, mine, span(x, depth)], zs.at[d - 1, j], zr.at[d - 1, j], at_z[d]
        )

    def z_arrival(j, d):
        return remote(block(j, d, x), block(j, d, x), zs.at[d - 1, j], zr.at[d - 1, j], at_z[d])

    def rows_of(b, column, piece):
        return rows.at[column * groups + piece, span(b, tok)]

    def by_z(*choices):
        return jnp.where(z == 0, choices[0], jnp.where(z == 1, choices[1], jnp.where(z == 2, choices[2], choices[3])))

    inner = jnp.logical_and(z > 0, z < groups - 1)
    way_of = [None, by_z(1, 0, 1, 0), by_z(1, 1, 0, 0), by_z(1, 1, 0, 0)]
    step_of = [None, by_z(0, 0, 0, 0), by_z(1, 0, 0, 1), by_z(2, 1, 1, 2)]
    block_of = [z, by_z(1, 0, 3, 2), by_z(2, 2, 1, 1), by_z(3, 3, 0, 0)]

    def out_part(core, column):
        return out_wide.at[core, span(column, depth)]

    own_out = pltpu.make_async_copy(w_out, out_part(c, x), loc_w.at[4])
    own_out.start()
    out_x = remote(w_out, out_part(c, x), us.at[0], ur.at[0], at_x)
    out_c = remote(w_out, out_part(c, x), us.at[1], ur.at[1], at_c)
    out_on = remote(out_part(c, 1 - x), out_part(c, 1 - x), us.at[2], ur.at[2], at_c)

    def h_own(way, p):
        part = rows_of(z, y, p)
        return remote(part, part, hs.at[way, 0, p], hr.at[way, 0, p], {"z": z + 1 - 2 * way})

    def h_arrival(e, p):
        part = rows_of(block_of[e], y, p)
        return remote(part, part, hs.at[way_of[e], step_of[e], p], hr.at[way_of[e], step_of[e], p], at_y)

    def h_onward(e, p):
        part = rows_of(block_of[e], y, p)
        at = step_of[e] + 1
        return remote(part, part, hs.at[way_of[e], at, p], hr.at[way_of[e], at, p], {"z": z + 1 - 2 * way_of[e]})

    def y_copy(e, p):
        part = rows_of(block_of[e], y, p)
        return remote(part, part, ys.at[e - 1, p], yr.at[e - 1, p], at_y)

    def y_arrival(e, p):
        part = rows_of(block_of[e], 1 - y, p)
        return remote(part, part, ys.at[e - 1, p], yr.at[e - 1, p], at_y)

    def up(p):
        @pl.when(z < groups - 1)
        def _():
            h_own(0, p).start()

        @pl.when(z > 0)
        def _():
            h_own(1, p).start()

    def arrive(e):
        for p in range(groups):
            h_arrival(e, p).wait_recv()

            @pl.when(inner)
            def _():
                h_onward(e, p).start()

            y_copy(e, p).start()

    def p_copy(d):
        return remote(pos_all.at[z], pos_all.at[z], ps.at[d - 1], pr.at[d - 1], at_z[d])

    def p_arrival(d):
        part = pos_all.at[from_z[d]]
        return remote(part, part, ps.at[d - 1], pr.at[d - 1], at_z[d])

    some = 16
    width = 2 * groups * wid

    def norm_block(b):
        def norm(i, carry):
            these = pl.ds(pl.multiple_of(b * tok + i * some, some), some)
            total = jnp.zeros((some, wid), F32)
            for kb in range(2 * groups):
                total += rows[kb, these].astype(F32)
            mean = jnp.sum(total, axis=1, keepdims=True) / width
            total = jnp.zeros((some, wid), F32)
            for kb in range(2 * groups):
                centred = rows[kb, these].astype(F32) - mean
                total += centred * centred
            scale = lax.rsqrt(jnp.sum(total, axis=1, keepdims=True) / width + EPS)
            for kb in range(2 * groups):
                normed[kb, these] = ((rows[kb, these].astype(F32) - mean) * scale).astype(BF)
            mean_out[these] = mean
            return carry

        lax.fori_loop(0, tok // some, norm, 0)

    for copy in own_rows:
        copy.wait()
    for d in NEAR:
        p_copy(d).start()
    for d in NEAR:
        z_copy(0, d).start()
    for j in range(3):
        own_weights[j].wait()
        x_copy(j, 0).start()
        c_copy(j, 0, 0).start()
    norm_block(z)

    def relay(j, d):
        z_arrival(j, d).wait_recv()
        x_copy(j, d).start()
        c_copy(j, d, 0).start()

    def second_relay(j, d):
        x_arrival(j, d).wait_recv()
        c_copy(j, d, 1).start()

    for j in range(3):
        second_relay(j, 0)
    relay(0, 1)
    for d in NEAR:
        z_copy(1, d).start()
    relay(0, 3)
    relay(0, 2)
    for p in range(groups):
        up(p)
    for d in NEAR:
        second_relay(0, d)
    relay(1, 1)
    relay(1, 3)
    relay(1, 2)
    for d in NEAR:
        second_relay(1, d)
    out_x.start()
    out_c.start()
    arrive(1)

    @pl.when(inner)
    def _():
        arrive(2)

    for d in NEAR:
        p_arrival(d).wait_recv()
    lane = lax.broadcasted_iota(jnp.int32, (tok, HD), 1)
    even = lax.rem(lane, 2) == 0
    for m in range(groups):
        held = pos_all[m]
        full = jnp.concatenate([held, jnp.zeros((HD - held.shape[0], held.shape[1]), F32)], axis=0)
        column = jnp.transpose(full)[:tok]
        angles = sum(column[:, a : a + 1] * table[a : a + 1, :] for a in range(3))
        rot[0, m * tok : (m + 1) * tok] = jnp.cos(angles)
        sinus = jnp.sin(angles)
        rot[1, m * tok : (m + 1) * tok] = jnp.where(even, -sinus, sinus)

    def rotated(these, total):
        turned = []
        even = lax.rem(lax.broadcasted_iota(jnp.int32, (total.shape[0], HD), 1), 2) == 0
        for h in range(heads):
            part = total[:, h * HD : (h + 1) * HD]
            scale = lax.rsqrt(jnp.mean(part * part, axis=1, keepdims=True) + EPS)
            swapped = jnp.where(even, pltpu.roll(part, HD - 1, 1), pltpu.roll(part, 1, 1))
            turned.append((part * rot[0, these] + swapped * rot[1, these]) * scale)
        return jnp.concatenate(turned, axis=1).astype(BF)

    def pair_copy(e):
        part = pairs.at[x, :, span(block_of[e], tok)]
        return remote(part, part, ks.at[e], kr.at[e], at_x)

    def pair_arrival(e):
        part = pairs.at[1 - x, :, span(block_of[e], tok)]
        return remote(part, part, ks.at[e], kr.at[e], at_x)

    def project(e, j):
        these = span(block_of[e], tok) if j < 2 else span(e, 2 * tok)
        total = jnp.dot(normed[0, these], wide[j, 0], preferred_element_type=F32)
        for kb in range(1, 2 * groups):
            total += jnp.dot(normed[kb, these], wide[j, kb], preferred_element_type=F32)
        if j == 0:
            pairs[x, 0, these] = rotated(these, total)
        elif j == 1:
            pairs[x, 1, these] = total.astype(BF)
            pair_copy(e).start()
        else:
            queries[these] = rotated(these, total)

    def all_here(j):
        for d in range(groups):
            c_arrival(j, d, 0).wait_recv()
            c_arrival(j, d, 1).wait_recv()

    def finish(e):
        for p in range(groups):
            y_arrival(e, p).wait_recv()
        norm_block(block_of[e])
        project(e, 0)
        project(e, 1)

    all_here(0)
    all_here(1)
    project(0, 0)
    project(0, 1)

    @pl.when(inner)
    def _():
        arrive(3)

    @pl.when(jnp.logical_not(inner))
    def _():
        arrive(2)

    for d in NEAR:
        z_copy(2, d).start()
    out_here = remote(out_part(c, 1 - x), out_part(c, 1 - x), us.at[0], ur.at[0], at_x)
    out_here.wait_recv()
    out_on.start()
    finish(1)

    @pl.when(jnp.logical_not(inner))
    def _():
        arrive(3)

    relay(2, 1)
    relay(2, 3)
    raws = [
        pltpu.make_async_copy(rows.at[half * groups + z], raw_out.at[half], raw_sem.at[half]) for half in (0, 1)
    ]
    finish(2)
    relay(2, 2)
    for d in NEAR:
        second_relay(2, d)
    finish(3)
    for copy in raws:
        copy.start()
    all_here(2)

    def ask(m, carry):
        project(m, 2)
        return carry

    lax.fori_loop(0, groups // 2, ask, 0)
    for e in range(groups):
        pair_arrival(e).wait_recv()

    lane = lax.broadcasted_iota(jnp.int32, (1, groups * tok), 1)
    behind = sum((lane >= k * tok).astype(jnp.int32) for k in range(1, groups))
    key_tenant = [tenants_at(lane + (behind + part) * tok, lengths) for part in (0, 1)]
    ones = jnp.ones((groups * tok, HD), BF)

    def attend_block(m, carry):
        these = span(m, tok)
        index = lax.broadcasted_iota(jnp.int32, (tok, 1), 0) + (m * 2 + x) * tok
        tenant = tenants_at(index, lengths)
        for h in range(heads):
            lanes = slice(h * HD, (h + 1) * HD)
            summed = jnp.zeros((tok, 2 * HD), F32)
            for part in (0, 1):
                scores = nt_dot(queries[these, lanes], pairs[part, 0, :, lanes]) * (1.0 / math.sqrt(HD))
                chances = jnp.where(tenant == key_tenant[part], jnp.exp(scores), 0.0).astype(BF)
                both = jnp.concatenate([pairs[part, 1, :, lanes], ones], axis=1)
                summed += jnp.dot(chances, both, preferred_element_type=F32)
            mixed_out[these, lanes] = (summed[:, :HD] / summed[:, HD:]).astype(BF)
        return carry

    lax.fori_loop(0, groups, attend_block, 0)

    for copy in raws:
        copy.wait()
    for p in range(groups):
        @pl.when(z < groups - 1)
        def _():
            h_own(0, p).wait_send()

        @pl.when(z > 0)
        def _():
            h_own(1, p).wait_send()

        for e in (1, 2, 3):
            @pl.when(inner)
            def _():
                h_onward(e, p).wait_send()

            y_copy(e, p).wait_send()
    for d in NEAR:
        p_copy(d).wait_send()
        for j in range(3):
            z_copy(j, d).wait_send()
    for d in range(groups):
        for j in range(3):
            x_copy(j, d).wait_send()
            c_copy(j, d, 0).wait_send()
            c_copy(j, d, 1).wait_send()
    for e in range(groups):
        pair_copy(e).wait_send()
    own_out.wait()
    out_x.wait_send()
    for index, part in ((1, out_part(1 - c, x)), (2, out_part(1 - c, 1 - x))):
        remote(part, part, us.at[index], ur.at[index], at_c).wait()


def self_attention_call(lengths, hidden, positions, wk, wv, wq, w_out):
    tok, width = hidden.shape
    groups = LINE
    depth, local_cols = wk.shape
    cols = local_cols // groups
    rows = groups * tok
    wid = width // (2 * groups)
    anywhere = pl.BlockSpec(memory_space=pl.ANY)
    vmem = pl.BlockSpec(memory_space=pltpu.VMEM)
    smem = pl.BlockSpec(memory_space=pltpu.SMEM)
    dma = pltpu.SemaphoreType.DMA
    made = [
        jax.ShapeDtypeStruct((rows, cols), BF),
        jax.ShapeDtypeStruct((2, rows, wid), BF),
        jax.ShapeDtypeStruct((rows, 1), F32),
        jax.ShapeDtypeStruct((2, 2 * depth, local_cols), BF),
    ]
    table = np.zeros((8, HD), np.float32)
    table[:3] = rotary_tables()[0]
    return pl.pallas_call(
        self_attention_kernel,
        out_shape=made,
        in_specs=[smem, vmem, vmem] + [anywhere] * 5,
        out_specs=[vmem] * 3 + [anywhere],
        scratch_shapes=[
            pltpu.VMEM((3, 2 * groups, 2 * depth, cols), BF),
            pltpu.VMEM((2 * groups, rows, wid), BF),
            pltpu.VMEM((2 * groups, rows, wid), BF),
            pltpu.VMEM((2, 2, rows, cols), BF),
            pltpu.VMEM((rows, cols), BF),
            pltpu.VMEM((groups, 8, tok + -tok % HD), F32),
            pltpu.VMEM((2, rows, HD), F32),
            dma((5,)), dma((2 * groups,)), dma((2,)),
            dma((3, 3)), dma((3, 3)),
            dma((2, 3, 4)), dma((2, 3, 4)),
            dma((3,)), dma((3,)),
            dma((4, 3)), dma((4, 3)),
            dma((2, 4, 3)), dma((2, 4, 3)),
            dma((3, 4)), dma((3, 4)),
            dma((4,)), dma((4,)), dma((3,)), dma((3,)),
        ],
        compiler_params=pltpu.CompilerParams(
            collective_id=0, has_side_effects=True, vmem_limit_bytes=56 * 2**20
        ),
        cost_estimate=pl.CostEstimate(
            flops=6 * rows * width * cols, bytes_accessed=20 * 2**20, transcendentals=0
        ),
    )(lengths, positions.T, jnp.asarray(table), hidden, wk, wv, wq, w_out)


def line_places(z):
    def block(way, s):
        return z - s if way == 0 else z + s

    def sends(way, s):
        if way == 0:
            return jnp.logical_and(z - s >= 0, z + 1 < LINE)
        return jnp.logical_and(z + s < LINE, z >= 1)

    def gets(way, s):
        return z - 1 - s >= 0 if way == 0 else z + 1 + s < LINE

    return block, sends, gets


def pack_columns(first, second):
    tok = first.shape[0]
    lane = lax.broadcasted_iota(jnp.int32, (tok, HD), 1)
    both = jnp.where(lane == 0, first, jnp.where(lane == 1, second, 0.0))
    both = jnp.concatenate([both, jnp.zeros((-tok % HD, HD), F32)], axis=0)
    return jnp.transpose(both)[:8]


def unpack_columns(packed, tok):
    full = jnp.concatenate([packed, jnp.zeros((HD - packed.shape[0], packed.shape[1]), F32)], axis=0)
    column = jnp.transpose(full)[:tok]
    return column[:, 0:1], column[:, 1:2]


def cross_attention_kernel(
    lengths, text_lengths, guidance, step_size, mixed, raw, mean, head, latent, text_kv, w_out, w_cross, w_last,
    hidden_out, latent_out,
    wide, text, gath, own, left, right, left2, right2, kept, state, asked, answers, facts, facts_in, cols_out, cols_in,
    leaving, vel, vel_in, half_out, half_in, core_out, core_in,
    loc_w, loc_t, loc_g, loc_f, ws, wr, wcs, wcr, gs, gr, ys, yr, y2s, y2r, qs, qr, fs, fr, ss, sr, os_, or_, vs, vr, es, er,
):
    c, z, x, y = (lax.axis_index(a) for a in ("cfg", "z", "t", "wt"))
    groups = LINE
    rows, cols = mixed.shape
    tok = rows // groups
    depth = w_last.shape[0]
    wid = raw.shape[2]
    width = 2 * groups * wid
    heads = cols // HD
    channels = head.shape[0]
    slots = text.shape[1] // TENANTS
    at_z = [{"z": lax.rem(z + d, groups)} for d in range(groups)]
    from_z = [lax.rem(z + groups - d, groups) for d in range(groups)]
    at_x, at_c, at_y = {"t": 1 - x}, {"cfg": 1 - c}, {"wt": 1 - y}
    at_line = ({"z": jnp.minimum(z + 1, groups - 1)}, {"z": jnp.maximum(z - 1, 0)})
    line_block, line_sends, line_gets = line_places(z)
    own_weights = [pltpu.make_async_copy(w_out, wide.at[0], loc_w.at[0])]
    own_weights += [
        pltpu.make_async_copy(w, wide.at[j, c, span(x, depth)], loc_w.at[j]) for j, w in ((1, w_cross), (2, w_last))
    ]
    own_text = [pltpu.make_async_copy(text_kv.at[k, 0, :, span(z, cols)], text.at[k], loc_t.at[k]) for k in (0, 1)]
    for copy in own_weights + own_text:
        copy.start()
    own[0] = mixed[...].reshape(groups, tok, cols)
    meet([at_z[1], at_z[2], at_z[3], at_x, at_c, at_y])

    def g_local(f, i):
        return pltpu.make_async_copy(own.at[f, i], gath.at[f, i, :, span(z, cols)], loc_g.at[f, i])

    def g_copy(f, i, way, s):
        part = gath.at[f, i, :, span(line_block(way, s), cols)]
        return remote(own.at[f, i] if s == 0 else part, part, gs.at[f, i, way, s], gr.at[f, i, way, s], at_line[way])

    def g_arrival(f, i, way, s):
        part = gath.at[f, i, :, span(line_block(way, s + 1), cols)]
        return remote(part, part, gs.at[f, i, way, s], gr.at[f, i, way, s], at_line[way])

    def g_start(f, i):
        for way in (0, 1):
            @pl.when(line_sends(way, 0))
            def _():
                g_copy(f, i, way, 0).start()
        g_local(f, i).start()

    def g_step(f, i, s):
        for way in (0, 1):
            @pl.when(line_gets(way, s))
            def _():
                g_arrival(f, i, way, s).wait_recv()
                if s + 1 < groups - 1:
                    @pl.when(line_sends(way, s + 1))
                    def _():
                        g_copy(f, i, way, s + 1).start()
        if s == groups - 2:
            g_local(f, i).wait()

    def w_part(j, core, column):
        return wide.at[j, core, span(column, depth)]

    def w_copy(j):
        return remote(w_part(j, c, x), w_part(j, c, x), ws.at[j], wr.at[j], at_x)

    def w_arrival(j):
        return remote(w_part(j, c, 1 - x), w_part(j, c, 1 - x), ws.at[j], wr.at[j], at_x)

    def wc_copy(j, second):
        part = w_part(j, c, 1 - x if second else x)
        return remote(part, part, wcs.at[j, second], wcr.at[j, second], at_c)

    def wc_arrival(j, second):
        part = w_part(j, 1 - c, 1 - x if second else x)
        return remote(part, part, wcs.at[j, second], wcr.at[j, second], at_c)

    def w_relay(j):
        w_arrival(j).wait_recv()
        wc_copy(j, 1).start()

    def w_ready(j):
        wc_arrival(j, 0).wait_recv()
        wc_arrival(j, 1).wait_recv()

    turn = (0, 3, 1, 2)
    for i in turn:
        g_start(0, i)
    for j in (1, 2):
        own_weights[j].wait()
        w_copy(j).start()
        wc_copy(j, 0).start()

    for copy in own_text:
        copy.wait()

    def norm_text(i, carry):
        these = span(i, HD)
        for h in range(heads):
            lanes = slice(h * HD, (h + 1) * HD)
            part = text[0, these, lanes].astype(F32)
            scale = lax.rsqrt(jnp.mean(part * part, axis=1, keepdims=True) + EPS)
            text[0, these, lanes] = (part * scale).astype(BF)
        return carry

    lax.fori_loop(0, text.shape[1] // HD, norm_text, 0)
    totals = nt_dot(jnp.ones((16, width), BF), head[...])[0:1]

    def y_copy(i):
        return remote(left.at[i], right.at[i], ys.at[i], yr.at[i], at_y)

    def y2_copy(i):
        return remote(left2.at[i], right2.at[i], y2s.at[i], y2r.at[i], at_y)

    def q_copy(i, d):
        return remote(asked.at[i, lax.rem(z + d, groups)], answers.at[i, z], qs.at[i, d - 1], qr.at[i, d - 1], at_z[d])

    def q_arrival(i, d):
        part = answers.at[i, from_z[d]]
        return remote(part, part, qs.at[i, d - 1], qr.at[i, d - 1], at_z[d])

    def f_copy(i, d):
        return remote(facts.at[i], facts_in.at[i, z], fs.at[i, d - 1], fr.at[i, d - 1], at_z[d])

    def f_arrival(i, d):
        part = facts_in.at[i, from_z[d]]
        return remote(part, part, fs.at[i, d - 1], fr.at[i, d - 1], at_z[d])

    def s_copy(d):
        return remote(cols_out.at[lax.rem(z + d, groups)], cols_in.at[z], ss.at[d - 1], sr.at[d - 1], at_z[d])

    def s_arrival(d):
        part = cols_in.at[from_z[d]]
        return remote(part, part, ss.at[d - 1], sr.at[d - 1], at_z[d])

    def project_out(i):
        for half in (0, 1):
            left[i, :, half * wid : (half + 1) * wid] = nt_dot(gath[0, i], wide[0, half]).astype(BF)
        y_copy(i).start()

    def sum_columns():
        ones = jnp.ones((16, wid), BF)
        for g in range(groups):
            lanes = slice(g * cols, (g + 1) * cols)
            total = jnp.dot(ones, wide[1, 0, :, lanes], preferred_element_type=F32)
            total += jnp.dot(ones, wide[1, 1, :, lanes], preferred_element_type=F32)
            cols_out[g] = total[:8]
        for d in NEAR:
            s_copy(d).start()

    def update(i):
        y_copy(i).wait_recv()
        these = slice(i * tok, (i + 1) * tok)
        shift = mean[these]
        first = second = jnp.zeros((tok, 1), F32)
        for half in (0, 1):
            lanes = slice(half * wid, (half + 1) * wid)
            both = left[i, :, lanes].astype(F32) + right[i, :, lanes].astype(F32)
            new = (raw[half, these].astype(F32) - shift) + both
            state[i, half] = new
            first += jnp.sum(new, axis=1, keepdims=True)
            second += jnp.sum(new * new, axis=1, keepdims=True)
        facts[i] = pack_columns(first, second)
        for d in NEAR:
            f_copy(i, d).start()
        for g in range(groups):
            lanes = slice(g * cols, (g + 1) * cols)
            part = jnp.dot(state[i, 0].astype(BF), wide[1, 0, :, lanes], preferred_element_type=F32)
            part += jnp.dot(state[i, 1].astype(BF), wide[1, 1, :, lanes], preferred_element_type=F32)
            asked[i, g] = part.astype(BF)
        for d in NEAR:
            q_copy(i, d).start()

    def cross(i):
        packed = facts[i]
        crossed = asked[i, z].astype(F32)
        column_sums = cols_out[z, 0:1]
        for d in NEAR:
            q_arrival(i, d).wait_recv()
            f_arrival(i, d).wait_recv()
            if i == turn[0]:
                s_arrival(d).wait_recv()
            packed = packed + facts_in[i, from_z[d]]
            crossed = crossed + answers[i, from_z[d]].astype(F32)
            column_sums = column_sums + cols_in[from_z[d], 0:1]
        first, second = unpack_columns(packed, tok)
        average = first / width
        variance = jnp.maximum(second / width - average * average, 0.0)
        crossed = crossed - average * column_sums
        index = lax.broadcasted_iota(jnp.int32, (tok, 1), 0) + (i * 2 + x) * tok
        tenant = tenants_at(index, lengths)
        slot = lax.broadcasted_iota(jnp.int32, (1, slots), 1)
        ones = jnp.ones((slots, HD), BF)
        for h in range(heads):
            lanes = slice(h * HD, (h + 1) * HD)
            part = crossed[:, lanes]
            square = jnp.mean(part * part, axis=1, keepdims=True)
            query = (part * lax.rsqrt(square + EPS * (variance + EPS))).astype(BF)
            summed = jnp.zeros((tok, 2 * HD), F32)
            for t in range(TENANTS):
                these = slice(t * slots, (t + 1) * slots)
                scores = nt_dot(query, text[0, these, lanes]) * (1.0 / math.sqrt(HD))
                allowed = jnp.logical_and(tenant == t, slot < text_lengths[0, t])
                chances = jnp.where(allowed, jnp.exp(scores), 0.0).astype(BF)
                both = jnp.concatenate([text[1, these, lanes], ones], axis=1)
                summed += jnp.dot(chances, both, preferred_element_type=F32)
            own[1, i, :, lanes] = (summed[:, :HD] / summed[:, HD:]).astype(BF)
        g_start(1, i)

    def project_last(i):
        left2[i] = nt_dot(gath[1, i], wide[2, 1 - y]).astype(BF)
        y2_copy(i).start()
        kept[i] = nt_dot(gath[1, i], wide[2, y]).astype(BF)

    def o_remote(i):
        return remote(leaving.at[i], hidden_out.at[:, span(z, wid)], os_.at[i], or_.at[z], {"z": i})

    def o_local(i):
        return pltpu.make_async_copy(leaving.at[i], hidden_out.at[:, span(z, wid)], loc_f)

    def v_remote(i):
        return remote(vel.at[i], vel_in.at[z], vs.at[i], vr.at[z], {"z": i})

    def finish(i):
        y2_copy(i).wait_recv()
        these = slice(i * tok, (i + 1) * tok)
        final = state[i, y] + kept[i].astype(F32) + right2[i].astype(F32)
        leaving[i] = (final + mean[these]).astype(BF)

        @pl.when(z != i)
        def _():
            o_remote(i).start()

        @pl.when(z == i)
        def _():
            o_local(i).start()

        rows_here = pl.ds(pl.multiple_of((y * groups + z) * wid, wid), wid)
        some = nt_dot(final.astype(BF), head[:, rows_here])
        first = jnp.sum(final, axis=1, keepdims=True)
        second = jnp.sum(final * final, axis=1, keepdims=True)
        lane = lax.broadcasted_iota(jnp.int32, (tok, HD - channels), 1)
        tail = jnp.where(lane == 0, first, jnp.where(lane == 1, second, 0.0))
        vel[i] = jnp.concatenate([some, tail], axis=1)

        @pl.when(z != i)
        def _():
            v_remote(i).start()

    g_step(0, turn[0], 0)
    g_step(0, turn[1], 0)
    g_step(0, turn[0], 1)
    g_step(0, turn[2], 0)
    g_step(0, turn[1], 1)
    g_step(0, turn[0], 2)
    own_weights[0].wait()
    project_out(turn[0])
    g_step(0, turn[3], 0)
    g_step(0, turn[2], 1)
    g_step(0, turn[1], 2)
    project_out(turn[1])
    w_relay(1)
    g_step(0, turn[3], 1)
    g_step(0, turn[2], 2)
    project_out(turn[2])
    w_ready(1)
    sum_columns()
    update(turn[0])
    g_step(0, turn[3], 2)
    project_out(turn[3])
    update(turn[1])
    cross(turn[0])
    update(turn[2])
    w_relay(2)
    g_step(1, turn[0], 0)
    cross(turn[1])
    update(turn[3])
    g_step(1, turn[1], 0)
    g_step(1, turn[0], 1)
    cross(turn[2])
    g_step(1, turn[2], 0)
    g_step(1, turn[1], 1)
    g_step(1, turn[0], 2)
    w_ready(2)
    project_last(turn[0])
    cross(turn[3])
    g_step(1, turn[3], 0)
    g_step(1, turn[2], 1)
    g_step(1, turn[1], 2)
    project_last(turn[1])
    finish(turn[0])
    g_step(1, turn[3], 1)
    g_step(1, turn[2], 2)
    project_last(turn[2])
    finish(turn[1])
    g_step(1, turn[3], 2)
    project_last(turn[3])
    finish(turn[2])
    finish(turn[3])

    total = vel[z]
    for d in NEAR:
        part = vel_in.at[from_z[d]]
        remote(part, part, vs.at[d], vr.at[from_z[d]], at_z[d]).wait_recv()
        total = total + vel_in[from_z[d]]
    half_out[...] = total
    over_y = remote(half_out, half_in, es.at[0], er.at[0], at_y)
    over_y.start()
    over_y.wait()
    total = half_out[...] + half_in[...]
    average = total[:, channels : channels + 1] / width
    variance = jnp.maximum(total[:, channels + 1 : channels + 2] / width - average * average, 0.0)
    velocity = (total[:, :channels] - average * totals) * lax.rsqrt(variance + EPS)
    core_out[...] = jnp.concatenate([velocity, velocity], axis=1)
    over_c = remote(core_out, core_in, es.at[1], er.at[1], at_c)
    over_c.start()
    over_c.wait()
    span_out = latent.shape[0]
    turned = []
    for held in (core_out, core_in):
        full = jnp.concatenate([held[...], jnp.zeros((-tok % HD, HD), F32)], axis=0)
        both = jnp.transpose(full)[:, :tok]
        turned.append(jnp.where(c == 0, both[:span_out], both[span_out : 2 * span_out]))
    conditional = jnp.where(c == 0, turned[0], turned[1])
    null_text = jnp.where(c == 0, turned[1], turned[0])
    latent_out[...] = latent[...] + step_size[0] * (null_text + guidance[0] * (conditional - null_text))

    for d in NEAR:
        part = hidden_out.at[:, span(from_z[d], wid)]
        remote(part, part, os_.at[d], or_.at[from_z[d]], at_z[d]).wait_recv()
    for i in range(groups):
        @pl.when(z != i)
        def _():
            o_remote(i).wait_send()
            v_remote(i).wait_send()

        @pl.when(z == i)
        def _():
            o_local(i).wait()

        y_copy(i).wait_send()
        y2_copy(i).wait_send()
        for d in NEAR:
            q_copy(i, d).wait_send()
            f_copy(i, d).wait_send()
        for f in (0, 1):
            for way in (0, 1):
                for s in range(groups - 1):
                    @pl.when(line_sends(way, s))
                    def _():
                        g_copy(f, i, way, s).wait_send()
    for d in NEAR:
        s_copy(d).wait_send()
    for j in (1, 2):
        w_copy(j).wait_send()
        wc_copy(j, 0).wait_send()
        wc_copy(j, 1).wait_send()


def cross_attention_call(
    lengths, text_lengths, guidance, step_size, mixed, raw, mean, head, latent, text_kv, w_out, w_cross, w_last
):
    groups = LINE
    rows, cols = mixed.shape
    tok = rows // groups
    wid = raw.shape[2]
    depth, local_cols = w_last.shape
    padded = tok + -tok % HD
    anywhere = pl.BlockSpec(memory_space=pl.ANY)
    vmem = pl.BlockSpec(memory_space=pltpu.VMEM)
    smem = pl.BlockSpec(memory_space=pltpu.SMEM)
    dma = pltpu.SemaphoreType.DMA
    return pl.pallas_call(
        cross_attention_kernel,
        out_shape=[
            jax.ShapeDtypeStruct((tok, groups * wid), BF),
            jax.ShapeDtypeStruct(latent.shape, F32),
        ],
        in_specs=[smem] * 4 + [vmem] * 5 + [anywhere] * 4,
        out_specs=[anywhere, vmem],
        scratch_shapes=[
            pltpu.VMEM((3, 2, 2 * depth, local_cols), BF),
            pltpu.VMEM((2, text_kv.shape[2], cols), BF),
            pltpu.VMEM((2, groups, tok, local_cols), BF),
            pltpu.VMEM((2, groups, tok, cols), BF),
            pltpu.VMEM((groups, tok, 2 * wid), BF),
            pltpu.VMEM((groups, tok, 2 * wid), BF),
            pltpu.VMEM((groups, tok, wid), BF),
            pltpu.VMEM((groups, tok, wid), BF),
            pltpu.VMEM((groups, tok, wid), BF),
            pltpu.VMEM((groups, 2, tok, wid), F32),
            pltpu.VMEM((groups, groups, tok, cols), BF),
            pltpu.VMEM((groups, groups, tok, cols), BF),
            pltpu.VMEM((groups, 8, padded), F32),
            pltpu.VMEM((groups, groups, 8, padded), F32),
            pltpu.VMEM((groups, 8, cols), F32),
            pltpu.VMEM((groups, 8, cols), F32),
            pltpu.VMEM((groups, tok, wid), BF),
            pltpu.VMEM((groups, tok, HD), F32),
            pltpu.VMEM((groups, tok, HD), F32),
            pltpu.VMEM((tok, HD), F32),
            pltpu.VMEM((tok, HD), F32),
            pltpu.VMEM((tok, HD), F32),
            pltpu.VMEM((tok, HD), F32),
            dma((3,)), dma((2,)), dma((2, groups)), dma,
            dma((3,)), dma((3,)), dma((3, 2)), dma((3, 2)),
            dma((2, groups, 2, 3)), dma((2, groups, 2, 3)),
            dma((groups,)), dma((groups,)), dma((groups,)), dma((groups,)),
            dma((groups, 3)), dma((groups, 3)), dma((groups, 3)), dma((groups, 3)),
            dma((3,)), dma((3,)),
            dma((groups,)), dma((groups,)), dma((groups,)), dma((groups,)),
            dma((2,)), dma((2,)),
        ],
        compiler_params=pltpu.CompilerParams(
            collective_id=1, has_side_effects=True, vmem_limit_bytes=56 * 2**20
        ),
        cost_estimate=pl.CostEstimate(
            flops=20 * rows * wid * local_cols, bytes_accessed=20 * 2**20, transcendentals=0
        ),
    )(lengths, text_lengths, guidance, step_size, mixed, raw, mean, head, latent, text_kv, w_out, w_cross, w_last)


def on_device(
    hidden,
    latent,
    tenant_lengths,
    grid_positions,
    text_kv,
    text_lengths,
    w_query,
    w_key,
    w_value,
    w_out,
    w_cross_query,
    w_cross_out,
    w_head,
    guidance,
    step_size,
):
    halves, groups, parts, columns = (lax.axis_size(a) for a in ("cfg", "z", "t", "wt"))
    half_index, z_index, t_index, wt_index = (
        lax.axis_index(a) for a in ("cfg", "z", "t", "wt")
    )
    tok, width = hidden.shape[1:]
    rows = groups * tok
    local_cols = w_query.shape[1]
    my_cols = local_cols // groups
    heads = my_cols // HD
    paired = halves == 2 and parts == 2
    block = w_query.shape[0]
    if paired and groups == LINE and columns == 2 and tok % 16 == 0 and block % 16 == 0 and my_cols % HD == 0:
        mixed, raw, mean, out_wide = self_attention_call(
            tenant_lengths, hidden[0], grid_positions, w_key, w_value, w_query, w_out
        )
        hidden_out, latent_next = cross_attention_call(
            tenant_lengths, text_lengths, guidance, step_size, mixed, raw, mean, w_head.T, latent.T,
            text_kv, out_wide, w_cross_query, w_cross_out,
        )
        return (hidden_out[None], latent_next.T)
    ends = running_ends(tenant_lengths)

    def tenant_of(indices):
        return jnp.sum((indices[:, None] >= ends[None, :]).astype(jnp.int32), axis=1)

    def ordered(mine, other, index):
        return jnp.where(
            index == 0, jnp.concatenate([mine, other]), jnp.concatenate([other, mine])
        )

    def wide(w):
        if not paired:
            return lax.all_gather(w, ("cfg", "t"), axis=0, tiled=True)
        two = ordered(w, flip(w, "t"), t_index)
        return ordered(two, flip(two, "cfg"), half_index)

    def over_groups(x):
        return x if groups == 1 else lax.all_to_all(x, "z", 0, 0, tiled=True)

    def join_groups(x):
        if groups == 1:
            return x
        x = lax.all_gather(x, "z", axis=0)
        return jnp.swapaxes(x, 0, 1).reshape(x.shape[1], local_cols)

    def sum_at_owner(x):
        if groups == 1:
            return x[0].astype(F32)
        return jnp.sum(lax.all_to_all(x, "z", 0, 0).astype(F32), axis=0)

    def sum_groups(x):
        if groups == 1:
            return x
        return lax.psum_scatter(x, "z", scatter_dimension=0, tiled=True)

    def to_groups(x, n):
        return jnp.swapaxes(x.reshape(x.shape[0], groups, n), 0, 1)

    def both_columns(terms):
        terms = terms.astype(BF)
        if columns == 1:
            return terms.astype(F32)
        if columns == 2:
            return terms.astype(F32) + flip(terms, "wt").astype(F32)
        return lax.psum(terms, "wt").astype(F32)

    if paired:
        key_pair = ordered(w_key, flip(w_key, "t"), t_index)
        key_pair, w_query, w_value = lax.optimization_barrier((key_pair, w_query, w_value))
        wide_key = ordered(key_pair, flip(key_pair, "cfg"), half_index)
    else:
        wide_key = wide(w_key)
    wide_query, wide_value = wide(w_query), wide(w_value)
    wide_out, wide_cross, wide_cross_out = wide(w_out), wide(w_cross_query), wide(w_cross_out)

    chunks = CHUNKS if groups > 1 and tok % (CHUNKS * 16) == 0 else 1
    part = tok // chunks
    chunk_rows = rows // chunks

    def by_chunk(x):
        shape = (groups, chunks, part) + x.shape[2:]
        return jnp.swapaxes(x.reshape(shape), 0, 1).reshape((rows,) + x.shape[2:])

    def three_terms(x):
        high = lax.reduce_precision(x, 8, 7)
        middle = lax.reduce_precision(x - high, 8, 7)
        return [term.astype(BF) for term in (high, middle, x - high - middle)]

    own = hidden[0].astype(F32)
    mean = jnp.mean(own, axis=-1, keepdims=True)
    centred = own - mean
    scale = lax.rsqrt(jnp.mean(centred * centred, axis=-1, keepdims=True) + EPS)
    facts = jnp.concatenate([mean, scale, grid_positions.astype(F32)], axis=1)
    slice_width = width // groups
    if groups == 1:
        sliced = own
    else:
        extra = jnp.concatenate(three_terms(facts), axis=1)
        extra = jnp.pad(extra, ((0, 0), (0, 128 - extra.shape[1])))
        features = hidden[0].reshape(tok, halves, groups, slice_width // halves)
        features = jnp.concatenate(
            [features[:, half] for half in range(halves)]
            + [jnp.broadcast_to(extra[:, None], (tok, groups, 128))],
            axis=2,
        )
        arrived = lax.all_to_all(jnp.swapaxes(features, 0, 1), "z", 0, 0)
        arrived = by_chunk(arrived).astype(F32)
        sliced = arrived[:, :slice_width]
        extra = arrived[:, slice_width : slice_width + 15]
        facts = extra[:, 0:5] + extra[:, 5:10] + extra[:, 10:15]
    normed = ((sliced - facts[:, 0:1]) * facts[:, 1:2]).astype(BF)

    def project(w):
        return to_groups(jnp.dot(normed, w, preferred_element_type=F32).astype(BF), my_cols)

    projected_keys = sum_at_owner(project(wide_key)).astype(BF)
    projected = jnp.concatenate([project(wide_query), project(wide_value)], axis=2)
    projected = sum_groups(projected.reshape(groups * rows, 2 * my_cols))

    table, swap = rotary_tables()
    angles = (
        facts[:, 2:3] * table[0][None] + facts[:, 3:4] * table[1][None] + facts[:, 4:5] * table[2][None]
    )
    cosine, sinus = jnp.cos(angles)[:, None, :], jnp.sin(angles)[:, None, :]

    def rotated(x):
        shaped = x.reshape(rows, heads, HD)
        swapped = jnp.einsum("thd,de->the", shaped, jnp.asarray(swap, BF), preferred_element_type=F32)
        shaped = shaped.astype(F32)
        return ((shaped * cosine + swapped * sinus) * head_scale(shaped)).astype(BF)

    keys = rotated(projected_keys).reshape(rows, my_cols)
    queries = rotated(projected[:, :my_cols])
    values = projected[:, my_cols:]

    base = jnp.arange(groups, dtype=jnp.int32)[:, None] * (parts * tok)
    base = by_chunk(base + jnp.arange(tok, dtype=jnp.int32)[None])
    my_tenant = tenant_of(base + t_index * tok)
    if parts == 2:
        keys = jnp.concatenate([keys, flip(keys, "t")], axis=0)
        values = jnp.concatenate([values, flip(values, "t")], axis=0)
        key_tenant = jnp.concatenate([my_tenant, tenant_of(base + (1 - t_index) * tok)])
    else:
        keys = lax.all_gather(keys, "t", axis=0, tiled=True)
        values = lax.all_gather(values, "t", axis=0, tiled=True)
        key_tenant = tenant_of(
            (jnp.arange(parts, dtype=jnp.int32)[:, None] * tok + base[None]).reshape(-1)
        )
    keys = keys.reshape(-1, heads, HD)
    values = values.reshape(-1, heads, HD)

    spans = [slice(i * chunk_rows, (i + 1) * chunk_rows) for i in range(chunks)]
    mixed = [
        attend(queries[i], keys, values, my_tenant[i][:, None] == key_tenant[None, :])
        for i in spans
    ]

    def project_out(mixed, weight):
        return lax.dot_general(
            join_groups(mixed), weight, (((1,), (1,)), ((), ())), preferred_element_type=F32
        )

    column_sums = jnp.dot(jnp.ones((8, slice_width), BF), wide_cross, preferred_element_type=F32)
    column_sums = column_sums[0].reshape(groups, 1, my_cols)
    riding = groups > 1 and chunk_rows <= my_cols

    text = lax.dynamic_slice_in_dim(text_kv[:, 0], z_index * my_cols, my_cols, 2)
    text_keys = text[0].reshape(-1, heads, HD).astype(F32)
    text_keys = (text_keys * head_scale(text_keys)).astype(BF)
    text_values = text[1].reshape(-1, heads, HD)
    text_index = jnp.arange(text_kv.shape[2], dtype=jnp.int32)
    text_tenant = text_index // TEXT
    slots = text_tenant[:, None] == jnp.arange(TENANTS, dtype=jnp.int32)[None, :]
    live_length = jnp.sum(jnp.where(slots, text_lengths[0][None, :], 0), axis=1)
    live = text_index % TEXT < live_length

    states, cross_mixed = [], []
    for i, block_mixed in zip(spans, mixed):
        shifted = (sliced[i] - facts[i, 0:1]) + both_columns(project_out(block_mixed, wide_out))
        states.append(shifted)
        sums = jnp.stack([jnp.sum(shifted, axis=1), jnp.sum(shifted * shifted, axis=1)])
        crossed = jnp.dot(shifted.astype(BF), wide_cross, preferred_element_type=F32).astype(BF)
        crossed = to_groups(crossed, my_cols)
        if riding:
            sums = jnp.concatenate(three_terms(sums))
            sums = jnp.pad(sums, ((0, 0), (0, my_cols - chunk_rows)))
            sums = jnp.broadcast_to(sums[None], (groups,) + sums.shape)
            below = jnp.concatenate([sums] + three_terms(column_sums), axis=1)
            below = jnp.pad(below, ((0, 0), (0, 16 - below.shape[1]), (0, 0)))
            arrived = sum_at_owner(jnp.concatenate([crossed, below], axis=1))
            crossed, below = arrived[:chunk_rows], arrived[chunk_rows:]
            sums = (below[0:2] + below[2:4] + below[4:6])[:, :chunk_rows]
            all_columns = below[6:7] + below[7:8] + below[8:9]
        else:
            sums = sum_at_owner(jnp.broadcast_to(sums[None], (groups,) + sums.shape))
            all_columns = sum_at_owner(column_sums)
            crossed = sum_at_owner(crossed)
        sums = sums / width
        variance = jnp.maximum(sums[1] - sums[0] * sums[0], 0.0)[:, None, None]
        shaped = (crossed - sums[0][:, None] * all_columns).reshape(chunk_rows, heads, HD)
        square = jnp.mean(shaped * shaped, axis=-1, keepdims=True)
        cross_queries = (shaped * lax.rsqrt(square + EPS * (variance + EPS))).astype(BF)
        allowed = (my_tenant[i][:, None] == text_tenant[None, :]) & live[None]
        cross_mixed.append(attend(cross_queries, text_keys, text_values, allowed))

    channels = w_head.shape[1]
    head_rows = lax.dynamic_index_in_dim(
        w_head.reshape(halves, groups, parts * block, channels), z_index, 1, keepdims=False
    ).reshape(-1, channels)
    totals = jnp.sum(w_head.astype(F32), axis=0)[None]
    out_width = width // columns

    leaving, sums = [], []
    for i, shifted, block_mixed in zip(spans, states, cross_mixed):
        shifted = shifted + both_columns(project_out(block_mixed, wide_cross_out))
        final = (shifted + facts[i, 0:1]).astype(BF)
        if groups > 1 and columns == halves:
            span = slice_width // halves
            final = lax.dynamic_slice_in_dim(final, wt_index * span, span, 1)
        leaving.append(final.reshape(groups, part, -1))
        some = jnp.concatenate(
            [
                jnp.dot(shifted.astype(BF), head_rows, preferred_element_type=F32),
                jnp.sum(shifted, axis=1, keepdims=True),
                jnp.sum(shifted * shifted, axis=1, keepdims=True),
            ],
            axis=1,
        )
        sums.append(some.reshape(groups, part, channels + 2))
    sums = sum_at_owner(jnp.concatenate(sums, axis=1))
    mean = sums[:, channels : channels + 1] / width
    variance = jnp.maximum(sums[:, channels + 1 :] / width - mean * mean, 0.0)
    velocity = (sums[:, :channels] - mean * totals) * lax.rsqrt(variance + EPS)

    leaving = jnp.concatenate(leaving, axis=1)
    if groups == 1:
        hidden_out = lax.dynamic_slice_in_dim(leaving[0], wt_index * out_width, out_width, 1)
    else:
        leaving = jnp.swapaxes(lax.all_to_all(leaving, "z", 0, 0), 0, 1)
        if columns == halves:
            hidden_out = leaving.reshape(tok, out_width)
        else:
            leaving = jnp.swapaxes(leaving.reshape(tok, groups, halves, -1), 1, 2)
            hidden_out = lax.dynamic_slice_in_dim(
                leaving.reshape(tok, width), wt_index * out_width, out_width, 1
            )

    channel_half = latent.shape[1]
    outgoing = lax.dynamic_slice_in_dim(velocity, (1 - half_index) * channel_half, channel_half, 1)
    partner = flip(outgoing, "cfg")
    own_part = lax.dynamic_slice_in_dim(velocity, half_index * channel_half, channel_half, 1)
    conditional = jnp.where(half_index == 0, own_part, partner)
    null_text = jnp.where(half_index == 0, partner, own_part)
    latent_next = latent + step_size[0] * (null_text + guidance[0] * (conditional - null_text))
    return (hidden_out[None], latent_next)


def solution(mesh):
    halves, seq, columns = (mesh.shape[a] for a in ("cfg", "seq", "wt"))

    def run(*args):
        heads_here = args[6].shape[1] // columns // HD
        groups = math.gcd(heads_here, seq)
        fine = Mesh(
            mesh.devices.reshape(halves, groups, seq // groups, columns), ("cfg", "z", "t", "wt")
        )
        seq_axes = ("z", "t")
        weight = P(("cfg", "z", "t"), "wt")
        return jax.shard_map(
            on_device,
            mesh=fine,
            in_specs=(
                P("cfg", seq_axes, None),
                P(seq_axes, "cfg"),
                P(),
                P(seq_axes, None),
                P(None, "cfg", None, "wt"),
                P("cfg", None),
                weight,
                weight,
                weight,
                weight,
                weight,
                weight,
                P(),
                P(),
                P(),
            ),
            out_specs=(P("cfg", seq_axes, "wt"), P(seq_axes, "cfg")),
            check_vma=False,
        )(*args)

    return run
```
